32 devices in a mesh: groups: 2 (over y), depth: 16 (over z, x, core).
Axes of the slice: x: 2, y: 2, z: 4, core: 2. Of those that a mesh axis runs over, the one named last changes fastest.
Arguments:
- sources: float32 [2, 8, 8, 128], P(None, 'groups'), parts along dimension 1, may hold values from -6 to 6
- plan: int32 [8], P('groups'), parts along dimension 0, may hold values from 0 to 1023
- absorb: float32 [16, 16, 128], P('depth', 'groups'), parts along dimension 1, as said below
- labels: int32 [16, 16, 128], P('depth', 'groups'), parts along dimension 1, may hold values from 0 to 7
- region_kk: float32 [8], replicated, may hold values from 0.1 to 1
- damp_cells: int32 [256], P('groups'), parts along dimension 0, may hold values from 0 to 1023
- initial_guess: float32 [2, 8, 1024, 8, 128], P(None, 'groups', 'depth'), parts along dimension 1, may hold values from -3 to 3
Outputs:
- solution: float32 [2, 8, 1024, 8, 128], P(None, 'groups', 'depth'), parts along dimension 1
The draws below stay inside these ranges and needn't reach their ends.
There are 2 independent parts, one for each index of `groups`. The reference program is written for one: setup_inputs(seed, part) draws one part's arguments, and reference() takes and returns one part's arrays. A program takes and returns all parts, laid end to end along the dimension named above; an argument that names none is the same for every part. Nothing has to cross between parts.
Inputs may be any that keep to these rules, and one draw needn't show every extreme that they name: `plan`: each source sits on one plane, counted over the whole depth. `damp_cells`: entries may repeat. `absorb`: every entry is positive.
All inputs are finite; a program needn't handle non-finite values.
Results may differ from the reference program's by a relative error of at most 0.0003.
Values sent between devices are 32-bit elements; how exact they have to be, the bound alone decides.
No kernel may reach another device: no remote copies, remote signals or barrier semaphores. Data moves between devices by JAX's collectives and lax.ppermute only.
A program may use at most 64 MiB of HBM per device.

```python
import jax
import jax.numpy as jnp
from jax import lax

NY = 8
NZ = 128
SLAB = 64
SRC = 4
STEPS = 2
REGIONS = 8
SLAB_COUNT = 16
PLANES = 1024
NDAMP = 128


def draw_absorb(key, part):
    random_key_list = jax.random.split(jax.random.fold_in(key, 7301), 6)
    fast_share = 0.5
    pick = jax.random.uniform(random_key_list[0], (NY, NZ), jnp.float32) < fast_share
    fast_rate = jnp.exp(jax.random.uniform(random_key_list[1], (NY, NZ), jnp.float32, jnp.log(0.046), jnp.log(0.077)))
    slow_rate = jnp.exp(jax.random.uniform(random_key_list[2], (NY, NZ), jnp.float32, jnp.log(0.0004), jnp.log(0.003)))
    base = jnp.where(pick, fast_rate, slow_rate)
    jitter = jnp.exp(jax.random.uniform(random_key_list[3], (SLAB_COUNT, NY, NZ), jnp.float32, jnp.log(0.6), jnp.log(1.6)))
    grouped_slab_block = jax.random.randint(random_key_list[4], (2,), 0, SLAB_COUNT)
    source_hit_mask = jnp.any(jnp.arange(SLAB_COUNT)[:, None] == grouped_slab_block[None, :], axis=1).astype(jnp.float32)
    loss = jax.random.uniform(random_key_list[5], (SLAB_COUNT, NY, NZ), jnp.float32, 0.22, 0.69)
    return (base[None] * jitter + source_hit_mask[:, None, None] * loss).astype(jnp.float32)


def set_ends(array, stream_key, smallest, high):
    longest = array.shape.index(max(array.shape))
    spots = []
    for shift in (0, 1):
        where = [jax.random.randint(jax.random.fold_in(stream_key, axis), (), 0, length) for axis, length in enumerate(array.shape)]
        where[longest] = (where[longest] + shift) % array.shape[longest]
        spots.append(tuple(where))
    return array.at[spots[0]].set(smallest).at[spots[1]].set(high)


def block_scale(stream_key, shape, shards, low, high):
    gain = 1.0
    for position, blocks in shards:
        draws = jax.random.uniform(jax.random.fold_in(jax.random.fold_in(stream_key, 6), position), (blocks,), jnp.float32, low / len(shards), high / len(shards))
        gain = gain * jnp.repeat(jnp.exp(draws), shape[position] // blocks).reshape((-1,) + (1,) * (len(shape) - 1 - position))
    return gain


def centred(stream_key, extent, width, bound, cuts=(), kind=jnp.bfloat16):
    values = width * jax.random.normal(stream_key, extent, jnp.float32)
    if cuts:
        values = values * block_scale(stream_key, extent, cuts, -0.22, 0.18)
    return jnp.clip(values, -bound, bound).astype(kind)


def setup_inputs(seed: int = 0, part: int = 0) -> dict:
    key_of = jax.random.split(jax.random.key(seed), 8)
    part_keys = jax.random.split(jax.random.fold_in(key_of[7], part), 8)
    return {
        "sources": centred(part_keys[0], (2, SRC, NY, NZ), 1.0, 6.0, (), jnp.float32),
        "plan": set_ends(jax.random.randint(part_keys[1], (SRC,), 0, PLANES), jax.random.fold_in(part_keys[1], 1), 0, PLANES - 1).astype(jnp.int32),
        "absorb": draw_absorb(jax.random.fold_in(jax.random.fold_in(key_of[7], part), 71), part),
        "labels": set_ends(jax.random.randint(part_keys[3], (SLAB_COUNT, NY, NZ), 0, REGIONS), jax.random.fold_in(part_keys[3], 1), 0, REGIONS - 1).astype(jnp.int32),
        "region_kk": jnp.clip(jax.random.uniform(key_of[4], (REGIONS,), jnp.float32, 0.1, 1.0), 0.1, 1.0),
        "damp_cells": set_ends(jax.random.randint(part_keys[5], (NDAMP,), 0, NY * NZ), jax.random.fold_in(part_keys[5], 1), 0, (NY * NZ) - 1).astype(jnp.int32),
        "initial_guess": centred(part_keys[6], (2, SRC, PLANES, NY, NZ), 0.5, 3.0, ((2, 16),), jnp.float32),
    }


relax_weight = 0.8
shift_ratio = 0.5
damping = 3.0
coupling = 0.25

def complex_mul(left, right):
    return jnp.stack([left[0] * right[0] - left[1] * right[1], left[0] * right[1] + left[1] * right[0]])

def lateral_sum(field):
    widths = [(0, 0)] * (field.ndim - 2) + [(1, 1), (0, 0)]
    padded = jnp.pad(field, widths)
    total = padded[..., 2:, :] + padded[..., :-2, :]
    widths = [(0, 0)] * (field.ndim - 1) + [(1, 1)]
    padded = jnp.pad(field, widths)
    return total + padded[..., 2:] + padded[..., :-2]

def neighbours(extended):
    middle = extended[:, :, 1:-1]
    return extended[:, :, 2:] + extended[:, :, :-2] + lateral_sum(middle)

def pad_depth(field):
    return jnp.pad(field, ((0, 0), (0, 0), (1, 1), (0, 0), (0, 0)))

def sweep_chain(passage, emitted, backward):
    items = (jnp.moveaxis(passage, 1, 0), jnp.moveaxis(emitted, 2, 0))
    start = jnp.zeros((2, SRC, NY, NZ), jnp.float32)

    def advance(carry, item):
        return (complex_mul(item[0], carry) + item[1], carry)
    unused, seen = lax.scan(advance, start, items, reverse=backward)
    return jnp.moveaxis(seen, 0, 2)

def reference(sources, plan, absorb, labels, region_kk, damp_cells, initial_guess):
    regions = jnp.arange(REGIONS)
    squared = lax.optimization_barrier(jnp.sum(jnp.where(labels[..., None] == regions, region_kk, 0.0), axis=-1))
    cells = jnp.arange(NY * NZ)
    layer = jnp.any(damp_cells[:, None] == cells[None, :], axis=0).astype(jnp.float32).reshape(NY, NZ)
    diagonal_real_part = 6.0 - squared
    imag_diag = shift_ratio * squared + damping * layer
    complex_magnitude = diagonal_real_part * diagonal_real_part + imag_diag * imag_diag
    inverse = jnp.stack([diagonal_real_part / complex_magnitude, -imag_diag / complex_magnitude])
    orders = jnp.arange(SLAB + 1).astype(jnp.float32)[None, :, None, None]
    magnitude = jnp.exp(-orders * absorb[:, None] / SLAB)
    phase_angle_sum = orders * jnp.sqrt(squared)[:, None]
    powers = jnp.stack([magnitude * jnp.cos(phase_angle_sum), magnitude * jnp.sin(phase_angle_sum)])
    passage = powers[:, :, SLAB]
    toward_next = powers[:, :, :SLAB][:, :, ::-1][:, None]
    toward_prev = powers[:, :, :SLAB][:, None]
    entry_next = powers[:, :, 1:][:, None]
    entry_prev = powers[:, :, 1:][:, :, ::-1][:, None]
    plane_real = jnp.repeat(diagonal_real_part, SLAB, axis=0)
    inverse_planes = jnp.repeat(inverse, SLAB, axis=1)[:, None]
    planes = jnp.arange(PLANES)
    hits = (planes[None, :] == plan[:, None]).astype(jnp.float32)
    forcing = sources[:, :, None] * hits[None, :, :, None, None]
    solution = initial_guess
    for turn in range(STEPS):
        beside_all = neighbours(pad_depth(solution))
        applied = jnp.stack([plane_real * solution[0] - beside_all[0] - damping * layer * solution[1], plane_real * solution[1] - beside_all[1] + damping * layer * solution[0]])
        residual = forcing - applied
        blocks = residual.reshape(2, SRC, SLAB_COUNT, SLAB, NY, NZ)
        emit_next = lax.optimization_barrier(jnp.sum(complex_mul(toward_next, blocks), axis=3))
        emit_prev = lax.optimization_barrier(jnp.sum(complex_mul(toward_prev, blocks), axis=3))
        incoming_next = sweep_chain(passage, emit_next, False)
        incoming_prev = sweep_chain(passage, emit_prev, True)
        corrected_field = blocks + coupling * (complex_mul(entry_next, incoming_next[:, :, :, None]) + complex_mul(entry_prev, incoming_prev[:, :, :, None]))
        corrected_field = corrected_field.reshape(2, SRC, PLANES, NY, NZ)
        update = relax_weight * complex_mul(inverse_planes, corrected_field)
        for inner in range(2):
            update = (1.0 - relax_weight) * update + relax_weight * complex_mul(inverse_planes, corrected_field + neighbours(pad_depth(update)))
        solution = solution + update
    return solution
```

```python
import functools

import jax
import jax.numpy as jnp
from jax import lax
from jax.experimental import pallas as pl
from jax.experimental.pallas import tpu as pltpu
from jax.sharding import PartitionSpec as P

relax_weight = 0.8
shift_ratio = 0.5
damping = 3.0
coupling = 0.25

DEEP = 6
keep = 1.0 - relax_weight

VMEM = pltpu.VMEM
SMEM = pltpu.SMEM
ANY = pl.ANY


def cmul(a, b):
    return a[0] * b[0] - a[1] * b[1], a[0] * b[1] + a[1] * b[0]


def add(a, b):
    return a[0] + b[0], a[1] + b[1]


def scale(c, a):
    return c * a[0], c * a[1]


def pick(cond, a, b):
    return jnp.where(cond, a[0], b[0]), jnp.where(cond, a[1], b[1])


def edge_masks(height, breadth):
    row = lax.broadcasted_iota(jnp.int32, (height, breadth), 0)
    lane = lax.broadcasted_iota(jnp.int32, (height, breadth), 1)
    return row > 0, row < height - 1, lane > 0, lane < breadth - 1


def lateral(field, masks):
    height, breadth = field.shape[-2:]
    rows, lanes = field.ndim - 2, field.ndim - 1
    total = jnp.where(masks[0], pltpu.roll(field, 1, rows), 0.0)
    total += jnp.where(masks[1], pltpu.roll(field, height - 1, rows), 0.0)
    total += jnp.where(masks[2], pltpu.roll(field, 1, lanes), 0.0)
    total += jnp.where(masks[3], pltpu.roll(field, breadth - 1, lanes), 0.0)
    return total


def around(before, here, after, masks):
    out = []
    for part in range(2):
        total = lateral(here[part], masks)
        if before is not None:
            total += before[part]
        if after is not None:
            total += after[part]
        out.append(total)
    return tuple(out)


def minus_a(before, here, after, diagonal, layer3, masks):
    beside = around(before, here, after, masks)
    return (
        beside[0] - diagonal * here[0] + layer3 * here[1],
        beside[1] - diagonal * here[1] - layer3 * here[0],
    )


def coefficients(squared, layer):
    diagonal = 6.0 - squared
    imag = shift_ratio * squared + damping * layer
    size = diagonal * diagonal + imag * imag
    return diagonal, (relax_weight * diagonal / size, -relax_weight * imag / size)


def wave(absorb, squared, slab):
    size = jnp.exp(-absorb / slab)
    angle = jnp.sqrt(squared)
    return size * jnp.cos(angle), size * jnp.sin(angle)


def region_values(labels, kk_ref):
    squared = jnp.zeros(labels.shape, jnp.float32)
    for region in range(kk_ref.shape[0]):
        squared = jnp.where(labels == region, kk_ref[region], squared)
    return squared


def loop(start, stop, body, carry, unroll):
    trips = (stop - start) // unroll

    def several(trip, carry):
        for i in range(unroll):
            carry = body(start + trip * unroll + i, carry)
        return carry

    carry = lax.fori_loop(0, trips, several, carry)
    for plane in range(start + trips * unroll, stop):
        carry = body(plane, carry)
    return carry


def start_kernel(
    plan, kk, damp, sources, absorb, labels, guess,
    residual, emits, media, power, ends,
):
    slab = guess.shape[2]
    count = guess.shape[1]
    height, breadth = guess.shape[-2:]
    masks = edge_masks(height, breadth)
    row = lax.broadcasted_iota(jnp.int32, (height, breadth), 0)
    lane = lax.broadcasted_iota(jnp.int32, (height, breadth), 1)
    cell = row * breadth + lane

    def mark(i, hit):
        return jnp.where(cell == damp[i], 1.0, hit)

    layer = loop(0, damp.shape[0], mark, jnp.zeros((height, breadth), jnp.float32), 8)
    squared = region_values(labels[0], kk)
    diagonal, inverse = coefficients(squared, layer)
    layer3 = damping * layer
    factor = wave(absorb[0], squared, slab)
    media[0], media[1], media[2], media[3] = inverse[0], inverse[1], diagonal, layer3
    media[4], media[5] = factor

    power[0, 0] = jnp.ones((height, breadth), jnp.float32)
    power[0, 1] = jnp.zeros((height, breadth), jnp.float32)
    for first, last in halves(count):
        pick_s = slice(first, last)

        def get(k):
            return guess[0, pick_s, k], guess[1, pick_s, k]

        def plane(k, carry, before=True, after=True):
            toward_next, toward_prev, w = carry
            r = minus_a(
                get(k - 1) if before else None, get(k), get(k + 1) if after else None,
                diagonal, layer3, masks,
            )
            residual[0, pick_s, k], residual[1, pick_s, k] = r
            toward_next = add(cmul(factor, toward_next), r)
            toward_prev = add(toward_prev, cmul(w, r))
            w = cmul(factor, w)
            power[k + 1, 0], power[k + 1, 1] = w
            return toward_next, toward_prev, w

        zero = jnp.zeros((last - first, height, breadth), jnp.float32)
        carry = ((zero, zero), (zero, zero), (power[0, 0], power[0, 1]))
        carry = plane(0, carry, before=False)
        carry = loop(1, slab - 1, plane, carry, 2)
        carry = plane(slab - 1, carry, after=False)
        for part in range(2):
            emits[0, part, pick_s] = carry[0][part]
            emits[1, part, pick_s] = carry[1][part]
    first_plane = lax.axis_index("depth") * slab
    for s in range(count):
        k = plan[s] - first_plane

        @pl.when((k >= 0) & (k < slab))
        def _():
            src = sources[0, s], sources[1, s]
            for part in range(2):
                residual[part, s, k] += src[part]
            one = cmul((power[slab - 1 - k, 0], power[slab - 1 - k, 1]), src)
            two = cmul((power[k, 0], power[k, 1]), src)
            for part in range(2):
                emits[0, part, s] += one[part]
                emits[1, part, s] += two[part]

    for end, k in enumerate((0, slab - 1)):
        for part in range(2):
            ends[0, end, part] = guess[part, :, k]
            ends[1, end, part] = residual[part, :, k]


def halves(count):
    if count == 1:
        return [(0, 1)]
    return [(0, count // 2), (count // 2, count)]


def arrange_kernel(
    got_even, got_odd, ends, emits, media, power, full, *sends,
):
    count = emits.shape[2]
    slab = power.shape[0] - 1
    place = lax.axis_index("depth")
    even = lax.rem(place, 2) == 0
    weight = power[slab - 1, 0], power[slab - 1, 1]
    tile = lambda part, s, k: (part * count + s) * DEEP + k
    for s in range(count):
        low = tuple(
            jnp.where(even, got_odd[tile(c, s, DEEP - 1)], got_even[tile(c, s, DEEP - 1)])
            for c in range(2)
        )
        high = tuple(
            jnp.where(even, got_even[tile(c, s, 0)], got_odd[tile(c, s, 0)])
            for c in range(2)
        )
        toward_next = add(add(cmul(weight, low), high), (emits[0, 0, s], emits[0, 1, s]))
        toward_prev = add(add(cmul(weight, high), low), (emits[1, 0, s], emits[1, 1, s]))
        for part in range(2):
            full[0, part, s] = toward_next[part]
            full[1, part, s] = toward_prev[part]
    fill_sends(place, full, sends, halves(count), (power[slab, 0], power[slab, 1]))


def fill_sends(place, full, sends, spans, passage=None):
    for send, (first, last) in zip(sends, spans):
        width = last - first

        def one(j, unused):
            later = j > place
            for part in range(2):
                send[j, pl.ds(part * width, width)] = jnp.where(
                    later, full[0, part, first:last], full[1, part, first:last]
                )
            if passage is not None and first == 0:
                send[j, 2 * width] = passage[0]
                send[j, 2 * width + 1] = passage[1]
            return unused

        lax.fori_loop(0, send.shape[0], one, 0)


def prepare_kernel(
    plan, kk, got_even, got_odd, sources, ends, media,
    near, near_residual, near_media, near_power,
):
    count = sources.shape[1]
    slab = near_power.shape[1] - 1
    height, breadth = sources.shape[-2:]
    masks = edge_masks(height, breadth)
    place = lax.axis_index("depth")
    last_place = lax.axis_size("depth") - 1
    even = lax.rem(place, 2) == 0
    tiles = 2 * count * DEEP
    layer3 = media[3]
    layer = layer3 / damping
    for side in range(2):
        first, second = (got_odd, got_even) if side == 0 else (got_even, got_odd)

        def copy(i, unused):
            part = i // count
            s = lax.rem(i, count)
            near[side, part, s] = jnp.where(
                even, first[pl.ds(i * DEEP, DEEP)], second[pl.ds(i * DEEP, DEEP)]
            )
            return unused

        lax.fori_loop(0, 2 * count, copy, 0)
        absorb = jnp.where(even, first[tiles], second[tiles])
        labels = jnp.where(even, first[tiles + 1], second[tiles + 1]).astype(jnp.int32)
        squared = region_values(labels, kk)
        diagonal, inverse = coefficients(squared, layer)
        inside = (place > 0) if side == 0 else (place < last_place)
        for part in range(2):
            near_media[side, part] = jnp.where(inside, inverse[part], 0.0)
        near_media[side, 2] = diagonal
        near_media[side, 3] = layer3
        factor = wave(absorb, squared, slab)
        near_media[side, 4], near_media[side, 5] = factor
        near_power[side, 0, 0] = jnp.ones((height, breadth), jnp.float32)
        near_power[side, 0, 1] = jnp.zeros((height, breadth), jnp.float32)

    def raise_power(k, w):
        out = []
        for side in range(2):
            next_w = cmul((near_media[side, 4], near_media[side, 5]), w[side])
            near_power[side, k + 1, 0], near_power[side, k + 1, 1] = next_w
            out.append(next_w)
        return tuple(out)

    start = tuple((near_power[side, 0, 0], near_power[side, 0, 1]) for side in range(2))
    loop(0, slab, raise_power, start, 4)

    for first, last in halves(count):
        pick_s = slice(first, last)
        for side in range(2):

            def get(i):
                if side == 0 and i == DEEP:
                    return ends[0, 0, 0, pick_s], ends[0, 0, 1, pick_s]
                if side == 1 and i == -1:
                    return ends[0, 1, 0, pick_s], ends[0, 1, 1, pick_s]
                return near[side, 0, pick_s, i], near[side, 1, pick_s, i]

            for i in range(1 - side, DEEP - side):
                r = minus_a(
                    get(i - 1), get(i), get(i + 1),
                    near_media[side, 2], layer3, masks,
                )
                for part in range(2):
                    near_residual[side, part, pick_s, i if side else i - 1] = r[part]

    for s in range(count):
        k = plan[s] - place * slab
        for side, low in ((0, 1 - DEEP), (1, slab)):
            i = k - low

            @pl.when((i >= 0) & (i < DEEP - 1))
            def _():
                for part in range(2):
                    near_residual[side, part, s, i] += sources[part, s]


def own_incoming(place, last_place, got, passages, at, width, full, span, power, slab):
    shape = got.shape[-2:]
    zero = jnp.zeros((width,) + shape, jnp.float32)

    def wave_of(j):
        return got[j, pl.ds(0, width)], got[j, pl.ds(width, width)]

    def step(j, state):
        return add(cmul((passages[j, at], passages[j, at + 1]), state), wave_of(j))

    below = jnp.maximum(place - 1, 0)
    above = jnp.minimum(place + 1, last_place)
    next_low = lax.fori_loop(0, below, step, (zero, zero))
    next_own = pick(place > 0, step(below, next_low), (zero, zero))
    prev_high = lax.fori_loop(
        0, last_place - above, lambda t, state: step(last_place - t, state), (zero, zero)
    )
    prev_own = pick(place < last_place, step(above, prev_high), (zero, zero))
    passage = power[slab, 0], power[slab, 1]
    first, last = span
    emit = lambda way: (full[way, 0, first:last], full[way, 1, first:last])
    next_high = add(cmul(passage, next_own), emit(0))
    prev_low = add(cmul(passage, prev_own), emit(1))
    return [
        (scale(coupling, a), scale(coupling, b))
        for a, b in ((next_low, prev_low), (next_own, prev_own), (next_high, prev_high))
    ]


def update_passes(
    reach, slab, incoming, residual_of, media, near_media, power, near_power,
    first_update, second_update, emit, masks,
):
    sides = (
        (-reach, 0, near_media.at[0], near_power.at[0], incoming[0], slab),
        (0, slab, media, power, incoming[1], 0),
        (slab, slab + reach, near_media.at[1], near_power.at[1], incoming[2], -slab),
    )
    for which, (start, stop, m, w, (onward, back), shift) in enumerate(sides):
        inverse = m[0], m[1]

        def begin(p, unused):
            k = p + shift
            c = residual_of(which, p)
            c = add(c, cmul((w[k + 1, 0], w[k + 1, 1]), onward))
            c = add(c, cmul((w[slab - k, 0], w[slab - k, 1]), back))
            u = cmul(inverse, c)
            first_update[0, :, p + reach], first_update[1, :, p + reach] = u
            return unused

        if which == 1:
            begin(0, 0)
            loop(1, slab - 1, begin, 0, 2)
            begin(slab - 1, 0)
        else:
            loop(start, stop, begin, 0, 1)
    for which, (start, stop, m, *rest) in enumerate(sides):
        inverse = m[0], m[1]

        def second(p, unused):
            get = lambda q: (first_update[0, :, q + reach], first_update[1, :, q + reach])
            here = get(p)
            beside = around(get(p - 1), here, get(p + 1), masks)
            u = add(scale(1.0 + keep, here), cmul(inverse, beside))
            second_update[0, :, p + reach - 1], second_update[1, :, p + reach - 1] = u
            return unused

        loop(max(start, 1 - reach), min(stop, slab + reach - 1), second, 0, 2)
    for which, (start, stop, m, *rest) in enumerate(sides):
        inverse = m[0], m[1]

        def third(p, unused):
            get = lambda q: (
                second_update[0, :, q + reach - 1],
                second_update[1, :, q + reach - 1],
            )
            here = get(p)
            beside = around(get(p - 1), here, get(p + 1), masks)
            u = add(scale(keep, here), cmul(inverse, beside))
            u = add(u, (first_update[0, :, p + reach], first_update[1, :, p + reach]))
            emit(which, p, u)
            return unused

        loop(max(start, 2 - reach), min(stop, slab + reach - 2), third, 0, 2)


def middle_kernel(
    span, at, plan, sources, guess, residual, near, near_residual, ends, media, power,
    near_media, near_power, got, passages, full,
    solution, next_residual, next_full, send, first_update, second_update,
):
    first, last = span
    width = last - first
    slab = guess.shape[2]
    height, breadth = guess.shape[-2:]
    masks = edge_masks(height, breadth)
    place = lax.axis_index("depth")
    last_place = lax.axis_size("depth") - 1
    reach = DEEP - 1
    even = lax.rem(place, 2) == 0
    incoming = own_incoming(
        place, last_place, got, passages, at, width, full, span, power, slab
    )

    def residual_of(which, p):
        if which == 0:
            i = p + reach
            return near_residual[0, 0, first:last, i], near_residual[0, 1, first:last, i]
        if which == 2:
            i = p - slab
            return near_residual[1, 0, first:last, i], near_residual[1, 1, first:last, i]
        r = residual[0, first:last, p], residual[1, first:last, p]
        if isinstance(p, int) and p == 0:
            r = add(r, (near[0, 0, first:last, DEEP - 1], near[0, 1, first:last, DEEP - 1]))
        if isinstance(p, int) and p == slab - 1:
            r = add(r, (near[1, 0, first:last, 0], near[1, 1, first:last, 0]))
        return r

    ext = reach - 2

    def emit(which, p, u):
        for part in range(2):
            if which == 0:
                old = near[0, part, first:last, p + DEEP]
            elif which == 1:
                old = guess[part, first:last, p]
            else:
                old = near[1, part, first:last, p - slab]
            solution[part, :, p + ext] = old + u[part]

    update_passes(
        reach, slab, incoming, residual_of, media, near_media, power, near_power,
        first_update, second_update, emit, masks,
    )

    get = lambda p: (solution[0, :, p + ext], solution[1, :, p + ext])
    layer3 = media[3]
    more = ext - 1
    factor = media[4], media[5]

    def outside(diagonal):
        def one(p, unused):
            r = minus_a(get(p - 1), get(p), get(p + 1), diagonal, layer3, masks)
            next_residual[0, :, p + more], next_residual[1, :, p + more] = r
            return unused

        return one

    loop(-more, 0, outside(near_media[0, 2]), 0, 1)
    loop(slab, slab + more, outside(near_media[1, 2]), 0, 1)
    diagonal = media[2]

    def inside(p, carry):
        toward_next, toward_prev = carry
        r = minus_a(get(p - 1), get(p), get(p + 1), diagonal, layer3, masks)
        next_residual[0, :, p + more], next_residual[1, :, p + more] = r
        toward_next = add(cmul(factor, toward_next), r)
        toward_prev = add(toward_prev, cmul((power[p, 0], power[p, 1]), r))
        return toward_next, toward_prev

    zero = jnp.zeros((width, height, breadth), jnp.float32)
    carry = loop(0, slab, inside, ((zero, zero), (zero, zero)), 2)
    for way in range(2):
        for part in range(2):
            next_full[way, part] = carry[way][part]
    for s in range(width):
        k = plan[first + s] - place * slab
        src = sources[0, first + s], sources[1, first + s]

        @pl.when((k >= -more) & (k < slab + more))
        def _():
            for part in range(2):
                next_residual[part, s, k + more] += src[part]

        @pl.when((k >= 0) & (k < slab))
        def _():
            one = cmul((power[slab - 1 - k, 0], power[slab - 1 - k, 1]), src)
            two = cmul((power[k, 0], power[k, 1]), src)
            for part in range(2):
                next_full[0, part, s] += one[part]
                next_full[1, part, s] += two[part]

    fill_sends(place, next_full, (send,), [(0, width)])


def final_kernel(
    span, at, aliased, residual, solution, media, power, near_media, near_power,
    got, passages, full, *rest,
):
    if aliased:
        rest = rest[1:]
    out, first_update, second_update, stage, sems = rest
    first, last = span
    width = last - first
    slab = out.shape[2]
    height, breadth = out.shape[-2:]
    masks = edge_masks(height, breadth)
    place = lax.axis_index("depth")
    last_place = lax.axis_size("depth") - 1
    reach = 2
    ext = DEEP - 3
    incoming = own_incoming(
        place, last_place, got, passages, at, width, full, (0, width), power, slab
    )

    def residual_of(which, p):
        return residual[0, :, p + reach], residual[1, :, p + reach]

    def emit(which, p, u):
        for part in range(2):
            stage[part, :, p] = solution[part, :, p + ext] + u[part]

    update_passes(
        reach, slab, incoming, residual_of, media, near_media, power, near_power,
        first_update, second_update, emit, masks,
    )
    copies = []
    for part in range(2):
        copies.append(
            pltpu.make_async_copy(
                stage.at[part], out.at[part, pl.ds(first, width)], sems.at[part]
            )
        )
        copies[-1].start()
    for copy in copies:
        copy.wait()


def call(kernel, operands, out_shape, spaces, out_spaces=None, scratch=(), cost=0, alias=None, name=None):
    space = lambda s: pl.BlockSpec(memory_space=s)
    single = not isinstance(out_shape, (tuple, list))
    outs = (out_shape,) if single else tuple(out_shape)
    out_spaces = out_spaces or (VMEM,) * len(outs)
    result = pl.pallas_call(
        kernel,
        out_shape=tuple(jax.ShapeDtypeStruct(s, jnp.float32) for s in outs),
        in_specs=[space(s) for s in spaces],
        out_specs=tuple(space(s) for s in out_spaces),
        scratch_shapes=scratch,
        input_output_aliases=alias or {},
        compiler_params=pltpu.CompilerParams(vmem_limit_bytes=24 << 20),
        cost_estimate=pl.CostEstimate(flops=cost, bytes_accessed=4 << 20, transcendentals=0),
        name=name,
    )(*operands)
    return result


def local(sources, plan, absorb, labels, region_kk, damp_cells, guess):
    size = lax.axis_size("depth")
    place = lax.axis_index("depth")
    _, count, slab, height, breadth = guess.shape
    tile = (height, breadth)
    spans = halves(count)

    even = place % 2 == 0
    top = slab - DEEP

    def payload(start):
        planes = lax.dynamic_slice_in_dim(guess, start, DEEP, axis=2)
        return jnp.concatenate(
            [planes.reshape((-1,) + tile), absorb, labels.astype(jnp.float32)], axis=0
        )

    even_pairs = [(i, i ^ 1) for i in range(size) if i ^ 1 < size]
    odd_pairs = [(i, i + 1) for i in range(1, size - 1, 2)]
    odd_pairs += [(b, a) for a, b in odd_pairs]
    got_odd = lax.ppermute(payload(jnp.where(even, 0, top)), "depth", odd_pairs)
    got_even = lax.ppermute(payload(jnp.where(even, top, 0)), "depth", even_pairs)

    field = (2, count, slab) + tile
    residual, emits, media, power, ends = call(
        start_kernel,
        (plan, region_kk, damp_cells, sources, absorb, labels, guess),
        (
            field,
            (2, 2, count) + tile,
            (6,) + tile,
            (slab + 1, 2) + tile,
            (2, 2, 2, count) + tile,
        ),
        (SMEM, SMEM, SMEM, VMEM, VMEM, VMEM, VMEM),
        cost=40_000_000,
        name="start",
    )
    sends = tuple(
        (size, 2 * (b - a) + (2 if a == 0 else 0)) + tile for a, b in spans
    )
    full, *sends = call(
        arrange_kernel,
        (got_even, got_odd, ends, emits, media, power),
        ((2, 2, count) + tile,) + sends,
        (VMEM,) * 6,
        cost=1_000_000,
        name="arrange",
    )
    got = [lax.all_to_all(send, "depth", 0, 0) for send in sends]
    near, near_residual, near_media, near_power = call(
        prepare_kernel,
        (plan, region_kk, got_even, got_odd, sources, ends, media),
        (
            (2, 2, count, DEEP) + tile,
            (2, 2, count, DEEP - 1) + tile,
            (2, 6) + tile,
            (2, slab + 1, 2) + tile,
        ),
        (SMEM, SMEM, VMEM, VMEM, VMEM, VMEM, VMEM),
        cost=2_000_000,
        name="prepare",
    )
    passages = got[0]
    at = 2 * (spans[0][1] - spans[0][0])
    middles = []
    for span, piece in zip(spans, got):
        width = span[1] - span[0]
        middles.append(
            call(
                functools.partial(middle_kernel, span, at),
                (
                    plan, sources, guess, residual, near, near_residual, ends, media,
                    power, near_media, near_power, piece, passages, full,
                ),
                (
                    (2, width, slab + 2 * (DEEP - 3)) + tile,
                    (2, width, slab + 2 * (DEEP - 4)) + tile,
                    (2, 2, width) + tile,
                    (size, 2 * width) + tile,
                ),
                (SMEM,) + (VMEM,) * 13,
                scratch=[
                    pltpu.VMEM((2, width, slab + 2 * DEEP - 2) + tile, jnp.float32),
                    pltpu.VMEM((2, width, slab + 2 * DEEP - 4) + tile, jnp.float32),
                ],
                cost=40_000_000,
                name="middle",
            )
        )
    got = [lax.all_to_all(m[3], "depth", 0, 0) for m in middles]
    out = None
    for span, piece, (solution, next_residual, next_full, _) in zip(spans, got, middles):
        width = span[1] - span[0]
        operands = (
            next_residual, solution, media, power, near_media, near_power,
            piece, passages, next_full,
        )
        spaces = (VMEM,) * 9
        alias = {}
        if out is not None:
            operands += (out,)
            spaces += (ANY,)
            alias = {9: 0}
        (out,) = call(
            functools.partial(final_kernel, span, at, out is not None),
            operands,
            (field,),
            spaces,
            (ANY,),
            scratch=[
                pltpu.VMEM((2, width, slab + 4) + tile, jnp.float32),
                pltpu.VMEM((2, width, slab + 2) + tile, jnp.float32),
                pltpu.VMEM((2, width, slab) + tile, jnp.float32),
                pltpu.SemaphoreType.DMA((2,)),
            ],
            cost=30_000_000,
            alias=alias,
            name="final",
        )
    return out


def solution(mesh):
    return jax.shard_map(
        local,
        mesh=mesh,
        in_specs=(
            P(None, "groups", None, None),
            P("groups"),
            P("depth", "groups", None),
            P("depth", "groups", None),
            P(),
            P("groups"),
            P(None, "groups", "depth", None, None),
        ),
        out_specs=P(None, "groups", "depth", None, None),
        check_vma=False,
    )
```

```python
import functools

import jax
import jax.numpy as jnp
from jax import lax
from jax.experimental import pallas as pl
from jax.experimental.pallas import tpu as pltpu
from jax.sharding import PartitionSpec as P

relax_weight = 0.8
shift_ratio = 0.5
damping = 3.0
coupling = 0.25
keep = 1.0 - relax_weight

DEEP = 6
UNROLL = 4
PIECES = 4


def cmul(a, b):
    return a[0] * b[0] - a[1] * b[1], a[0] * b[1] + a[1] * b[0]


def add(a, b):
    return a[0] + b[0], a[1] + b[1]


def scale(c, a):
    return c * a[0], c * a[1]


def pick(cond, a, b):
    return jnp.where(cond, a[0], b[0]), jnp.where(cond, a[1], b[1])


def tile_of(ref, *at):
    return ref[at + (0,)], ref[at + (1,)]


class Inward:
    def __init__(self, source, target, sem):
        self.ref = target
        self.copy = pltpu.make_async_copy(source, target, sem)
        self.copy.start()

    def wait(self):
        self.copy.wait()
        return self.ref


def kernel_call(body, inputs, outputs, scratch=(), pieces=0, cost=0, name=None):
    n_in, n_out = len(inputs), len(outputs)
    extra = []
    for array, place in inputs:
        if place != "hbm":
            space = pltpu.SMEM if place == "smem" else pltpu.VMEM
            extra.append(space(array.shape, array.dtype))
    for shape, place in outputs:
        if place != "hbm":
            extra.append(pltpu.VMEM(shape, jnp.float32))
    n_extra = len(extra)

    def kernel(*refs):
        ins, outs = refs[:n_in], refs[n_in : n_in + n_out]
        buffers = iter(refs[n_in + n_out : n_in + n_out + n_extra])
        sems = refs[n_in + n_out + n_extra]
        rest = refs[n_in + n_out + n_extra + 1 :]
        used = iter(range(n_extra + pieces))
        pending = []

        def start(source, target):
            return Inward(source, target, sems.at[next(used)])

        def send(source, target):
            pending.append(start(source, target))

        def arrive():
            given = []
            for ref, (_, place) in zip(ins, inputs):
                given.append(ref if place == "hbm" else start(ref, next(buffers)))
            return given

        given = arrive()
        made = []
        for ref, (_, place) in zip(outs, outputs):
            if place == "hbm":
                made.append(ref)
            else:
                buffer = next(buffers)
                made.append((buffer, functools.partial(send, buffer, ref)))
        body(start, send, given, made, rest)
        for copy in pending:
            copy.wait()

    anywhere = pl.BlockSpec(memory_space=pl.ANY)
    return pl.pallas_call(
        kernel,
        out_shape=tuple(jax.ShapeDtypeStruct(s, jnp.float32) for s, _ in outputs),
        in_specs=[anywhere] * n_in,
        out_specs=(anywhere,) * n_out,
        scratch_shapes=[
            *extra,
            pltpu.SemaphoreType.DMA((n_extra + pieces,)),
            *scratch,
        ],
        compiler_params=pltpu.CompilerParams(vmem_limit_bytes=62 << 20),
        cost_estimate=pl.CostEstimate(
            flops=cost, bytes_accessed=4 << 20, transcendentals=0
        ),
        name=name,
    )(*[array for array, _ in inputs])


class Field:
    def __init__(self, ref, first, height):
        self.ref, self.first, self.height = ref, first, height

    @staticmethod
    def shape(count, planes, tile):
        return pltpu.VMEM((2, count, (2 * planes + 1) * tile[0], tile[1]), jnp.float32)

    def rows(self, plane, shift=0):
        start = (2 * (plane - self.first) + 1) * self.height + shift
        if shift % self.height == 0:
            start = pl.multiple_of(start, self.height)
        return pl.ds(start, self.height)

    def clear(self):
        edge = self.ref[:, :, : self.height]
        self.ref[:, :, : self.height] = jnp.zeros_like(edge)

    def get(self, part, plane, shift=0):
        return self.ref[part, :, self.rows(plane, shift)]

    def both(self, plane):
        return self.get(0, plane), self.get(1, plane)

    def put(self, part, plane, value):
        self.ref[part, :, self.rows(plane)] = value
        self.ref[part, :, self.rows(plane, self.height)] = jnp.zeros_like(value)

    def put_both(self, plane, value):
        for part in range(2):
            self.put(part, plane, value[part])

    def bump(self, plane, s, value):
        for part in range(2):
            self.ref[part, s, self.rows(plane)] += value[part]

    def around(self, plane, masks):
        heres, totals = [], []
        for part in range(2):
            here = self.get(part, plane)
            breadth = here.shape[-1]
            lanes = here.ndim - 1
            ahead = jnp.where(masks[0], pltpu.roll(here, 1, lanes), 0.0)
            behind = jnp.where(masks[1], pltpu.roll(here, breadth - 1, lanes), 0.0)
            beside = self.get(part, plane, -1) + self.get(part, plane, 1)
            depth = self.get(part, plane - 1) + self.get(part, plane + 1)
            heres.append(here)
            totals.append((beside + depth) + (ahead + behind))
        return tuple(heres), tuple(totals)

    def minus_a(self, plane, diagonal, layer3, masks):
        here, total = self.around(plane, masks)
        return (
            (total[0] - diagonal * here[0]) + layer3 * here[1],
            (total[1] - diagonal * here[1]) - layer3 * here[0],
        )


def lane_masks(tile):
    lane = lax.broadcasted_iota(jnp.int32, tile, 1)
    return lane > 0, lane < tile[1] - 1


def coefficients(squared, layer):
    diagonal = 6.0 - squared
    imag = shift_ratio * squared + damping * layer
    size = diagonal * diagonal + imag * imag
    return diagonal, (relax_weight * diagonal / size, -relax_weight * imag / size)


def wave(absorb, squared, slab):
    size = jnp.exp(-absorb / slab)
    angle = jnp.sqrt(squared)
    return size * jnp.cos(angle), size * jnp.sin(angle)


def region_values(labels, kk_ref):
    squared = jnp.zeros(labels.shape, jnp.float32)
    for region in range(kk_ref.shape[0]):
        squared = jnp.where(labels == region, kk_ref[region], squared)
    return squared


def loop(start, stop, body, carry, unroll=UNROLL):
    trips = (stop - start) // unroll

    def several(trip, carry):
        for i in range(unroll):
            carry = body(start + trip * unroll + i, carry)
        return carry

    if trips > 1:
        carry = lax.fori_loop(0, trips, several, carry)
        start += trips * unroll
    for plane in range(start, stop):
        carry = body(plane, carry)
    return carry


def cuts(planes):
    edges = [planes * i // PIECES for i in range(PIECES + 1)]
    return list(zip(edges[:-1], edges[1:]))


def start_kernel(start, send, given, made, rest):
    plan, kk, damp, sources, absorb, labels, guess = given
    residual, (emits, emits_out), (media, media_out), (power, power_out) = made
    loaded, held, ref = rest
    _, count, slab, height, breadth = guess.shape
    tile = (height, breadth)
    copies = []
    edges = [0] + [min(b + 1, slab) for _, b in cuts(slab)]
    for a, b in zip(edges[:-1], edges[1:]):
        part = pl.ds(a, b - a)
        copies.append(start(guess.at[:, :, part], loaded.at[:, :, part]))
    masks = lane_masks(tile)
    field = Field(ref, -1, height)
    zero = jnp.zeros((count,) + tile, jnp.float32)
    field.clear()
    field.put_both(-1, (zero, zero))
    field.put_both(slab, (zero, zero))

    plan, kk, damp = plan.wait(), kk.wait(), damp.wait()
    row = lax.broadcasted_iota(jnp.int32, tile, 0)
    lane = lax.broadcasted_iota(jnp.int32, tile, 1)
    cell = row * breadth + lane

    def mark(i, hit):
        return jnp.where(cell == damp[i], 1.0, hit)

    layer = loop(0, damp.shape[0], mark, jnp.zeros(tile, jnp.float32), 16)
    sources, absorb, labels = sources.wait(), absorb.wait(), labels.wait()
    squared = region_values(labels[0], kk)
    diagonal, inverse = coefficients(squared, layer)
    layer3 = damping * layer
    factor = wave(absorb[0], squared, slab)
    for i, value in enumerate((*inverse, diagonal, layer3, *factor)):
        media[i] = value
    media_out()

    def load(p):
        for part in range(2):
            field.put(part, p, loaded[part, :, p])

    def plane(k, carry):
        toward_next, toward_prev, w = carry
        power[k, 0], power[k, 1] = w
        r = field.minus_a(k, diagonal, layer3, masks)
        for part in range(2):
            held[part, :, k] = r[part]
        toward_next = add(cmul(factor, toward_next), r)
        toward_prev = add(toward_prev, cmul(w, r))
        return toward_next, toward_prev, cmul(factor, w)

    one = jnp.ones(tile, jnp.float32), jnp.zeros(tile, jnp.float32)
    carry = ((zero, zero), (zero, zero), one)
    for (a, b), copy in zip(cuts(slab), copies):
        copy.wait()
        if a == 0:
            load(0)
        top = min(b, slab - 1)

        def group(trip, carry):
            for i in range(UNROLL):
                load(a + trip * UNROLL + i + 1)
            for i in range(UNROLL):
                carry = plane(a + trip * UNROLL + i, carry)
            return carry

        trips = (top - a) // UNROLL
        carry = lax.fori_loop(0, trips, group, carry)
        for k in range(a + trips * UNROLL, b):
            if k + 1 < slab:
                load(k + 1)
            carry = plane(k, carry)
        part = pl.ds(a, b - a)
        send(held.at[:, :, part], residual.at[:, :, part])
    toward_next, toward_prev, w = carry
    power[slab, 0], power[slab, 1] = w
    power_out()
    for part in range(2):
        emits[0, part] = toward_next[part]
        emits[1, part] = toward_prev[part]
    force_emits(plan, 0, emits, sources, power, slab)
    emits_out()


def force_emits(plan, shift, emits, sources, power, slab):
    first_plane = lax.axis_index("depth") * slab
    for s in range(sources.shape[1]):
        k = plan[s] - first_plane

        @pl.when((k >= 0) & (k < slab))
        def _():
            src = sources[0, s], sources[1, s]
            onward = cmul(tile_of(power, slab - 1 - k), src)
            back = cmul(tile_of(power, k), src)
            for part in range(2):
                emits[0, part, s] += onward[part]
                emits[1, part, s] += back[part]


def fill_send(send, full, passage):
    place = lax.axis_index("depth")
    count = full.shape[2]

    def one(j, unused):
        way = jnp.where(j > place, 0, 1)
        for part in range(2):
            send[j, pl.ds(part * count, count)] = full[way, part]
        if passage is not None:
            send[j, 2 * count] = passage[0]
            send[j, 2 * count + 1] = passage[1]
        return unused

    loop(0, send.shape[0], one, 0, 4)


def arrange_kernel(start, send, given, made, rest):
    got_even, got_odd, emits, power = given
    (full, full_out), (slots, slots_out) = made
    (weights,) = rest
    slab = power.shape[0] - 1
    copy = start(power.at[pl.ds(slab - 1, 2)], weights)
    even = lax.rem(lax.axis_index("depth"), 2) == 0
    got_even, got_odd, emits = got_even.wait(), got_odd.wait(), emits.wait()
    copy.wait()
    count = emits.shape[2]
    weight = tile_of(weights, 0)
    for s in range(count):
        at = [(part * count + s) * DEEP for part in range(2)]
        low = tuple(
            jnp.where(even, got_odd[i + DEEP - 1], got_even[i + DEEP - 1]) for i in at
        )
        high = tuple(jnp.where(even, got_even[i], got_odd[i]) for i in at)
        toward_next = add(add(cmul(weight, low), high), (emits[0, 0, s], emits[0, 1, s]))
        toward_prev = add(add(cmul(weight, high), low), (emits[1, 0, s], emits[1, 1, s]))
        for part in range(2):
            full[0, part, s] = toward_next[part]
            full[1, part, s] = toward_prev[part]
    fill_send(slots, full, tile_of(weights, 1))
    slots_out()
    full_out()


def prepare_kernel(start, send, given, made, rest):
    plan, kk, got_even, got_odd, sources, media, guess = given
    (near, near_out), (res, res_out), (near_media, media_out), (waves, waves_out) = made
    ends, ref = rest
    _, count, slab, height, breadth = guess.shape
    tile = (height, breadth)
    copies = [
        start(guess.at[:, :, slab - 1 if end else 0], ends.at[end]) for end in range(2)
    ]
    plan, kk = plan.wait(), kk.wait()
    got_even, got_odd = got_even.wait(), got_odd.wait()
    sources, media = sources.wait(), media.wait()
    masks = lane_masks(tile)
    place = lax.axis_index("depth")
    last_place = lax.axis_size("depth") - 1
    even = lax.rem(place, 2) == 0
    tiles = 2 * count * DEEP
    layer3 = media[3]
    layer = layer3 / damping
    factors, diagonals = [], []
    for side in range(2):
        first, second = (got_odd, got_even) if side == 0 else (got_even, got_odd)
        for i in range(2 * count):
            rows = pl.ds(i * DEEP, DEEP)
            near[side, i // count, i % count] = jnp.where(
                even, first[rows], second[rows]
            )
        absorb = jnp.where(even, first[tiles], second[tiles])
        labels = jnp.where(even, first[tiles + 1], second[tiles + 1]).astype(jnp.int32)
        squared = region_values(labels, kk)
        diagonal, inverse = coefficients(squared, layer)
        inside = (place > 0) if side == 0 else (place < last_place)
        inverse = tuple(jnp.where(inside, v, 0.0) for v in inverse)
        factor = wave(absorb, squared, slab)
        for i, value in enumerate((*inverse, diagonal, layer3, *factor)):
            near_media[side, i] = value
        factors.append(factor)
        diagonals.append(diagonal)
    near_out()
    media_out()

    ws = list(factors)
    edge = DEEP - 1

    def keep_power(k, ws):
        for side in range(2):
            for way in range(2):
                if side == way:
                    i = k - (slab - edge + 1)
                    i = edge - 1 - i if side else i
                else:
                    i = k - 1
                    i = i if side else edge - 1 - i
                if 0 <= i < edge:
                    for part in range(2):
                        waves[side, way, i, part] = ws[side][part]

    def next_power(k, ws):
        return tuple(cmul(factors[side], ws[side]) for side in range(2))

    k = 1
    while k <= slab:
        if edge < k < slab - edge + 1:
            ws = loop(k, slab - edge + 1, next_power, tuple(ws), 8)
            k = slab - edge + 1
        keep_power(k, ws)
        ws = next_power(k, ws)
        k += 1
    waves_out()
    for copy in copies:
        copy.wait()
    for side in range(2):
        field = Field(ref, 0, height)
        field.clear()
        for i in range(DEEP + 1):
            for part in range(2):
                if side == 0:
                    value = near[0, part, :, i] if i < DEEP else ends[0, part]
                else:
                    value = near[1, part, :, i - 1] if i > 0 else ends[1, part]
                field.put(part, i, value)
        for i in range(1, DEEP):
            r = field.minus_a(i, diagonals[side], layer3, masks)
            for part in range(2):
                res[side, part, :, i - 1] = r[part]
    for s in range(count):
        k = plan[s] - place * slab
        for side, low in ((0, -edge), (1, slab)):
            i = k - low

            @pl.when((i >= 0) & (i < edge))
            def _():
                for part in range(2):
                    res[side, part, s, i] += sources[part, s]

    res_out()


def incoming_waves(got, passages, full, passage):
    place = lax.axis_index("depth")
    last_place = lax.axis_size("depth") - 1
    count = full.shape[2]
    zero = jnp.zeros(full.shape[2:], jnp.float32)

    def step(j, state):
        came = got[j, pl.ds(0, count)], got[j, pl.ds(count, count)]
        return add(cmul(passages(j), state), came)

    below = jnp.maximum(place - 1, 0)
    above = jnp.minimum(place + 1, last_place)
    next_low = lax.fori_loop(0, below, step, (zero, zero))
    next_own = pick(place > 0, step(below, next_low), (zero, zero))
    prev_high = lax.fori_loop(
        0, last_place - above, lambda t, state: step(last_place - t, state), (zero, zero)
    )
    prev_own = pick(place < last_place, step(above, prev_high), (zero, zero))
    next_high = add(cmul(passage, next_own), (full[0, 0], full[0, 1]))
    prev_low = add(cmul(passage, prev_own), (full[1, 0], full[1, 1]))
    return [
        (scale(coupling, a), scale(coupling, b))
        for a, b in ((next_low, prev_low), (next_own, prev_own), (next_high, prev_high))
    ]


def update_passes(
    reach, slab, tile, incoming, residual_of, media, near_media, power, waves,
    refs, ready, after_first, emit, done, masks,
):
    edge = DEEP - 1
    first_update = Field(refs[0], -reach, tile[0])
    second_update = Field(refs[1], 1 - reach, tile[0])
    first_update.clear()
    second_update.clear()
    own = lambda p: (tile_of(power, p + 1), tile_of(power, slab - p))
    low = lambda p: (tile_of(waves, 0, 0, p + edge), tile_of(waves, 0, 1, p + edge))
    high = lambda p: (tile_of(waves, 1, 0, p - slab), tile_of(waves, 1, 1, p - slab))
    sides = (
        (-reach, 0, near_media.at[0], low, incoming[0]),
        (0, slab, media, own, incoming[1]),
        (slab, slab + reach, near_media.at[1], high, incoming[2]),
    )

    def begin(which, p):
        _, _, m, powers, (onward, back) = sides[which]
        on, off = powers(p)
        c = add(cmul(on, onward), cmul(off, back))
        first_update.put_both(p, cmul((m[0], m[1]), add(c, residual_of(which, p))))

    for which in (0, 2):
        for p in range(*sides[which][:2]):
            begin(which, p)
    for piece, (a, b) in enumerate(cuts(slab)):
        ready(piece)
        loop(a, b, lambda p, unused: begin(1, p) or unused, 0)
    after_first(first_update)

    def second(m, p):
        here, total = first_update.around(p, masks)
        u = add(scale(1.0 + keep, here), cmul((m[0], m[1]), total))
        second_update.put_both(p, u)

    def third(which, m, p):
        here, total = second_update.around(p, masks)
        u = add(scale(keep, here), cmul((m[0], m[1]), total))
        emit(which, p, add(u, first_update.both(p)))

    for which, (a, b, m, *_) in enumerate(sides):
        a, b = max(a, 1 - reach), min(b, slab + reach - 1)
        loop(a, b, lambda p, unused: second(m, p) or unused, 0)
    for which, (a, b, m, *_) in enumerate(sides):
        a, b = max(a, 2 - reach), min(b, slab + reach - 2)
        spans = cuts(slab) if which == 1 else [(a, b)]
        for piece, (a, b) in enumerate(spans):
            loop(a, b, lambda p, unused: third(which, m, p) or unused, 0)
            if which == 1:
                done(piece)


def middle_kernel(start, send, given, made, rest):
    (
        plan, got, full, sources, media, near_media, waves, near, near_residual, power,
        residual, guess,
    ) = given
    new_field, new_residual, (next_full, full_out), (slots, slots_out) = made
    held, loaded, next_held, *refs = rest
    _, count, slab, height, breadth = guess.shape
    tile = (height, breadth)
    halves = [pl.ds(a, b - a) for a, b in cuts(slab)]
    res_copies = [start(residual.at[:, :, h], held.at[:, :, h]) for h in halves]
    field_copies = [start(guess.at[:, :, h], loaded.at[:, :, h]) for h in halves]
    masks = lane_masks(tile)
    place = lax.axis_index("depth")
    reach = DEEP - 1
    ext = reach - 2
    more = ext - 1
    new = Field(refs[2], -ext, height)
    new.clear()
    plan, got, full, sources = plan.wait(), got.wait(), full.wait(), sources.wait()
    media, near_media, waves = media.wait(), near_media.wait(), waves.wait()
    near, near_residual, power = near.wait(), near_residual.wait(), power.wait()
    incoming = incoming_waves(
        got, lambda j: (got[j, 2 * count], got[j, 2 * count + 1]), full, tile_of(power, slab)
    )

    def residual_of(which, p):
        if which == 1:
            return held[0, :, p], held[1, :, p]
        i = p + reach if which == 0 else p - slab
        return near_residual[which // 2, 0, :, i], near_residual[which // 2, 1, :, i]

    def ready(piece):
        res_copies[piece].wait()

    def after_first(update):
        inverse = media[0], media[1]
        for side, (p, i) in enumerate(((0, DEEP - 1), (slab - 1, 0))):
            lacks = cmul(inverse, (near[side, 0, :, i], near[side, 1, :, i]))
            update.put_both(p, add(update.both(p), lacks))
        for s in range(count):
            k = plan[s] - place * slab

            @pl.when((k >= 0) & (k < slab))
            def _():
                update.bump(k, s, cmul(inverse, (sources[0, s], sources[1, s])))

        for copy in field_copies:
            copy.wait()

    def emit(which, p, u):
        for part in range(2):
            if which == 1:
                value = loaded[part, :, p] + u[part]
                loaded[part, :, p] = value
            else:
                i = p + DEEP if which == 0 else p - slab
                value = near[which // 2, part, :, i] + u[part]
            new.put(part, p, value)

    def done(piece):
        send(loaded.at[:, :, halves[piece]], new_field.at[:, :, halves[piece]])

    update_passes(
        reach, slab, tile, incoming, residual_of, media, near_media, power, waves,
        refs, ready, after_first, emit, done, masks,
    )

    layer3 = media[3]
    factor = media[4], media[5]

    def outside(side):
        def one(p, unused):
            r = new.minus_a(p, near_media[side, 2], layer3, masks)
            for part in range(2):
                next_held[part, :, p + more] = r[part]
            return unused

        return one

    loop(-more, 0, outside(0), 0)
    loop(slab, slab + more, outside(1), 0)
    diagonal = media[2]

    def inside(p, carry):
        toward_next, toward_prev = carry
        r = new.minus_a(p, diagonal, layer3, masks)
        for part in range(2):
            next_held[part, :, p + more] = r[part]
        toward_next = add(cmul(factor, toward_next), r)
        toward_prev = add(toward_prev, cmul(tile_of(power, p), r))
        return toward_next, toward_prev

    zero = jnp.zeros((count,) + tile, jnp.float32)
    carry = ((zero, zero), (zero, zero))
    for piece, (a, b) in enumerate(cuts(slab)):
        carry = loop(a, b, inside, carry)
        low = a + more if piece else 0
        high = b + more if piece < PIECES - 1 else slab + 2 * more
        part = pl.ds(low, high - low)
        send(next_held.at[:, :, part], new_residual.at[:, :, part])
    for way in range(2):
        for part in range(2):
            next_full[way, part] = carry[way][part]
    force_emits(plan, 0, next_full, sources, power, slab)
    fill_send(slots, next_full, None)
    slots_out()
    full_out()


def final_kernel(start, send, given, made, rest):
    (
        plan, got, full, sources, media, near_media, waves, power, passages,
        residual, field,
    ) = given
    (out,) = made
    passage_of, held, loaded, *refs = rest
    _, count, slab, height, breadth = field.shape
    tile = (height, breadth)
    copy = start(passages.at[:, pl.ds(2 * count, 2)], passage_of)
    halves = [pl.ds(a, b - a) for a, b in cuts(slab)]
    reach = 2
    res_copies = []
    for piece, (a, b) in enumerate(cuts(slab)):
        low = a + reach if piece else 0
        high = b + reach if piece < PIECES - 1 else slab + 2 * reach
        part = pl.ds(low, high - low)
        res_copies.append(start(residual.at[:, :, part], held.at[:, :, part]))
    field_copies = [start(field.at[:, :, h], loaded.at[:, :, h]) for h in halves]
    masks = lane_masks(tile)
    place = lax.axis_index("depth")
    plan, got, full, sources = plan.wait(), got.wait(), full.wait(), sources.wait()
    media, near_media, waves = media.wait(), near_media.wait(), waves.wait()
    power = power.wait()
    copy.wait()
    incoming = incoming_waves(
        got, lambda j: tile_of(passage_of, j), full, tile_of(power, slab)
    )
    for copy in (res_copies[0], res_copies[-1]):
        copy.wait()

    def residual_of(which, p):
        return held[0, :, p + reach], held[1, :, p + reach]

    def ready(piece):
        if 0 < piece < PIECES - 1:
            res_copies[piece].wait()

    def after_first(update):
        for s in range(count):
            k = plan[s] - place * slab
            src = sources[0, s], sources[1, s]
            for m, a, b in (
                (media, 0, slab),
                (near_media.at[0], -reach, 0),
                (near_media.at[1], slab, slab + reach),
            ):

                @pl.when((k >= a) & (k < b))
                def _():
                    update.bump(k, s, cmul((m[0], m[1]), src))

        for copy in field_copies:
            copy.wait()

    def emit(which, p, u):
        for part in range(2):
            loaded[part, :, p] += u[part]

    def done(piece):
        send(loaded.at[:, :, halves[piece]], out.at[:, :, halves[piece]])

    update_passes(
        reach, slab, tile, incoming, residual_of, media, near_media, power, waves,
        refs, ready, after_first, emit, done, masks,
    )


def local(sources, plan, absorb, labels, region_kk, damp_cells, guess):
    size = lax.axis_size("depth")
    place = lax.axis_index("depth")
    _, count, slab, height, breadth = guess.shape
    tile = (height, breadth)
    edge = DEEP - 1
    planes = lambda n: (2, count, n) + tile
    scratch = lambda shape: pltpu.VMEM(shape, jnp.float32)

    even = place % 2 == 0
    top = slab - DEEP

    def payload(first):
        part = lax.dynamic_slice_in_dim(guess, first, DEEP, axis=2)
        return jnp.concatenate(
            [part.reshape((-1,) + tile), absorb, labels.astype(jnp.float32)], axis=0
        )

    even_pairs = [(i, i ^ 1) for i in range(size) if i ^ 1 < size]
    odd_pairs = [(i, i + 1) for i in range(1, size - 1, 2)]
    odd_pairs += [(b, a) for a, b in odd_pairs]
    got_odd = lax.ppermute(payload(jnp.where(even, 0, top)), "depth", odd_pairs)
    got_even = lax.ppermute(payload(jnp.where(even, top, 0)), "depth", even_pairs)

    residual, emits, media, power = kernel_call(
        start_kernel,
        [
            (plan, "smem"), (region_kk, "smem"), (damp_cells, "smem"),
            (sources, "vmem"), (absorb, "vmem"), (labels, "vmem"), (guess, "hbm"),
        ],
        [
            (planes(slab), "hbm"), ((2, 2, count) + tile, "vmem"),
            ((6,) + tile, "vmem"), ((slab + 1, 2) + tile, "vmem"),
        ],
        [scratch(planes(slab)), scratch(planes(slab)), Field.shape(count, slab + 2, tile)],
        pieces=2 * PIECES, cost=20_000_000, name="start",
    )
    full, slots = kernel_call(
        arrange_kernel,
        [(got_even, "vmem"), (got_odd, "vmem"), (emits, "vmem"), (power, "hbm")],
        [((2, 2, count) + tile, "vmem"), ((size, 2 * count + 2) + tile, "vmem")],
        [scratch((2, 2) + tile)],
        pieces=1, cost=1_000_000, name="arrange",
    )
    first_got = lax.all_to_all(slots, "depth", 0, 0)
    near, near_residual, near_media, waves = kernel_call(
        prepare_kernel,
        [
            (plan, "smem"), (region_kk, "smem"), (got_even, "vmem"), (got_odd, "vmem"),
            (sources, "vmem"), (media, "vmem"), (guess, "hbm"),
        ],
        [
            ((2, 2, count, DEEP) + tile, "vmem"), ((2, 2, count, edge) + tile, "vmem"),
            ((2, 6) + tile, "vmem"), ((2, 2, edge, 2) + tile, "vmem"),
        ],
        [scratch((2, 2, count) + tile), Field.shape(count, DEEP + 1, tile)],
        pieces=2, cost=4_000_000, name="prepare",
    )
    new_field, new_residual, next_full, slots = kernel_call(
        middle_kernel,
        [
            (plan, "smem"), (first_got, "vmem"), (full, "vmem"), (sources, "vmem"),
            (media, "vmem"), (near_media, "vmem"), (waves, "vmem"), (near, "vmem"),
            (near_residual, "vmem"), (power, "vmem"), (residual, "hbm"), (guess, "hbm"),
        ],
        [
            (planes(slab), "hbm"), (planes(slab + 2 * (DEEP - 4)), "hbm"),
            ((2, 2, count) + tile, "vmem"), ((size, 2 * count) + tile, "vmem"),
        ],
        [
            scratch(planes(slab)), scratch(planes(slab)),
            scratch(planes(slab + 2 * (DEEP - 4))),
            Field.shape(count, slab + 2 * edge, tile),
            Field.shape(count, slab + 2 * edge - 2, tile),
            Field.shape(count, slab + 2 * edge - 4, tile),
        ],
        pieces=4 * PIECES, cost=80_000_000, name="middle",
    )
    got = lax.all_to_all(slots, "depth", 0, 0)
    (out,) = kernel_call(
        final_kernel,
        [
            (plan, "smem"), (got, "vmem"), (next_full, "vmem"), (sources, "vmem"),
            (media, "vmem"), (near_media, "vmem"), (waves, "vmem"), (power, "vmem"),
            (first_got, "hbm"), (new_residual, "hbm"), (new_field, "hbm"),
        ],
        [(planes(slab), "hbm")],
        [
            scratch((size, 2) + tile),
            scratch(planes(slab + 2 * (DEEP - 4))), scratch(planes(slab)),
            Field.shape(count, slab + 4, tile), Field.shape(count, slab + 2, tile),
        ],
        pieces=3 * PIECES + 1, cost=60_000_000, name="final",
    )
    return out


def solution(mesh):
    return jax.shard_map(
        local,
        mesh=mesh,
        in_specs=(
            P(None, "groups", None, None),
            P("groups"),
            P("depth", "groups", None),
            P("depth", "groups", None),
            P(),
            P("groups"),
            P(None, "groups", "depth", None, None),
        ),
        out_specs=P(None, "groups", "depth", None, None),
        check_vma=False,
    )
```

```python
import functools

import jax
import jax.numpy as jnp
from jax import lax
from jax.experimental import pallas as pl
from jax.experimental.pallas import tpu as pltpu
from jax.sharding import PartitionSpec as P

relax_weight = 0.8
shift_ratio = 0.5
damping = 3.0
coupling = 0.25
keep = 1.0 - relax_weight

DEEP = 6
UNROLL = 4
PIECES = 4


def cmul(a, b):
    return a[0] * b[0] - a[1] * b[1], a[0] * b[1] + a[1] * b[0]


def add(a, b):
    return a[0] + b[0], a[1] + b[1]


def scale(c, a):
    return c * a[0], c * a[1]


def pick(cond, a, b):
    return jnp.where(cond, a[0], b[0]), jnp.where(cond, a[1], b[1])


def tile_of(ref, *at):
    return ref[at + (0,)], ref[at + (1,)]


class Inward:
    def __init__(self, source, target, sem):
        self.ref = target
        self.copy = pltpu.make_async_copy(source, target, sem)
        self.copy.start()

    def wait(self):
        self.copy.wait()
        return self.ref


def kernel_call(body, inputs, outputs, scratch=(), pieces=0, cost=0, name=None, limit=62):
    n_in, n_out = len(inputs), len(outputs)
    extra = []
    for array, place in inputs:
        if place in ("vmem", "smem"):
            space = pltpu.SMEM if place == "smem" else pltpu.VMEM
            extra.append(space(array.shape, array.dtype))
    for shape, place in outputs:
        if place == "vmem":
            extra.append(pltpu.VMEM(shape, jnp.float32))
    n_extra = len(extra)

    def kernel(*refs):
        ins, outs = refs[:n_in], refs[n_in : n_in + n_out]
        buffers = iter(refs[n_in + n_out : n_in + n_out + n_extra])
        sems = refs[n_in + n_out + n_extra]
        rest = refs[n_in + n_out + n_extra + 1 :]
        used = iter(range(n_extra + pieces))
        pending = []

        def start(source, target):
            return Inward(source, target, sems.at[next(used)])

        def send(source, target):
            pending.append(start(source, target))

        def arrive():
            given = []
            for ref, (_, place) in zip(ins, inputs):
                copied = place in ("vmem", "smem")
                given.append(start(ref, next(buffers)) if copied else ref)
            return given

        given = arrive()
        made = []
        for ref, (_, place) in zip(outs, outputs):
            if place != "vmem":
                made.append(ref)
            else:
                buffer = next(buffers)
                made.append((buffer, functools.partial(send, buffer, ref)))
        body(start, send, given, made, rest)
        for copy in pending:
            copy.wait()

    def spec(place):
        return pl.BlockSpec(memory_space=pltpu.VMEM if place == "direct" else pl.ANY)

    return pl.pallas_call(
        kernel,
        out_shape=tuple(jax.ShapeDtypeStruct(s, jnp.float32) for s, _ in outputs),
        in_specs=[spec(place) for _, place in inputs],
        out_specs=tuple(spec(place) for _, place in outputs),
        scratch_shapes=[
            *extra,
            pltpu.SemaphoreType.DMA((max(1, n_extra + pieces),)),
            *scratch,
        ],
        compiler_params=pltpu.CompilerParams(vmem_limit_bytes=limit << 20),
        cost_estimate=pl.CostEstimate(
            flops=cost, bytes_accessed=4 << 20, transcendentals=0
        ),
        name=name,
    )(*[array for array, _ in inputs])


def lane_sum(here, masks):
    breadth = here.shape[-1]
    axis = here.ndim - 1
    ahead = jnp.where(masks[0], pltpu.roll(here, 1, axis), 0.0)
    behind = jnp.where(masks[1], pltpu.roll(here, breadth - 1, axis), 0.0)
    return ahead + behind


class Field:
    def __init__(self, ref, first, height):
        self.ref, self.first, self.height = ref, first, height

    @staticmethod
    def shape(count, planes, tile):
        return pltpu.VMEM((2, count, (2 * planes + 1) * tile[0], tile[1]), jnp.float32)

    def rows(self, plane, shift=0):
        start = (2 * (plane - self.first) + 1) * self.height + shift
        if shift % self.height == 0:
            start = pl.multiple_of(start, self.height)
        return pl.ds(start, self.height)

    def clear(self):
        edge = self.ref[:, :, : self.height]
        self.ref[:, :, : self.height] = jnp.zeros_like(edge)

    def get(self, part, plane, shift=0):
        return self.ref[part, :, self.rows(plane, shift)]

    def both(self, plane):
        return self.get(0, plane), self.get(1, plane)

    def put(self, part, plane, value):
        self.ref[part, :, self.rows(plane)] = value
        self.ref[part, :, self.rows(plane, self.height)] = jnp.zeros_like(value)

    def put_both(self, plane, value):
        for part in range(2):
            self.put(part, plane, value[part])

    def bump(self, plane, s, value):
        for part in range(2):
            self.ref[part, s, self.rows(plane)] += value[part]

    def lanes(self, part, plane, masks):
        return lane_sum(self.get(part, plane), masks)

    def around(self, plane, lanes):
        heres, totals = [], []
        for part in range(2):
            here = self.get(part, plane)
            beside = self.get(part, plane, -1) + self.get(part, plane, 1)
            depth = self.get(part, plane - 1) + self.get(part, plane + 1)
            heres.append(here)
            totals.append((beside + depth) + lanes(part, plane))
        return tuple(heres), tuple(totals)

    def minus_a(self, plane, diagonal, layer3, lanes):
        here, total = self.around(plane, lanes)
        return (
            (total[0] - diagonal * here[0]) + layer3 * here[1],
            (total[1] - diagonal * here[1]) - layer3 * here[0],
        )


class Lanes:
    def __init__(self, field, ref, masks):
        self.field, self.ref, self.masks = field, ref, masks

    def now(self, part, plane):
        return self.field.lanes(part, plane, self.masks)

    def kept(self, part, plane):
        return self.ref[part, :, plane]

    def fill(self, plane):
        for part in range(2):
            self.ref[part, :, plane] = self.now(part, plane)

    def sweep(self, start, stop, total, body, carry, before=None):
        trips = (stop - start) // UNROLL
        assert trips * UNROLL == stop - start

        def group(base, carry, ahead):
            if before is not None:
                for i in range(UNROLL):
                    before(base + i)
            if ahead:
                for i in range(UNROLL):
                    self.fill(base + UNROLL + i)
            for i in range(UNROLL):
                carry = body(base + i, carry)
            return carry

        ahead = trips if stop < total else trips - 1
        carry = lax.fori_loop(
            0, ahead, lambda t, c: group(start + t * UNROLL, c, True), carry
        )
        if ahead < trips:
            carry = group(stop - UNROLL, carry, False)
        return carry


def lane_masks(tile):
    lane = lax.broadcasted_iota(jnp.int32, tile, 1)
    return lane > 0, lane < tile[1] - 1


INVERSE, DIAGONAL, LAYER, WAVE, SECOND, THIRD, MEDIA = 0, 2, 3, 4, 6, 8, 10


def set_media(ref, squared, layer, absorb, slab, inside=None):
    diagonal = 6.0 - squared
    imag = shift_ratio * squared + damping * layer
    size = diagonal * diagonal + imag * imag
    inverse = relax_weight * diagonal / size, -relax_weight * imag / size
    if inside is not None:
        inverse = tuple(jnp.where(inside, v, 0.0) for v in inverse)
    grow = 1.0 + keep
    decay = jnp.exp(-absorb / slab)
    angle = jnp.sqrt(squared)
    factor = decay * jnp.cos(angle), decay * jnp.sin(angle)
    values = (
        *inverse, diagonal, damping * layer, *factor,
        *scale(1.0 / grow, inverse), *scale(grow, inverse),
    )
    for i, value in enumerate(values):
        ref[i] = value
    return factor


def pair(ref, i):
    return ref[i], ref[i + 1]


def region_values(labels, kk_ref):
    squared = jnp.zeros(labels.shape, jnp.float32)
    for region in range(kk_ref.shape[0]):
        squared = jnp.where(labels == region, kk_ref[region], squared)
    return squared


def loop(start, stop, body, carry, unroll=UNROLL):
    trips = (stop - start) // unroll

    def several(trip, carry):
        for i in range(unroll):
            carry = body(start + trip * unroll + i, carry)
        return carry

    if trips > 1:
        carry = lax.fori_loop(0, trips, several, carry)
        start += trips * unroll
    for plane in range(start, stop):
        carry = body(plane, carry)
    return carry


def cuts(planes, pieces=PIECES):
    edges = [planes * i // pieces for i in range(pieces + 1)]
    return list(zip(edges[:-1], edges[1:]))


def start_kernel(start, send, given, made, rest):
    plan, kk, damp, sources, absorb, labels, guess = given
    residual, (emits, emits_out), (media, media_out), (power, power_out) = made
    loaded, held, side, ref = rest
    _, count, slab, height, breadth = guess.shape
    tile = (height, breadth)
    copies = []
    edges = [0] + [min(b + UNROLL, slab) for _, b in cuts(slab)]
    for a, b in zip(edges[:-1], edges[1:]):
        part = pl.ds(a, b - a)
        copies.append(start(guess.at[:, :, part], loaded.at[:, :, part]))
    masks = lane_masks(tile)
    field = Field(ref, -1, height)
    zero = jnp.zeros((count,) + tile, jnp.float32)
    field.clear()
    field.put_both(-1, (zero, zero))
    field.put_both(slab, (zero, zero))
    lanes = Lanes(field, side, masks)

    def fill(p):
        for part in range(2):
            value = loaded[part, :, p]
            field.put(part, p, value)
            side[part, :, p] = lane_sum(value, masks)

    lanes.fill = fill

    plan, kk, damp = plan.wait(), kk.wait(), damp.wait()
    row = lax.broadcasted_iota(jnp.int32, tile, 0)
    lane = lax.broadcasted_iota(jnp.int32, tile, 1)
    cell = row * breadth + lane

    def mark(i, hit):
        return jnp.where(cell == damp[i], 1.0, hit)

    layer = loop(0, damp.shape[0], mark, jnp.zeros(tile, jnp.float32), 16)
    sources, absorb, labels = sources.wait(), absorb.wait(), labels.wait()
    squared = region_values(labels[0], kk)
    factor = set_media(media, squared, layer, absorb[0], slab)
    diagonal, layer3 = media[DIAGONAL], media[LAYER]
    media_out()

    def plane(k, carry):
        toward_next, toward_prev, w = carry
        power[k, 0], power[k, 1] = w
        r = field.minus_a(k, diagonal, layer3, lanes.kept)
        for part in range(2):
            held[part, :, k] = r[part]
        toward_next = add(cmul(factor, toward_next), r)
        toward_prev = add(toward_prev, cmul(w, r))
        return toward_next, toward_prev, cmul(factor, w)

    one = jnp.ones(tile, jnp.float32), jnp.zeros(tile, jnp.float32)
    carry = ((zero, zero), (zero, zero), one)
    for (a, b), copy in zip(cuts(slab), copies):
        copy.wait()
        if a == 0:
            for p in range(UNROLL):
                fill(p)
        carry = lanes.sweep(a, b, slab, plane, carry)
        part = pl.ds(a, b - a)
        send(held.at[:, :, part], residual.at[:, :, part])
    toward_next, toward_prev, w = carry
    power[slab, 0], power[slab, 1] = w
    power_out()
    for part in range(2):
        emits[0, part] = toward_next[part]
        emits[1, part] = toward_prev[part]
    force_emits(plan, emits, sources, power, slab)
    emits_out()


def force_emits(plan, emits, sources, power, slab):
    first_plane = lax.axis_index("depth") * slab
    for s in range(sources.shape[1]):
        k = plan[s] - first_plane

        @pl.when((k >= 0) & (k < slab))
        def _():
            src = sources[0, s], sources[1, s]
            onward = cmul(tile_of(power, slab - 1 - k), src)
            back = cmul(tile_of(power, k), src)
            for part in range(2):
                emits[0, part, s] += onward[part]
                emits[1, part, s] += back[part]


def halves(count):
    return (0, count // 2), (count // 2, count)


def fill_send(slots, full, passage):
    place = lax.axis_index("depth")

    def one(chip, unused):
        for core, (a, b) in enumerate(halves(full.shape[2])):
            j = 2 * chip + core
            way = jnp.where(j > place, 0, 1)
            for part in range(2):
                slots[j, pl.ds(part * (b - a), b - a)] = full[way, part, a:b]
            if passage is not None:
                slots[j, 2 * (b - a)] = passage[0]
                slots[j, 2 * (b - a) + 1] = passage[1]
        return unused

    loop(0, slots.shape[0] // 2, one, 0, 4)


def arrange_kernel(start, send, given, made, rest):
    got_even, got_odd, emits, power = given
    (full, full_out), (slots, slots_out), (near, near_out), (extra, extra_out) = made
    (weights,) = rest
    slab = power.shape[0] - 1
    copy = start(power.at[pl.ds(slab - 1, 2)], weights)
    even = lax.rem(lax.axis_index("depth"), 2) == 0
    emits = emits.wait()
    copy.wait()
    count = emits.shape[2]
    weight = tile_of(weights, 0)
    for s in range(count):
        at = [(part * count + s) * DEEP for part in range(2)]
        low = tuple(
            jnp.where(even, got_odd[i + DEEP - 1], got_even[i + DEEP - 1]) for i in at
        )
        high = tuple(jnp.where(even, got_even[i], got_odd[i]) for i in at)
        toward_next = add(add(cmul(weight, low), high), (emits[0, 0, s], emits[0, 1, s]))
        toward_prev = add(add(cmul(weight, high), low), (emits[1, 0, s], emits[1, 1, s]))
        for part in range(2):
            full[0, part, s] = toward_next[part]
            full[1, part, s] = toward_prev[part]
    fill_send(slots, full, tile_of(weights, 1))
    slots_out()
    full_out()
    for side in range(2):
        first, second = (got_odd, got_even) if side == 0 else (got_even, got_odd)
        for i in range(2 * count):
            rows = pl.ds(i * DEEP, DEEP)
            near[side, i // count, i % count] = jnp.where(
                even, first[rows], second[rows]
            )
        for i in range(2):
            at = 2 * count * DEEP + i
            extra[side, i] = jnp.where(even, first[at], second[at])
    near_out()
    extra_out()


def prepare_kernel(start, send, given, made, rest):
    plan, kk, near, extra, sources, media, guess = given
    (res, res_out), (near_media, media_out), (waves, waves_out) = made
    ends, ref = rest
    _, count, slab, height, breadth = guess.shape
    tile = (height, breadth)
    copies = [
        start(guess.at[:, :, slab - 1 if end else 0], ends.at[end]) for end in range(2)
    ]
    plan, kk = plan.wait(), kk.wait()
    near, extra = near.wait(), extra.wait()
    sources, media = sources.wait(), media.wait()
    masks = lane_masks(tile)
    place = lax.axis_index("depth")
    last_place = lax.axis_size("depth") - 1
    layer3 = media[LAYER]
    layer = layer3 / damping
    factors = []
    for side in range(2):
        squared = region_values(extra[side, 1].astype(jnp.int32), kk)
        inside = (place > 0) if side == 0 else (place < last_place)
        factors.append(
            set_media(near_media.at[side], squared, layer, extra[side, 0], slab, inside)
        )
    media_out()

    ws = list(factors)
    edge = DEEP - 1

    def keep_power(k, ws):
        for side in range(2):
            for way in range(2):
                if side == way:
                    i = k - (slab - edge + 1)
                    i = edge - 1 - i if side else i
                else:
                    i = k - 1
                    i = i if side else edge - 1 - i
                if 0 <= i < edge:
                    for part in range(2):
                        waves[side, way, i, part] = ws[side][part]

    def next_power(k, ws):
        return tuple(cmul(factors[side], ws[side]) for side in range(2))

    k = 1
    while k <= slab:
        if edge < k < slab - edge + 1:
            ws = loop(k, slab - edge + 1, next_power, tuple(ws), 8)
            k = slab - edge + 1
        keep_power(k, ws)
        ws = next_power(k, ws)
        k += 1
    waves_out()
    for copy in copies:
        copy.wait()
    for side in range(2):
        field = Field(ref, 0, height)
        field.clear()
        for i in range(DEEP + 1):
            for part in range(2):
                if side == 0:
                    value = near[0, part, :, i] if i < DEEP else ends[0, part]
                else:
                    value = near[1, part, :, i - 1] if i > 0 else ends[1, part]
                field.put(part, i, value)
        lanes = Lanes(field, None, masks)
        for i in range(1, DEEP):
            r = field.minus_a(i, near_media[side, DIAGONAL], layer3, lanes.now)
            for part in range(2):
                res[side, part, :, i - 1] = r[part]
    for s in range(count):
        k = plan[s] - place * slab
        for side, low in ((0, -edge), (1, slab)):
            i = k - low

            @pl.when((i >= 0) & (i < edge))
            def _():
                for part in range(2):
                    res[side, part, s, i] += sources[part, s]

    res_out()


def chain_kernel(at, start, send, given, made, rest):
    got, passages, full = given
    mine, theirs = made
    full = full.wait()
    place = lax.axis_index("depth")
    last_place = lax.axis_size("depth") - 1
    count = full.shape[2]
    even = lax.rem(place, 2) == 0
    low = place - lax.rem(place, 2)
    high = low + 1
    (a, b), (c, d) = halves(count)
    width = b - a
    zero = jnp.zeros((width,) + full.shape[3:], jnp.float32)
    passage = lambda j: (passages[j, at], passages[j, at + 1])
    emit = lambda way: tuple(
        jnp.where(even, full[way, part, a:b], full[way, part, c:d]) for part in range(2)
    )
    came = lambda j: (got[j, pl.ds(0, width)], got[j, pl.ds(width, width)])

    def step(j, state):
        return add(cmul(passage(j), state), came(j))

    below = jnp.maximum(low - 1, 0)
    above = jnp.minimum(high + 1, last_place)
    next_before = lax.fori_loop(0, below, step, (zero, zero))
    next_low = pick(low > 0, step(below, next_before), (zero, zero))
    next_high = add(cmul(passage(low), next_low), pick(even, emit(0), came(low)))
    prev_after = lax.fori_loop(
        0, last_place - above, lambda t, state: step(last_place - t, state), (zero, zero)
    )
    prev_high = pick(high < last_place, step(above, prev_after), (zero, zero))
    prev_low = add(cmul(passage(high), prev_high), pick(even, came(high), emit(1)))
    for_low = next_before, next_low, prev_low, prev_high
    for_high = next_low, next_high, prev_high, prev_after
    for i in range(4):
        own, other = pick(even, for_low[i], for_high[i]), pick(even, for_high[i], for_low[i])
        for part in range(2):
            mine[i, part] = own[part]
            theirs[i, part] = other[part]


def set_incoming(ref, mine, theirs, full, passage):
    even = lax.rem(lax.axis_index("depth"), 2) == 0
    count = full.shape[2]
    spots = ((0, 0), (1, 0), (1, 1), (2, 1))
    for half, (a, b) in enumerate(halves(count)):
        own = even if half == 0 else jnp.logical_not(even)
        waves = [
            tuple(jnp.where(own, mine[i, part], theirs[i, part]) for part in range(2))
            for i in range(4)
        ]
        here = lambda way: (full[way, 0, a:b], full[way, 1, a:b])
        onward = add(cmul(passage, waves[1]), here(0))
        back = add(cmul(passage, waves[2]), here(1))
        for (side, way), value in zip(
            spots + ((2, 0), (0, 1)), [*waves, onward, back]
        ):
            for part in range(2):
                ref[side, way, part, a:b] = coupling * value[part]


def update_passes(
    reach, slab, tile, incoming, residual_of, media, near_media, power, waves,
    refs, side_ref, ready, after_first, emit, pieces, done, masks,
):
    edge = DEEP - 1
    first_update = Field(refs[0], -reach, tile[0])
    second_update = Field(refs[1], 1 - reach, tile[0])
    first_update.clear()
    second_update.clear()
    own = lambda p: (tile_of(power, p + 1), tile_of(power, slab - p))
    low = lambda p: (tile_of(waves, 0, 0, p + edge), tile_of(waves, 0, 1, p + edge))
    high = lambda p: (tile_of(waves, 1, 0, p - slab), tile_of(waves, 1, 1, p - slab))
    sides = (
        (-reach, 0, near_media.at[0], low),
        (0, slab, media, own),
        (slab, slab + reach, near_media.at[1], high),
    )

    def begin(which, p):
        _, _, m, powers = sides[which]
        on, off = powers(p)
        onward = incoming[which, 0, 0], incoming[which, 0, 1]
        back = incoming[which, 1, 0], incoming[which, 1, 1]
        c = add(cmul(on, onward), cmul(off, back))
        first_update.put_both(p, cmul(pair(m, INVERSE), add(c, residual_of(which, p))))

    for which in (0, 2):
        for p in range(*sides[which][:2]):
            begin(which, p)
    for piece, (a, b) in enumerate(cuts(slab)):
        ready(piece)
        loop(a, b, lambda p, unused: begin(1, p) or unused, 0)
    after_first(first_update)

    def smooth(field, margin, body, own_pieces, own_done):
        lanes = Lanes(field, side_ref, masks)
        for p in range(UNROLL):
            lanes.fill(p)
        for which in (0, 2, 1):
            a, b, m, _ = sides[which]
            a, b = max(a, margin - reach), min(b, slab + reach - margin)
            if which != 1:
                for p in range(a, b):
                    body(which, m, p, lanes.now)
                continue
            for piece, (a, b) in enumerate(cuts(slab, own_pieces)):
                lanes.sweep(
                    a, b, slab, lambda p, c: body(1, media, p, lanes.kept) or c, 0
                )
                own_done(piece)

    def second(which, m, p, lanes):
        here, total = first_update.around(p, lanes)
        second_update.put_both(p, add(here, cmul(pair(m, SECOND), total)))

    def third(which, m, p, lanes):
        here, total = second_update.around(p, lanes)
        u = add(scale(keep * (1.0 + keep), here), cmul(pair(m, THIRD), total))
        emit(which, p, add(u, first_update.both(p)))

    smooth(first_update, 1, second, 1, lambda piece: None)
    smooth(second_update, 2, third, pieces, done)


def middle_kernel(start, send, given, made, rest):
    (
        mine, theirs, plan, full, sources, media, near_media, waves, near,
        near_residual, power, residual, guess,
    ) = given
    new_field, new_residual, (next_full, full_out), (slots, slots_out) = made
    held, loaded, next_held, incoming, side_ref, *refs = rest
    _, count, slab, height, breadth = guess.shape
    tile = (height, breadth)
    spans = [pl.ds(a, b - a) for a, b in cuts(slab)]
    res_copies = [start(residual.at[:, :, h], held.at[:, :, h]) for h in spans]
    field_copies = [start(guess.at[:, :, h], loaded.at[:, :, h]) for h in spans]
    masks = lane_masks(tile)
    place = lax.axis_index("depth")
    reach = DEEP - 1
    ext = reach - 2
    more = ext - 1
    new = Field(refs[2], -ext, height)
    new.clear()
    plan, full, sources = plan.wait(), full.wait(), sources.wait()
    media, near_media, waves = media.wait(), near_media.wait(), waves.wait()
    near, near_residual, power = near.wait(), near_residual.wait(), power.wait()
    set_incoming(incoming, mine, theirs, full, tile_of(power, slab))

    def residual_of(which, p):
        if which == 1:
            return held[0, :, p], held[1, :, p]
        i = p + reach if which == 0 else p - slab
        return near_residual[which // 2, 0, :, i], near_residual[which // 2, 1, :, i]

    def ready(piece):
        res_copies[piece].wait()

    def after_first(update):
        inverse = pair(media, INVERSE)
        for side, (p, i) in enumerate(((0, DEEP - 1), (slab - 1, 0))):
            lacks = cmul(inverse, (near[side, 0, :, i], near[side, 1, :, i]))
            update.put_both(p, add(update.both(p), lacks))
        for s in range(count):
            k = plan[s] - place * slab

            @pl.when((k >= 0) & (k < slab))
            def _():
                update.bump(k, s, cmul(inverse, (sources[0, s], sources[1, s])))

        for copy in field_copies:
            copy.wait()

    def emit(which, p, u):
        for part in range(2):
            if which == 1:
                value = loaded[part, :, p] + u[part]
                loaded[part, :, p] = value
            else:
                i = p + DEEP if which == 0 else p - slab
                value = near[which // 2, part, :, i] + u[part]
            new.put(part, p, value)

    def done(piece):
        send(loaded, new_field)

    update_passes(
        reach, slab, tile, incoming, residual_of, media, near_media, power, waves,
        refs, side_ref, ready, after_first, emit, 1, done, masks,
    )

    layer3 = media[LAYER]
    factor = pair(media, WAVE)
    lanes = Lanes(new, side_ref, masks)
    for p in range(UNROLL):
        lanes.fill(p)

    def put(p, r):
        for part in range(2):
            next_held[part, :, p + more] = r[part]

    for p in range(-more, 0):
        put(p, new.minus_a(p, near_media[0, DIAGONAL], layer3, lanes.now))
    for p in range(slab, slab + more):
        put(p, new.minus_a(p, near_media[1, DIAGONAL], layer3, lanes.now))
    diagonal = media[DIAGONAL]

    def inside(p, carry):
        toward_next, toward_prev = carry
        r = new.minus_a(p, diagonal, layer3, lanes.kept)
        put(p, r)
        toward_next = add(cmul(factor, toward_next), r)
        toward_prev = add(toward_prev, cmul(tile_of(power, p), r))
        return toward_next, toward_prev

    zero = jnp.zeros((count,) + tile, jnp.float32)
    carry = ((zero, zero), (zero, zero))
    for piece, (a, b) in enumerate(cuts(slab)):
        carry = lanes.sweep(a, b, slab, inside, carry)
        low = a + more if piece else 0
        high = b + more if piece < PIECES - 1 else slab + 2 * more
        part = pl.ds(low, high - low)
        send(next_held.at[:, :, part], new_residual.at[:, :, part])
    for way in range(2):
        for part in range(2):
            next_full[way, part] = carry[way][part]
    force_emits(plan, next_full, sources, power, slab)
    fill_send(slots, next_full, None)
    slots_out()
    full_out()


def final_kernel(start, send, given, made, rest):
    (
        mine, theirs, plan, full, sources, media, near_media, waves, power,
        residual, field,
    ) = given
    (out,) = made
    held, loaded, incoming, side_ref, *refs = rest
    _, count, slab, height, breadth = field.shape
    tile = (height, breadth)
    spans = [pl.ds(a, b - a) for a, b in cuts(slab)]
    reach = 2
    res_copies = []
    for piece, (a, b) in enumerate(cuts(slab)):
        low = a + reach if piece else 0
        high = b + reach if piece < PIECES - 1 else slab + 2 * reach
        part = pl.ds(low, high - low)
        res_copies.append(start(residual.at[:, :, part], held.at[:, :, part]))
    field_copies = [start(field.at[:, :, h], loaded.at[:, :, h]) for h in spans]
    masks = lane_masks(tile)
    place = lax.axis_index("depth")
    plan, full, sources = plan.wait(), full.wait(), sources.wait()
    media, near_media, waves = media.wait(), near_media.wait(), waves.wait()
    power = power.wait()
    set_incoming(incoming, mine, theirs, full, tile_of(power, slab))
    for copy in (res_copies[0], res_copies[-1]):
        copy.wait()

    def residual_of(which, p):
        return held[0, :, p + reach], held[1, :, p + reach]

    def ready(piece):
        if 0 < piece < PIECES - 1:
            res_copies[piece].wait()

    def after_first(update):
        for s in range(count):
            k = plan[s] - place * slab
            src = sources[0, s], sources[1, s]
            for m, a, b in (
                (media, 0, slab),
                (near_media.at[0], -reach, 0),
                (near_media.at[1], slab, slab + reach),
            ):

                @pl.when((k >= a) & (k < b))
                def _():
                    update.bump(k, s, cmul(pair(m, INVERSE), src))

        for copy in field_copies:
            copy.wait()

    def emit(which, p, u):
        for part in range(2):
            loaded[part, :, p] += u[part]

    def done(piece):
        send(loaded.at[:, :, spans[piece]], out.at[:, :, spans[piece]])

    update_passes(
        reach, slab, tile, incoming, residual_of, media, near_media, power, waves,
        refs, side_ref, ready, after_first, emit, PIECES, done, masks,
    )


def local(sources, plan, absorb, labels, region_kk, damp_cells, guess):
    size = lax.axis_size("depth")
    place = lax.axis_index("depth")
    _, count, slab, height, breadth = guess.shape
    tile = (height, breadth)
    edge = DEEP - 1
    planes = lambda n: (2, count, n) + tile
    scratch = lambda shape: pltpu.VMEM(shape, jnp.float32)

    even = place % 2 == 0
    top = slab - DEEP

    def payload(first):
        part = lax.dynamic_slice_in_dim(guess, first, DEEP, axis=2)
        return jnp.concatenate(
            [part.reshape((-1,) + tile), absorb, labels.astype(jnp.float32)], axis=0
        )

    even_pairs = [(i, i ^ 1) for i in range(size)]
    odd_pairs = [(i, i + 1) for i in range(1, size - 1, 2)]
    odd_pairs += [(b, a) for a, b in odd_pairs]
    got_odd = lax.ppermute(payload(jnp.where(even, 0, top)), "depth", odd_pairs)
    got_even = lax.ppermute(payload(jnp.where(even, top, 0)), "depth", even_pairs)

    residual, emits, media, power = kernel_call(
        start_kernel,
        [
            (plan, "smem"), (region_kk, "smem"), (damp_cells, "smem"),
            (sources, "vmem"), (absorb, "vmem"), (labels, "vmem"), (guess, "hbm"),
        ],
        [
            (planes(slab), "hbm"), ((2, 2, count) + tile, "vmem"),
            ((MEDIA,) + tile, "vmem"), ((slab + 1, 2) + tile, "vmem"),
        ],
        [
            scratch(planes(slab)), scratch(planes(slab)), scratch(planes(slab)),
            Field.shape(count, slab + 2, tile),
        ],
        pieces=2 * PIECES, cost=20_000_000, name="start",
    )
    width = count // 2
    full, slots, near, extra = kernel_call(
        arrange_kernel,
        [(got_even, "direct"), (got_odd, "direct"), (emits, "vmem"), (power, "hbm")],
        [
            ((2, 2, count) + tile, "vmem"), ((size, 2 * width + 2) + tile, "vmem"),
            ((2, 2, count, DEEP) + tile, "vmem"), ((2, 2) + tile, "vmem"),
        ],
        [scratch((2, 2) + tile)],
        pieces=1, cost=1_000_000, name="arrange", limit=16,
    )
    first_got = lax.all_to_all(slots, "depth", 0, 0)
    near_residual, near_media, waves = kernel_call(
        prepare_kernel,
        [
            (plan, "smem"), (region_kk, "smem"), (near, "vmem"), (extra, "vmem"),
            (sources, "vmem"), (media, "vmem"), (guess, "hbm"),
        ],
        [
            ((2, 2, count, edge) + tile, "vmem"), ((2, MEDIA) + tile, "vmem"),
            ((2, 2, edge, 2) + tile, "vmem"),
        ],
        [scratch((2, 2, count) + tile), Field.shape(count, DEEP + 1, tile)],
        pieces=2, cost=4_000_000, name="prepare",
    )

    def chain(got, full):
        mine, theirs = kernel_call(
            functools.partial(chain_kernel, 2 * width),
            [(got, "direct"), (first_got, "direct"), (full, "vmem")],
            [((4, 2, width) + tile, "direct")] * 2,
            cost=1_000_000, name="chain", limit=16,
        )
        return mine, lax.ppermute(theirs, "depth", even_pairs)

    mine, theirs = chain(first_got, full)
    new_field, new_residual, next_full, slots = kernel_call(
        middle_kernel,
        [
            (mine, "direct"), (theirs, "direct"),
            (plan, "smem"), (full, "vmem"), (sources, "vmem"),
            (media, "vmem"), (near_media, "vmem"), (waves, "vmem"), (near, "vmem"),
            (near_residual, "vmem"), (power, "vmem"), (residual, "hbm"), (guess, "hbm"),
        ],
        [
            (planes(slab), "hbm"), (planes(slab + 2 * (DEEP - 4)), "hbm"),
            ((2, 2, count) + tile, "vmem"), ((size, 2 * width) + tile, "vmem"),
        ],
        [
            scratch(planes(slab)), scratch(planes(slab)),
            scratch(planes(slab + 2 * (DEEP - 4))), scratch((3, 2, 2, count) + tile),
            scratch(planes(slab)),
            Field.shape(count, slab + 2 * edge, tile),
            Field.shape(count, slab + 2 * edge - 2, tile),
            Field.shape(count, slab + 2 * edge - 4, tile),
        ],
        pieces=3 * PIECES + 1, cost=80_000_000, name="middle",
    )
    mine, theirs = chain(lax.all_to_all(slots, "depth", 0, 0), next_full)
    (out,) = kernel_call(
        final_kernel,
        [
            (mine, "direct"), (theirs, "direct"),
            (plan, "smem"), (next_full, "vmem"), (sources, "vmem"),
            (media, "vmem"), (near_media, "vmem"), (waves, "vmem"), (power, "vmem"),
            (new_residual, "hbm"), (new_field, "hbm"),
        ],
        [(planes(slab), "hbm")],
        [
            scratch(planes(slab + 2 * (DEEP - 4))), scratch(planes(slab)),
            scratch((3, 2, 2, count) + tile), scratch(planes(slab)),
            Field.shape(count, slab + 4, tile), Field.shape(count, slab + 2, tile),
        ],
        pieces=3 * PIECES, cost=60_000_000, name="final",
    )
    return out


def solution(mesh):
    return jax.shard_map(
        local,
        mesh=mesh,
        in_specs=(
            P(None, "groups", None, None),
            P("groups"),
            P("depth", "groups", None),
            P("depth", "groups", None),
            P(),
            P("groups"),
            P(None, "groups", "depth", None, None),
        ),
        out_specs=P(None, "groups", "depth", None, None),
        check_vma=False,
    )
```

```python
import functools

import jax
import jax.numpy as jnp
from jax import lax
from jax.experimental import pallas as pl
from jax.experimental.pallas import tpu as pltpu
from jax.sharding import PartitionSpec as P

relax_weight = 0.8
shift_ratio = 0.5
damping = 3.0
coupling = 0.25
keep = 1.0 - relax_weight

DEEP = 6
UNROLL = 4
LAG = UNROLL + 1
PIECES = 4


def cmul(a, b):
    return a[0] * b[0] - a[1] * b[1], a[0] * b[1] + a[1] * b[0]


def add(a, b):
    return a[0] + b[0], a[1] + b[1]


def scale(c, a):
    return c * a[0], c * a[1]


def pick(cond, a, b):
    return jnp.where(cond, a[0], b[0]), jnp.where(cond, a[1], b[1])


def tile_of(ref, *at):
    return ref[at + (0,)], ref[at + (1,)]


class Inward:
    def __init__(self, source, target, sem):
        self.ref = target
        self.copy = pltpu.make_async_copy(source, target, sem)
        self.copy.start()

    def wait(self):
        self.copy.wait()
        return self.ref


def kernel_call(body, inputs, outputs, scratch=(), pieces=0, cost=0, name=None, limit=56):
    n_in, n_out = len(inputs), len(outputs)
    extra = []
    for array, place in inputs:
        if place in ("vmem", "smem"):
            space = pltpu.SMEM if place == "smem" else pltpu.VMEM
            extra.append(space(array.shape, array.dtype))
    for shape, place in outputs:
        if place == "vmem":
            extra.append(pltpu.VMEM(shape, jnp.float32))
    n_extra = len(extra)

    def kernel(*refs):
        ins, outs = refs[:n_in], refs[n_in : n_in + n_out]
        buffers = iter(refs[n_in + n_out : n_in + n_out + n_extra])
        sems = refs[n_in + n_out + n_extra]
        rest = refs[n_in + n_out + n_extra + 1 :]
        used = iter(range(n_extra + pieces))
        pending = []

        def start(source, target):
            return Inward(source, target, sems.at[next(used)])

        def send(source, target):
            pending.append(start(source, target))

        def arrive():
            given = []
            for ref, (_, place) in zip(ins, inputs):
                copied = place in ("vmem", "smem")
                given.append(start(ref, next(buffers)) if copied else ref)
            return given

        given = arrive()
        made = []
        for ref, (_, place) in zip(outs, outputs):
            if place != "vmem":
                made.append(ref)
            else:
                buffer = next(buffers)
                made.append((buffer, functools.partial(send, buffer, ref)))
        body(start, send, given, made, rest)
        for copy in pending:
            copy.wait()

    def spec(place):
        return pl.BlockSpec(memory_space=pltpu.VMEM if place == "direct" else pltpu.HBM)

    return pl.pallas_call(
        kernel,
        out_shape=tuple(jax.ShapeDtypeStruct(s, jnp.float32) for s, _ in outputs),
        in_specs=[spec(place) for _, place in inputs],
        out_specs=tuple(spec(place) for _, place in outputs),
        scratch_shapes=[
            *extra,
            pltpu.SemaphoreType.DMA((max(1, n_extra + pieces),)),
            *scratch,
        ],
        compiler_params=pltpu.CompilerParams(vmem_limit_bytes=limit << 20),
        cost_estimate=pl.CostEstimate(
            flops=cost, bytes_accessed=4 << 20, transcendentals=0
        ),
        name=name,
    )(*[array for array, _ in inputs])


def lane_sum(here, masks):
    breadth = here.shape[-1]
    axis = here.ndim - 1
    ahead = jnp.where(masks[0], pltpu.roll(here, 1, axis), 0.0)
    behind = jnp.where(masks[1], pltpu.roll(here, breadth - 1, axis), 0.0)
    return ahead + behind


class Field:
    def __init__(self, ref, first, height):
        self.ref, self.first, self.height = ref, first, height

    @staticmethod
    def shape(count, planes, tile):
        return pltpu.VMEM((2, count, (2 * planes + 1) * tile[0], tile[1]), jnp.float32)

    def rows(self, plane, shift=0):
        start = (2 * (plane - self.first) + 1) * self.height + shift
        if shift % self.height == 0:
            start = pl.multiple_of(start, self.height)
        return pl.ds(start, self.height)

    def clear(self):
        edge = self.ref[:, :, : self.height]
        self.ref[:, :, : self.height] = jnp.zeros_like(edge)

    def get(self, part, plane, shift=0):
        return self.ref[part, :, self.rows(plane, shift)]

    def both(self, plane):
        return self.get(0, plane), self.get(1, plane)

    def put(self, part, plane, value):
        self.ref[part, :, self.rows(plane)] = value
        self.ref[part, :, self.rows(plane, self.height)] = jnp.zeros_like(value)

    def put_both(self, plane, value):
        for part in range(2):
            self.put(part, plane, value[part])

    def bump(self, plane, s, value):
        for part in range(2):
            self.ref[part, s, self.rows(plane)] += value[part]

    def lanes(self, part, plane, masks):
        return lane_sum(self.get(part, plane), masks)

    def around(self, plane, lanes):
        heres, totals = [], []
        for part in range(2):
            here = self.get(part, plane)
            beside = self.get(part, plane, -1) + self.get(part, plane, 1)
            depth = self.get(part, plane - 1) + self.get(part, plane + 1)
            heres.append(here)
            totals.append((beside + depth) + lanes(part, plane))
        return tuple(heres), tuple(totals)

    def minus_a(self, plane, diagonal, layer3, lanes):
        here, total = self.around(plane, lanes)
        return (
            (total[0] - diagonal * here[0]) + layer3 * here[1],
            (total[1] - diagonal * here[1]) - layer3 * here[0],
        )


class Lanes:
    def __init__(self, field, masks):
        self.field, self.masks = field, masks

    def now(self, part, plane):
        return self.field.lanes(part, plane, self.masks)


def lane_masks(tile):
    lane = lax.broadcasted_iota(jnp.int32, tile, 1)
    return lane > 0, lane < tile[1] - 1


INVERSE, DIAGONAL, LAYER, WAVE, SECOND, THIRD, MEDIA = 0, 2, 3, 4, 6, 8, 10


def set_media(ref, squared, layer, absorb, slab, inside=None):
    diagonal = 6.0 - squared
    imag = shift_ratio * squared + damping * layer
    size = diagonal * diagonal + imag * imag
    inverse = relax_weight * diagonal / size, -relax_weight * imag / size
    if inside is not None:
        inverse = tuple(jnp.where(inside, v, 0.0) for v in inverse)
    grow = 1.0 + keep
    decay = jnp.exp(-absorb / slab)
    angle = jnp.sqrt(squared)
    factor = decay * jnp.cos(angle), decay * jnp.sin(angle)
    values = (
        *inverse, diagonal, damping * layer, *factor,
        *scale(1.0 / grow, inverse), *scale(grow, inverse),
    )
    for i, value in enumerate(values):
        ref[i] = value
    return factor


def pair(ref, i):
    return ref[i], ref[i + 1]


def region_values(labels, kk_ref):
    squared = jnp.zeros(labels.shape, jnp.float32)
    for region in range(kk_ref.shape[0]):
        squared = jnp.where(labels == region, kk_ref[region], squared)
    return squared


def loop(start, stop, body, carry, unroll=UNROLL):
    trips = (stop - start) // unroll

    def several(trip, carry):
        for i in range(unroll):
            carry = body(start + trip * unroll + i, carry)
        return carry

    if trips > 1:
        carry = lax.fori_loop(0, trips, several, carry)
        start += trips * unroll
    for plane in range(start, stop):
        carry = body(plane, carry)
    return carry


def cuts(planes, pieces=PIECES):
    edges = [planes * i // pieces for i in range(pieces + 1)]
    return list(zip(edges[:-1], edges[1:]))


def media_of(pack):
    return pack.at[pl.ds(0, MEDIA)]


def emit_tiles(count, way, part):
    return pl.ds(MEDIA + 4 + (2 * way + part) * count, count)


def start_kernel(start, send, given, made, rest):
    plan, kk, damp, sources, absorb, labels, guess = given
    residual, (pack, pack_out), (power, power_out) = made
    loaded, held, emits, ref = rest
    _, count, slab, height, breadth = guess.shape
    tile = (height, breadth)
    media = media_of(pack)
    copies = []
    edges = [0] + [min(b + UNROLL, slab) for _, b in cuts(slab)]
    for a, b in zip(edges[:-1], edges[1:]):
        part = pl.ds(a, b - a)
        copies.append(start(guess.at[:, :, part], loaded.at[:, :, part]))
    masks = lane_masks(tile)
    field = Field(ref, -1, height)
    zero = jnp.zeros((count,) + tile, jnp.float32)
    field.clear()
    field.put_both(-1, (zero, zero))
    field.put_both(slab, (zero, zero))
    lanes = Lanes(field, masks)

    def fill(p):
        for part in range(2):
            value = loaded[part, :, p]
            field.put(part, p, value)

    plan, kk, damp = plan.wait(), kk.wait(), damp.wait()
    row = lax.broadcasted_iota(jnp.int32, tile, 0)
    lane = lax.broadcasted_iota(jnp.int32, tile, 1)
    cell = row * breadth + lane

    def mark(i, hit):
        return jnp.where(cell == damp[i], 1.0, hit)

    layer = loop(0, damp.shape[0], mark, jnp.zeros(tile, jnp.float32), 16)
    sources, absorb, labels = sources.wait(), absorb.wait(), labels.wait()
    squared = region_values(labels[0], kk)
    factor = set_media(media, squared, layer, absorb[0], slab)
    diagonal, layer3 = media[DIAGONAL], media[LAYER]

    def plane(k, carry):
        toward_next, toward_prev, w = carry
        power[k, 0], power[k, 1] = w
        r = field.minus_a(k, diagonal, layer3, lanes.now)
        for part in range(2):
            held[part, :, k] = r[part]
        toward_next = add(cmul(factor, toward_next), r)
        toward_prev = add(toward_prev, cmul(w, r))
        return toward_next, toward_prev, cmul(factor, w)

    one = jnp.ones(tile, jnp.float32), jnp.zeros(tile, jnp.float32)
    carry = ((zero, zero), (zero, zero), one)
    for (a, b), copy in zip(cuts(slab), copies):
        copy.wait()
        if a == 0:
            fill(0)

        def group(trip, carry):
            base = a + trip * UNROLL
            for i in range(UNROLL):
                fill(base + i + 1)
            for i in range(UNROLL):
                carry = plane(base + i, carry)
            return carry

        trips = (min(b, slab - 1) - a) // UNROLL
        carry = lax.fori_loop(0, trips, group, carry)
        for k in range(a + trips * UNROLL, b):
            if k + 1 < slab:
                fill(k + 1)
            carry = plane(k, carry)
        add_forcing(plan, held, sources, 0, slab, a, b)
        part = pl.ds(a, b - a)
        send(held.at[:, :, part], residual.at[:, :, part])
    toward_next, toward_prev, w = carry
    power[slab, 0], power[slab, 1] = w
    power_out()
    for part in range(2):
        emits[0, part] = toward_next[part]
        emits[1, part] = toward_prev[part]
        pack[MEDIA + part] = power[slab - 1, part]
        pack[MEDIA + 2 + part] = power[slab, part]
    force_emits(plan, emits, sources, power, slab)
    for way in range(2):
        for part in range(2):
            pack[emit_tiles(count, way, part)] = emits[way, part]
    pack_out()


def add_forcing(plan, held, sources, reach, slab, low=None, high=None):
    first_plane = lax.axis_index("depth") * slab
    low = -reach if low is None else low
    high = slab + reach if high is None else high
    for s in range(sources.shape[1]):
        k = plan[s] - first_plane

        @pl.when((k >= low) & (k < high))
        def _():
            for part in range(2):
                held[part, s, k + reach] += sources[part, s]


def force_emits(plan, emits, sources, power, slab):
    first_plane = lax.axis_index("depth") * slab
    for s in range(sources.shape[1]):
        k = plan[s] - first_plane

        @pl.when((k >= 0) & (k < slab))
        def _():
            src = sources[0, s], sources[1, s]
            onward = cmul(tile_of(power, slab - 1 - k), src)
            back = cmul(tile_of(power, k), src)
            for part in range(2):
                emits[0, part, s] += onward[part]
                emits[1, part, s] += back[part]


def halves(count):
    return (0, count // 2), (count // 2, count)


def fill_send(slots, full, passage):
    place = lax.axis_index("depth")

    def one(chip, unused):
        for core, (a, b) in enumerate(halves(full.shape[2])):
            j = 2 * chip + core
            way = jnp.where(j > place, 0, 1)
            for part in range(2):
                slots[j, pl.ds(part * (b - a), b - a)] = full[way, part, a:b]
            if passage is not None:
                slots[j, 2 * (b - a)] = passage[0]
                slots[j, 2 * (b - a) + 1] = passage[1]
        return unused

    loop(0, slots.shape[0] // 2, one, 0, 4)


def arrange_kernel(start, send, given, made, rest):
    got_even, got_odd, pack = given
    full, slots, near, extra = made
    even = lax.rem(lax.axis_index("depth"), 2) == 0
    count = full.shape[2]
    weight, passage = pair(pack, MEDIA), pair(pack, MEDIA + 2)
    emits = [[pack[emit_tiles(count, way, part)] for part in range(2)] for way in range(2)]
    for s in range(count):
        at = [(part * count + s) * DEEP for part in range(2)]
        low = tuple(
            jnp.where(even, got_odd[i + DEEP - 1], got_even[i + DEEP - 1]) for i in at
        )
        high = tuple(jnp.where(even, got_even[i], got_odd[i]) for i in at)
        toward_next = add(add(cmul(weight, low), high), (emits[0][0][s], emits[0][1][s]))
        toward_prev = add(add(cmul(weight, high), low), (emits[1][0][s], emits[1][1][s]))
        for part in range(2):
            full[0, part, s] = toward_next[part]
            full[1, part, s] = toward_prev[part]
    fill_send(slots, full, passage)
    for side in range(2):
        first, second = (got_odd, got_even) if side == 0 else (got_even, got_odd)
        for i in range(2 * count):
            rows = pl.ds(i * DEEP, DEEP)
            near[side, i // count, i % count] = jnp.where(
                even, first[rows], second[rows]
            )
        for i in range(2):
            at = 2 * count * DEEP + i
            extra[side, i] = jnp.where(even, first[at], second[at])


def prepare_kernel(start, send, given, made, rest):
    plan, kk, near, extra, sources, pack, guess = given
    res, near_media, waves = made
    (ref,) = rest
    _, count, slab, height, breadth = guess.shape
    tile = (height, breadth)
    plan, kk = plan.wait(), kk.wait()
    masks = lane_masks(tile)
    place = lax.axis_index("depth")
    last_place = lax.axis_size("depth") - 1
    layer3 = media_of(pack)[LAYER]
    layer = layer3 / damping
    factors = []
    for side in range(2):
        squared = region_values(extra[side, 1].astype(jnp.int32), kk)
        inside = (place > 0) if side == 0 else (place < last_place)
        factors.append(
            set_media(near_media.at[side], squared, layer, extra[side, 0], slab, inside)
        )

    ws = list(factors)
    edge = DEEP - 1

    def keep_power(k, ws):
        for side in range(2):
            for way in range(2):
                if side == way:
                    i = k - (slab - edge + 1)
                    i = edge - 1 - i if side else i
                else:
                    i = k - 1
                    i = i if side else edge - 1 - i
                if 0 <= i < edge:
                    for part in range(2):
                        waves[side, way, i, part] = ws[side][part]

    def next_power(k, ws):
        return tuple(cmul(factors[side], ws[side]) for side in range(2))

    k = 1
    while k <= slab:
        if edge < k < slab - edge + 1:
            ws = loop(k, slab - edge + 1, next_power, tuple(ws), 8)
            k = slab - edge + 1
        keep_power(k, ws)
        ws = next_power(k, ws)
        k += 1
    for side in range(2):
        field = Field(ref, 0, height)
        field.clear()
        for i in range(DEEP + 1):
            for part in range(2):
                if side == 0:
                    value = near[0, part, :, i] if i < DEEP else guess[part, :, 0]
                else:
                    value = near[1, part, :, i - 1] if i > 0 else guess[part, :, slab - 1]
                field.put(part, i, value)
        lanes = Lanes(field, masks)
        for i in range(1, DEEP):
            r = field.minus_a(i, near_media[side, DIAGONAL], layer3, lanes.now)
            for part in range(2):
                res[side, part, :, i - 1] = r[part]
    for s in range(count):
        k = plan[s] - place * slab
        for side, low in ((0, -edge), (1, slab)):
            i = k - low

            @pl.when((i >= 0) & (i < edge))
            def _():
                for part in range(2):
                    res[side, part, s, i] += sources[part, s]


def chain_kernel(at, start, send, given, made, rest):
    got, passages, full = given
    mine, theirs = made
    place = lax.axis_index("depth")
    last_place = lax.axis_size("depth") - 1
    count = full.shape[2]
    even = lax.rem(place, 2) == 0
    low = place - lax.rem(place, 2)
    high = low + 1
    (a, b), (c, d) = halves(count)
    width = b - a
    zero = jnp.zeros((width,) + full.shape[3:], jnp.float32)
    passage = lambda j: (passages[j, at], passages[j, at + 1])
    emit = lambda way: tuple(
        jnp.where(even, full[way, part, a:b], full[way, part, c:d]) for part in range(2)
    )
    came = lambda j: (got[j, pl.ds(0, width)], got[j, pl.ds(width, width)])

    def step(j, state):
        return add(cmul(passage(j), state), came(j))

    below = jnp.maximum(low - 1, 0)
    above = jnp.minimum(high + 1, last_place)
    next_before = lax.fori_loop(0, below, step, (zero, zero))
    next_low = pick(low > 0, step(below, next_before), (zero, zero))
    next_high = add(cmul(passage(low), next_low), pick(even, emit(0), came(low)))
    prev_after = lax.fori_loop(
        0, last_place - above, lambda t, state: step(last_place - t, state), (zero, zero)
    )
    prev_high = pick(high < last_place, step(above, prev_after), (zero, zero))
    prev_low = add(cmul(passage(high), prev_high), pick(even, came(high), emit(1)))
    for_low = next_before, next_low, prev_low, prev_high
    for_high = next_low, next_high, prev_high, prev_after
    for i in range(4):
        own, other = pick(even, for_low[i], for_high[i]), pick(even, for_high[i], for_low[i])
        for part in range(2):
            mine[i, part] = own[part]
            theirs[i, part] = other[part]


def set_incoming(ref, mine, theirs, full, passage):
    even = lax.rem(lax.axis_index("depth"), 2) == 0
    count = full.shape[2]
    spots = ((0, 0), (1, 0), (1, 1), (2, 1))
    for half, (a, b) in enumerate(halves(count)):
        own = even if half == 0 else jnp.logical_not(even)
        waves = [
            tuple(jnp.where(own, mine[i, part], theirs[i, part]) for part in range(2))
            for i in range(4)
        ]
        here = lambda way: (full[way, 0, a:b], full[way, 1, a:b])
        onward = add(cmul(passage, waves[1]), here(0))
        back = add(cmul(passage, waves[2]), here(1))
        for (side, way), value in zip(
            spots + ((2, 0), (0, 1)), [*waves, onward, back]
        ):
            for part in range(2):
                ref[side, way, part, a:b] = coupling * value[part]


class Stage:
    def __init__(self, below, own, above):
        self.below, self.own, self.above = below, own, above


def pipeline(stages, slab, carry, halfway):
    offsets = [LAG * (len(stages) - 1 - i) for i in range(len(stages))]
    trips = (slab - offsets[0]) // UNROLL

    def run(i, p, carry):
        out = stages[i].own(p, carry)
        return carry if out is None else out

    def own(i, start, stop, carry):
        body = lambda p, c: run(i, p, c)
        if start == 0 and stop > 0:
            carry = body(0, carry)
            start = 1
        if stop == slab and start < slab:
            return body(slab - 1, loop(start, slab - 1, body, carry))
        return loop(start, stop, body, carry)

    stages[0].below()
    stages[0].above()
    for i, stage in enumerate(stages):
        if i:
            stage.below()
        carry = own(i, 0, offsets[i], carry)

    def trip(t, carry):
        for i in reversed(range(len(stages))):
            for u in range(UNROLL):
                carry = run(i, t * UNROLL + offsets[i] + u, carry)
        return carry

    first = trips // 2
    carry = lax.fori_loop(0, first, trip, carry)
    halfway(0, [first * UNROLL + o for o in offsets])
    carry = lax.fori_loop(first, trips, trip, carry)
    halfway(1, [trips * UNROLL + o for o in offsets])
    for i, stage in enumerate(stages):
        carry = own(i, trips * UNROLL + offsets[i], slab, carry)
        if i:
            stage.above()
    return carry


def update_stages(
    reach, slab, tile, incoming, residual_of, media, near_media, power, waves,
    refs, emit, masks,
):
    edge = DEEP - 1
    first_update = Field(refs[0], -reach, tile[0])
    second_update = Field(refs[1], 1 - reach, tile[0])
    first_update.clear()
    second_update.clear()
    powers = (
        lambda p: (tile_of(waves, 0, 0, p + edge), tile_of(waves, 0, 1, p + edge)),
        lambda p: (tile_of(power, p + 1), tile_of(power, slab - p)),
        lambda p: (tile_of(waves, 1, 0, p - slab), tile_of(waves, 1, 1, p - slab)),
    )
    coefficients = near_media.at[0], media, near_media.at[1]
    first_lanes = Lanes(first_update, masks)
    second_lanes = Lanes(second_update, masks)

    def begin(which, p):
        on, off = powers[which](p)
        onward = incoming[which, 0, 0], incoming[which, 0, 1]
        back = incoming[which, 1, 0], incoming[which, 1, 1]
        c = add(cmul(on, onward), cmul(off, back))
        inverse = pair(coefficients[which], INVERSE)
        first_update.put_both(p, cmul(inverse, add(c, residual_of(which, p))))

    def second(which, p):
        here, total = first_update.around(p, first_lanes.now)
        smoothed = cmul(pair(coefficients[which], SECOND), total)
        second_update.put_both(p, add(here, smoothed))

    def third(which, p):
        here, total = second_update.around(p, second_lanes.now)
        smoothed = cmul(pair(coefficients[which], THIRD), total)
        u = add(scale(keep * (1.0 + keep), here), smoothed)
        emit(which, p, add(u, first_update.both(p)))

    def stage(body, margin):
        def beyond(which, a, b):
            for p in range(a, b):
                body(which, p)

        return Stage(
            lambda: beyond(0, margin - reach, 0),
            lambda p, unused: body(1, p),
            lambda: beyond(2, slab, slab + reach - margin),
        )

    return [stage(begin, 0), stage(second, 1), stage(third, 2)]


def middle_kernel(start, send, given, made, rest):
    (
        mine, theirs, plan, full, sources, pack, near_media, waves, near,
        near_residual, power, residual, guess,
    ) = given
    media = media_of(pack)
    new_field, new_residual, next_full, slots = made
    incoming, *refs = rest
    _, count, slab, height, breadth = guess.shape
    tile = (height, breadth)
    masks = lane_masks(tile)
    reach = DEEP - 1
    ext = reach - 2
    more = ext - 1
    new = Field(refs[2], -ext, height)
    new.clear()
    plan = plan.wait()
    set_incoming(incoming, mine, theirs, full, tile_of(power, slab))

    def residual_of(which, p):
        if which == 1:
            r = residual[0, :, p], residual[1, :, p]
            if isinstance(p, int) and p == 0:
                r = add(r, (near[0, 0, :, DEEP - 1], near[0, 1, :, DEEP - 1]))
            if isinstance(p, int) and p == slab - 1:
                r = add(r, (near[1, 0, :, 0], near[1, 1, :, 0]))
            return r
        i = p + reach if which == 0 else p - slab
        return near_residual[which // 2, 0, :, i], near_residual[which // 2, 1, :, i]

    def emit(which, p, u):
        for part in range(2):
            if which == 1:
                value = guess[part, :, p] + u[part]
                new_field[part, :, p] = value
            else:
                i = p + DEEP if which == 0 else p - slab
                value = near[which // 2, part, :, i] + u[part]
            new.put(part, p, value)

    stages = update_stages(
        reach, slab, tile, incoming, residual_of, media, near_media, power, waves,
        refs, emit, masks,
    )

    layer3 = media[LAYER]
    factor = pair(media, WAVE)
    lanes = Lanes(new, masks)

    def residual_at(p, diagonal):
        r = new.minus_a(p, diagonal, layer3, lanes.now)
        for part in range(2):
            new_residual[part, :, p + more] = r[part]
        return r

    def beyond(side, a, b):
        for p in range(a, b):
            residual_at(p, near_media[side, DIAGONAL])

    def inside(p, carry):
        toward_next, toward_prev = carry
        r = residual_at(p, media[DIAGONAL])
        toward_next = add(cmul(factor, toward_next), r)
        toward_prev = add(toward_prev, cmul(tile_of(power, p), r))
        return toward_next, toward_prev

    stages.append(
        Stage(lambda: beyond(0, -more, 0), inside, lambda: beyond(1, slab, slab + more))
    )
    zero = jnp.zeros((count,) + tile, jnp.float32)
    carry = pipeline(stages, slab, ((zero, zero), (zero, zero)), lambda i, reached: None)
    for way in range(2):
        for part in range(2):
            next_full[way, part] = carry[way][part]
    force_emits(plan, next_full, sources, power, slab)
    fill_send(slots, next_full, None)
    add_forcing(plan, new_residual, sources, more, slab)


def final_kernel(start, send, given, made, rest):
    (
        mine, theirs, full, pack, near_media, waves, power, residual, field,
    ) = given
    (out,) = made
    media = media_of(pack)
    held, incoming, *refs = rest
    _, count, slab, height, breadth = field.shape
    tile = (height, breadth)
    reach = 2
    masks = lane_masks(tile)
    set_incoming(incoming, mine, theirs, full, tile_of(power, slab))

    def residual_of(which, p):
        return residual[0, :, p + reach], residual[1, :, p + reach]

    def emit(which, p, u):
        for part in range(2):
            held[part, :, p] = field[part, :, p] + u[part]

    stages = update_stages(
        reach, slab, tile, incoming, residual_of, media, near_media, power, waves,
        refs, emit, masks,
    )
    sent = [0]

    def send_field(top):
        part = pl.ds(sent[0], top - sent[0])
        send(held.at[:, :, part], out.at[:, :, part])
        sent[0] = top

    pipeline(stages, slab, 0, lambda i, reached: send_field(reached[2]))
    send_field(slab)


def local(sources, plan, absorb, labels, region_kk, damp_cells, guess):
    size = lax.axis_size("depth")
    place = lax.axis_index("depth")
    _, count, slab, height, breadth = guess.shape
    tile = (height, breadth)
    edge = DEEP - 1
    planes = lambda n: (2, count, n) + tile
    scratch = lambda shape: pltpu.VMEM(shape, jnp.float32)

    even = place % 2 == 0
    top = slab - DEEP

    def payload(first):
        part = lax.dynamic_slice_in_dim(guess, first, DEEP, axis=2)
        return jnp.concatenate(
            [part.reshape((-1,) + tile), absorb, labels.astype(jnp.float32)], axis=0
        )

    even_pairs = [(i, i ^ 1) for i in range(size)]
    odd_pairs = [(i, i + 1) for i in range(1, size - 1, 2)]
    odd_pairs += [(b, a) for a, b in odd_pairs]
    got_odd = lax.ppermute(payload(jnp.where(even, 0, top)), "depth", odd_pairs)
    got_even = lax.ppermute(payload(jnp.where(even, top, 0)), "depth", even_pairs)

    residual, pack, power = kernel_call(
        start_kernel,
        [
            (plan, "smem"), (region_kk, "smem"), (damp_cells, "smem"),
            (sources, "vmem"), (absorb, "vmem"), (labels, "vmem"), (guess, "hbm"),
        ],
        [
            (planes(slab), "hbm"), ((MEDIA + 4 + 4 * count,) + tile, "vmem"),
            ((slab + 1, 2) + tile, "vmem"),
        ],
        [
            scratch(planes(slab)), scratch(planes(slab)), scratch((2, 2, count) + tile),
            Field.shape(count, slab + 2, tile),
        ],
        pieces=2 * PIECES, cost=20_000_000, name="start", limit=62,
    )
    width = count // 2
    full, slots, near, extra = kernel_call(
        arrange_kernel,
        [(got_even, "direct"), (got_odd, "direct"), (pack, "direct")],
        [
            ((2, 2, count) + tile, "direct"), ((size, 2 * width + 2) + tile, "direct"),
            ((2, 2, count, DEEP) + tile, "direct"), ((2, 2) + tile, "direct"),
        ],
        cost=1_000_000, name="arrange", limit=4,
    )
    first_got = lax.all_to_all(slots, "depth", 0, 0)
    near_residual, near_media, waves = kernel_call(
        prepare_kernel,
        [
            (plan, "smem"), (region_kk, "smem"), (near, "direct"), (extra, "direct"),
            (sources, "direct"), (pack, "direct"), (guess, "direct"),
        ],
        [
            ((2, 2, count, edge) + tile, "direct"), ((2, MEDIA) + tile, "direct"),
            ((2, 2, edge, 2) + tile, "direct"),
        ],
        [Field.shape(count, DEEP + 1, tile)],
        cost=4_000_000, name="prepare", limit=4,
    )

    def chain(got, full):
        mine, theirs = kernel_call(
            functools.partial(chain_kernel, 2 * width),
            [(got, "direct"), (first_got, "direct"), (full, "direct")],
            [((4, 2, width) + tile, "direct")] * 2,
            cost=1_000_000, name="chain", limit=4,
        )
        return mine, lax.ppermute(theirs, "depth", even_pairs)

    mine, theirs = chain(first_got, full)
    new_field, new_residual, next_full, slots = kernel_call(
        middle_kernel,
        [
            (mine, "direct"), (theirs, "direct"),
            (plan, "smem"), (full, "direct"), (sources, "direct"),
            (pack, "direct"), (near_media, "direct"), (waves, "direct"),
            (near, "direct"), (near_residual, "direct"), (power, "direct"),
            (residual, "direct"), (guess, "direct"),
        ],
        [
            (planes(slab), "direct"), (planes(slab + 2 * (DEEP - 4)), "direct"),
            ((2, 2, count) + tile, "direct"), ((size, 2 * width) + tile, "direct"),
        ],
        [
            scratch((3, 2, 2, count) + tile),
            Field.shape(count, slab + 2 * edge, tile),
            Field.shape(count, slab + 2 * edge - 2, tile),
            Field.shape(count, slab + 2 * edge - 4, tile),
        ],
        cost=80_000_000, name="middle", limit=20,
    )
    mine, theirs = chain(lax.all_to_all(slots, "depth", 0, 0), next_full)
    (out,) = kernel_call(
        final_kernel,
        [
            (mine, "direct"), (theirs, "direct"), (next_full, "direct"),
            (pack, "direct"), (near_media, "direct"), (waves, "direct"),
            (power, "direct"), (new_residual, "direct"), (new_field, "direct"),
        ],
        [(planes(slab), "hbm")],
        [
            scratch(planes(slab)), scratch((3, 2, 2, count) + tile),
            Field.shape(count, slab + 4, tile), Field.shape(count, slab + 2, tile),
        ],
        pieces=3, cost=60_000_000, name="final", limit=16,
    )
    return out


def solution(mesh):
    return jax.shard_map(
        local,
        mesh=mesh,
        in_specs=(
            P(None, "groups", None, None),
            P("groups"),
            P("depth", "groups", None),
            P("depth", "groups", None),
            P(),
            P("groups"),
            P(None, "groups", "depth", None, None),
        ),
        out_specs=P(None, "groups", "depth", None, None),
        check_vma=False,
    )
```

```python
import functools

import jax
import jax.numpy as jnp
from jax import lax
from jax.experimental import pallas as pl
from jax.experimental.pallas import tpu as pltpu
from jax.sharding import PartitionSpec as P

relax_weight = 0.8
shift_ratio = 0.5
damping = 3.0
coupling = 0.25
keep = 1.0 - relax_weight

DEEP = 6
UNROLL = 4
LAG = UNROLL + 1
PIECES = 4
PACK = 4


def cmul(a, b):
    return a[0] * b[0] - a[1] * b[1], a[0] * b[1] + a[1] * b[0]


def add(a, b):
    return a[0] + b[0], a[1] + b[1]


def scale(c, a):
    return c * a[0], c * a[1]


def pick(cond, a, b):
    return jnp.where(cond, a[0], b[0]), jnp.where(cond, a[1], b[1])


def tile_of(ref, *at):
    return ref[at + (0,)], ref[at + (1,)]


class Inward:
    def __init__(self, source, target, sem):
        self.ref = target
        self.copy = pltpu.make_async_copy(source, target, sem)
        self.copy.start()

    def wait(self):
        self.copy.wait()
        return self.ref


def kernel_call(body, inputs, outputs, scratch=(), pieces=0, cost=0, name=None, limit=56):
    n_in, n_out = len(inputs), len(outputs)
    pinned = ("hbm", "vmem", "smem")
    extra = []
    for array, place in inputs:
        if place in ("vmem", "smem"):
            space = pltpu.SMEM if place == "smem" else pltpu.VMEM
            extra.append(space(array.shape, array.dtype))
    for shape, place in outputs:
        if place == "vmem":
            extra.append(pltpu.VMEM(shape, jnp.float32))
    n_extra = len(extra)

    def kernel(*refs):
        ins, outs = refs[:n_in], refs[n_in : n_in + n_out]
        buffers = iter(refs[n_in + n_out : n_in + n_out + n_extra])
        sems = refs[n_in + n_out + n_extra]
        rest = refs[n_in + n_out + n_extra + 1 :]
        used = iter(range(n_extra + pieces))
        pending = []

        def start(source, target):
            return Inward(source, target, sems.at[next(used)])

        def send(source, target):
            pending.append(start(source, target))

        def arrive():
            given = []
            for ref, (_, place) in zip(ins, inputs):
                copied = place in ("vmem", "smem")
                given.append(start(ref, next(buffers)) if copied else ref)
            return given

        given = arrive()
        made = []
        for ref, (_, place) in zip(outs, outputs):
            if place != "vmem":
                made.append(ref)
            else:
                buffer = next(buffers)
                made.append((buffer, functools.partial(send, buffer, ref)))
        body(start, send, given, made, rest)
        for copy in pending:
            copy.wait()

    def spec(place):
        return pl.BlockSpec(memory_space=pltpu.VMEM if place == "direct" else pltpu.HBM)

    return pl.pallas_call(
        kernel,
        out_shape=tuple(jax.ShapeDtypeStruct(s, jnp.float32) for s, _ in outputs),
        in_specs=[spec(place) for _, place in inputs],
        out_specs=tuple(spec(place) for _, place in outputs),
        scratch_shapes=[
            *extra,
            pltpu.SemaphoreType.DMA((max(1, n_extra + pieces),)),
            *scratch,
        ],
        compiler_params=pltpu.CompilerParams(vmem_limit_bytes=limit << 20),
        cost_estimate=pl.CostEstimate(
            flops=cost, bytes_accessed=4 << 20, transcendentals=0
        ),
        name=name,
    )(*[
        pltpu.with_memory_space_constraint(array, pltpu.HBM) if place in pinned else array
        for array, place in inputs
    ])


def lane_sum(here, masks):
    breadth = here.shape[-1]
    axis = here.ndim - 1
    ahead = jnp.where(masks[0], pltpu.roll(here, 1, axis), 0.0)
    behind = jnp.where(masks[1], pltpu.roll(here, breadth - 1, axis), 0.0)
    return ahead + behind


class Field:
    def __init__(self, ref, first, height):
        self.ref, self.first, self.height = ref, first, height

    @staticmethod
    def shape(count, planes, tile):
        return pltpu.VMEM((2, count, (2 * planes + 1) * tile[0], tile[1]), jnp.float32)

    def rows(self, plane, shift=0):
        start = (2 * (plane - self.first) + 1) * self.height + shift
        if shift % self.height == 0:
            start = pl.multiple_of(start, self.height)
        return pl.ds(start, self.height)

    def clear(self):
        edge = self.ref[:, :, : self.height]
        self.ref[:, :, : self.height] = jnp.zeros_like(edge)

    def get(self, part, plane, shift=0):
        return self.ref[part, :, self.rows(plane, shift)]

    def both(self, plane):
        return self.get(0, plane), self.get(1, plane)

    def put(self, part, plane, value):
        self.ref[part, :, self.rows(plane)] = value
        self.ref[part, :, self.rows(plane, self.height)] = jnp.zeros_like(value)

    def put_both(self, plane, value):
        for part in range(2):
            self.put(part, plane, value[part])

    def bump(self, plane, s, value):
        for part in range(2):
            self.ref[part, s, self.rows(plane)] += value[part]

    def lanes(self, part, plane, masks):
        return lane_sum(self.get(part, plane), masks)

    def around(self, plane, lanes):
        heres, totals = [], []
        for part in range(2):
            here = self.get(part, plane)
            beside = self.get(part, plane, -1) + self.get(part, plane, 1)
            depth = self.get(part, plane - 1) + self.get(part, plane + 1)
            heres.append(here)
            totals.append((beside + depth) + lanes(part, plane))
        return tuple(heres), tuple(totals)

    def minus_a(self, plane, diagonal, layer3, lanes):
        here, total = self.around(plane, lanes)
        return (
            (total[0] - diagonal * here[0]) + layer3 * here[1],
            (total[1] - diagonal * here[1]) - layer3 * here[0],
        )


class Lanes:
    def __init__(self, field, masks):
        self.field, self.masks = field, masks

    def now(self, part, plane):
        return self.field.lanes(part, plane, self.masks)


def lane_masks(tile):
    lane = lax.broadcasted_iota(jnp.int32, tile, 1)
    return lane > 0, lane < tile[1] - 1


INVERSE, DIAGONAL, LAYER, WAVE, SECOND, THIRD, MEDIA = 0, 2, 3, 4, 6, 8, 10


def set_media(ref, squared, layer, absorb, slab, inside=None):
    diagonal = 6.0 - squared
    imag = shift_ratio * squared + damping * layer
    size = diagonal * diagonal + imag * imag
    inverse = relax_weight * diagonal / size, -relax_weight * imag / size
    if inside is not None:
        inverse = tuple(jnp.where(inside, v, 0.0) for v in inverse)
    grow = 1.0 + keep
    decay = jnp.exp(-absorb / slab)
    angle = jnp.sqrt(squared)
    factor = decay * jnp.cos(angle), decay * jnp.sin(angle)
    values = (
        *inverse, diagonal, damping * layer, *factor,
        *scale(1.0 / grow, inverse), *scale(grow, inverse),
    )
    for i, value in enumerate(values):
        ref[i] = value
    return factor


def pair(ref, i):
    return ref[i], ref[i + 1]


def region_values(labels, kk_ref):
    squared = jnp.zeros(labels.shape, jnp.float32)
    for region in range(kk_ref.shape[0]):
        squared = jnp.where(labels == region, kk_ref[region], squared)
    return squared


def loop(start, stop, body, carry, unroll=UNROLL):
    trips = (stop - start) // unroll

    def several(trip, carry):
        for i in range(unroll):
            carry = body(start + trip * unroll + i, carry)
        return carry

    if trips > 1:
        carry = lax.fori_loop(0, trips, several, carry)
        start += trips * unroll
    for plane in range(start, stop):
        carry = body(plane, carry)
    return carry


def cuts(planes, pieces=PIECES):
    edges = [planes * i // pieces for i in range(pieces + 1)]
    return list(zip(edges[:-1], edges[1:]))


def media_of(pack):
    return pack.at[pl.ds(0, MEDIA)]


def emit_tiles(count, way, part):
    return pl.ds(MEDIA + 4 + (2 * way + part) * count, count)


def pack_kernel(start, send, given, made, rest):
    kk, absorb, labels, guess = given
    _, count, slab, *_ = guess.shape
    even = lax.rem(lax.axis_index("depth"), 2) == 0
    top = slab - DEEP
    for out, first in zip(made, (jnp.where(even, top, 0), jnp.where(even, 0, top))):
        for i in range(2 * count):
            send(
                guess.at[i // count, i % count, pl.ds(first, DEEP)],
                out.at[pl.ds(i * DEEP, DEEP)],
            )
    kk, absorb, labels = kk.wait(), absorb.wait(), labels.wait()
    squared = region_values(labels[0], kk)
    for out in made:
        out[2 * count * DEEP] = absorb[0]
        out[2 * count * DEEP + 1] = squared


def start_kernel(start, send, given, made, rest):
    plan, kk, damp, sources, absorb, labels, guess = given
    residual, pack, power = made
    loaded, emits, ref = rest
    _, count, slab, height, breadth = guess.shape
    tile = (height, breadth)
    media = media_of(pack)
    copies = []
    edges = [0] + [min(b + UNROLL, slab) for _, b in cuts(slab)]
    for a, b in zip(edges[:-1], edges[1:]):
        part = pl.ds(a, b - a)
        copies.append(start(guess.at[:, :, part], loaded.at[:, :, part]))
    masks = lane_masks(tile)
    field = Field(ref, -1, height)
    zero = jnp.zeros((count,) + tile, jnp.float32)
    field.clear()
    field.put_both(-1, (zero, zero))
    field.put_both(slab, (zero, zero))
    lanes = Lanes(field, masks)

    def fill(p):
        for part in range(2):
            value = loaded[part, :, p]
            field.put(part, p, value)

    plan, kk, damp = plan.wait(), kk.wait(), damp.wait()
    row = lax.broadcasted_iota(jnp.int32, tile, 0)
    lane = lax.broadcasted_iota(jnp.int32, tile, 1)
    cell = row * breadth + lane

    def mark(i, hit):
        return jnp.where(cell == damp[i], 1.0, hit)

    layer = loop(0, damp.shape[0], mark, jnp.zeros(tile, jnp.float32), 16)
    sources, absorb, labels = sources.wait(), absorb.wait(), labels.wait()
    squared = region_values(labels[0], kk)
    factor = set_media(media, squared, layer, absorb[0], slab)
    diagonal, layer3 = media[DIAGONAL], media[LAYER]

    def plane(k, carry):
        toward_next, toward_prev, w = carry
        power[k, 0], power[k, 1] = w
        r = field.minus_a(k, diagonal, layer3, lanes.now)
        for part in range(2):
            residual[part, :, k] = r[part]
        toward_next = add(cmul(factor, toward_next), r)
        toward_prev = add(toward_prev, cmul(w, r))
        return toward_next, toward_prev, cmul(factor, w)

    one = jnp.ones(tile, jnp.float32), jnp.zeros(tile, jnp.float32)
    carry = ((zero, zero), (zero, zero), one)
    for (a, b), copy in zip(cuts(slab), copies):
        copy.wait()
        if a == 0:
            fill(0)

        def group(trip, carry):
            base = a + trip * UNROLL
            for i in range(UNROLL):
                fill(base + i + 1)
            for i in range(UNROLL):
                carry = plane(base + i, carry)
            return carry

        trips = (min(b, slab - 1) - a) // UNROLL
        carry = lax.fori_loop(0, trips, group, carry)
        for k in range(a + trips * UNROLL, b):
            if k + 1 < slab:
                fill(k + 1)
            carry = plane(k, carry)
    toward_next, toward_prev, w = carry
    power[slab, 0], power[slab, 1] = w
    add_forcing(plan, residual, sources, 0, slab)
    for part in range(2):
        emits[0, part] = toward_next[part]
        emits[1, part] = toward_prev[part]
        pack[MEDIA + part] = power[slab - 1, part]
        pack[MEDIA + 2 + part] = power[slab, part]
    force_emits(plan, emits, sources, power, slab)
    for way in range(2):
        for part in range(2):
            pack[emit_tiles(count, way, part)] = emits[way, part]


def add_forcing(plan, held, sources, reach, slab):
    first_plane = lax.axis_index("depth") * slab
    for s in range(sources.shape[1]):
        k = plan[s] - first_plane

        @pl.when((k >= -reach) & (k < slab + reach))
        def _():
            for part in range(2):
                held[part, s, k + reach] += sources[part, s]


def force_emits(plan, emits, sources, power, slab):
    first_plane = lax.axis_index("depth") * slab
    for s in range(sources.shape[1]):
        k = plan[s] - first_plane

        @pl.when((k >= 0) & (k < slab))
        def _():
            src = sources[0, s], sources[1, s]
            onward = cmul(tile_of(power, slab - 1 - k), src)
            back = cmul(tile_of(power, k), src)
            for part in range(2):
                emits[0, part, s] += onward[part]
                emits[1, part, s] += back[part]


def halves(count):
    return (0, count // 2), (count // 2, count)


def fill_send(slots, full, passage):
    place = lax.axis_index("depth")

    def one(chip, unused):
        for core, (a, b) in enumerate(halves(full.shape[2])):
            j = 2 * chip + core
            way = jnp.where(j > place, 0, 1)
            for part in range(2):
                slots[j, pl.ds(part * (b - a), b - a)] = full[way, part, a:b]
            if passage is not None:
                slots[j, 2 * (b - a)] = passage[0]
                slots[j, 2 * (b - a) + 1] = passage[1]
        return unused

    loop(0, slots.shape[0] // 2, one, 0, 4)


def arrange_kernel(start, send, given, made, rest):
    got_even, got_odd, pack = given
    full, slots, near, extra = made
    even = lax.rem(lax.axis_index("depth"), 2) == 0
    count = full.shape[2]
    weight, passage = pair(pack, MEDIA), pair(pack, MEDIA + 2)
    emits = [[pack[emit_tiles(count, way, part)] for part in range(2)] for way in range(2)]
    for s in range(count):
        at = [(part * count + s) * DEEP for part in range(2)]
        low = tuple(
            jnp.where(even, got_odd[i + DEEP - 1], got_even[i + DEEP - 1]) for i in at
        )
        high = tuple(jnp.where(even, got_even[i], got_odd[i]) for i in at)
        toward_next = add(add(cmul(weight, low), high), (emits[0][0][s], emits[0][1][s]))
        toward_prev = add(add(cmul(weight, high), low), (emits[1][0][s], emits[1][1][s]))
        for part in range(2):
            full[0, part, s] = toward_next[part]
            full[1, part, s] = toward_prev[part]
    fill_send(slots, full, passage)
    for side in range(2):
        first, second = (got_odd, got_even) if side == 0 else (got_even, got_odd)
        for i in range(2 * count):
            rows = pl.ds(i * DEEP, DEEP)
            near[side, i // count, i % count] = jnp.where(
                even, first[rows], second[rows]
            )
        for i in range(2):
            at = 2 * count * DEEP + i
            extra[side, i] = jnp.where(even, first[at], second[at])
    extra[0, 2] = extra[1, 2] = media_of(pack)[LAYER]


def prepare_kernel(start, send, given, made, rest):
    plan, near, extra, sources, guess = given
    res, near_media, waves = made
    (ref,) = rest
    _, count, slab, height, breadth = guess.shape
    tile = (height, breadth)
    masks = lane_masks(tile)
    place = lax.axis_index("depth")
    last_place = lax.axis_size("depth") - 1
    layer3 = extra[0, 2]
    layer = layer3 / damping
    factors = []
    for side in range(2):
        squared = extra[side, 1]
        inside = (place > 0) if side == 0 else (place < last_place)
        factors.append(
            set_media(near_media.at[side], squared, layer, extra[side, 0], slab, inside)
        )

    ws = list(factors)
    edge = DEEP - 1

    def keep_power(k, ws):
        for side in range(2):
            for way in range(2):
                if side == way:
                    i = k - (slab - edge + 1)
                    i = edge - 1 - i if side else i
                else:
                    i = k - 1
                    i = i if side else edge - 1 - i
                if 0 <= i < edge:
                    for part in range(2):
                        waves[side, way, i, part] = ws[side][part]

    def next_power(k, ws):
        return tuple(cmul(factors[side], ws[side]) for side in range(2))

    k = 1
    while k <= slab:
        if edge < k < slab - edge + 1:
            ws = loop(k, slab - edge + 1, next_power, tuple(ws), 8)
            k = slab - edge + 1
        keep_power(k, ws)
        ws = next_power(k, ws)
        k += 1
    for side in range(2):
        field = Field(ref, 0, height)
        field.clear()
        for i in range(DEEP + 1):
            for part in range(2):
                if side == 0:
                    value = near[0, part, :, i] if i < DEEP else guess[part, :, 0]
                else:
                    value = near[1, part, :, i - 1] if i > 0 else guess[part, :, slab - 1]
                field.put(part, i, value)
        lanes = Lanes(field, masks)
        for i in range(1, DEEP):
            r = field.minus_a(i, near_media[side, DIAGONAL], layer3, lanes.now)
            for part in range(2):
                res[side, part, :, i - 1] = r[part]
    plan = plan.wait()
    for s in range(count):
        k = plan[s] - place * slab
        for side, low in ((0, -edge), (1, slab)):
            i = k - low

            @pl.when((i >= 0) & (i < edge))
            def _():
                for part in range(2):
                    res[side, part, s, i] += sources[part, s]


def chain_kernel(at, start, send, given, made, rest):
    got, passages, full = given
    mine, theirs = made
    place = lax.axis_index("depth")
    last_place = lax.axis_size("depth") - 1
    count = full.shape[2]
    even = lax.rem(place, 2) == 0
    low = place - lax.rem(place, 2)
    high = low + 1
    (a, b), (c, d) = halves(count)
    width = b - a
    zero = jnp.zeros((width,) + full.shape[3:], jnp.float32)
    passage = lambda j: (passages[j, at], passages[j, at + 1])
    emit = lambda way: tuple(
        jnp.where(even, full[way, part, a:b], full[way, part, c:d]) for part in range(2)
    )
    came = lambda j: (got[j, pl.ds(0, width)], got[j, pl.ds(width, width)])

    def step(j, state):
        return add(cmul(passage(j), state), came(j))

    below = jnp.maximum(low - 1, 0)
    above = jnp.minimum(high + 1, last_place)
    next_before = lax.fori_loop(0, below, step, (zero, zero))
    next_low = pick(low > 0, step(below, next_before), (zero, zero))
    next_high = add(cmul(passage(low), next_low), pick(even, emit(0), came(low)))
    prev_after = lax.fori_loop(
        0, last_place - above, lambda t, state: step(last_place - t, state), (zero, zero)
    )
    prev_high = pick(high < last_place, step(above, prev_after), (zero, zero))
    prev_low = add(cmul(passage(high), prev_high), pick(even, came(high), emit(1)))
    for_low = next_before, next_low, prev_low, prev_high
    for_high = next_low, next_high, prev_high, prev_after
    for i in range(4):
        own, other = pick(even, for_low[i], for_high[i]), pick(even, for_high[i], for_low[i])
        for part in range(2):
            mine[i, part] = own[part]
            theirs[i, part] = other[part]


def set_incoming(ref, mine, theirs, full, passage):
    even = lax.rem(lax.axis_index("depth"), 2) == 0
    count = full.shape[2]
    spots = ((0, 0), (1, 0), (1, 1), (2, 1))
    for half, (a, b) in enumerate(halves(count)):
        own = even if half == 0 else jnp.logical_not(even)
        waves = [
            tuple(jnp.where(own, mine[i, part], theirs[i, part]) for part in range(2))
            for i in range(4)
        ]
        here = lambda way: (full[way, 0, a:b], full[way, 1, a:b])
        onward = add(cmul(passage, waves[1]), here(0))
        back = add(cmul(passage, waves[2]), here(1))
        for (side, way), value in zip(
            spots + ((2, 0), (0, 1)), [*waves, onward, back]
        ):
            for part in range(2):
                ref[side, way, part, a:b] = coupling * value[part]


class Stage:
    def __init__(self, below, own, above):
        self.below, self.own, self.above = below, own, above


def pipeline(stages, slab, carry, halfway):
    offsets = [LAG * (len(stages) - 1 - i) for i in range(len(stages))]
    trips = (slab - offsets[0]) // UNROLL

    def run(i, p, carry):
        out = stages[i].own(p, carry)
        return carry if out is None else out

    def own(i, start, stop, carry):
        body = lambda p, c: run(i, p, c)
        if start == 0 and stop > 0:
            carry = body(0, carry)
            start = 1
        if stop == slab and start < slab:
            return body(slab - 1, loop(start, slab - 1, body, carry))
        return loop(start, stop, body, carry)

    stages[0].below()
    stages[0].above()
    for i, stage in enumerate(stages):
        if i:
            stage.below()
        carry = own(i, 0, offsets[i], carry)

    def trip(t, carry):
        for i in reversed(range(len(stages))):
            for u in range(UNROLL):
                carry = run(i, t * UNROLL + offsets[i] + u, carry)
        return carry

    first = trips // 2
    carry = lax.fori_loop(0, first, trip, carry)
    halfway(0, [first * UNROLL + o for o in offsets])
    carry = lax.fori_loop(first, trips, trip, carry)
    halfway(1, [trips * UNROLL + o for o in offsets])
    for i, stage in enumerate(stages):
        carry = own(i, trips * UNROLL + offsets[i], slab, carry)
        if i:
            stage.above()
    return carry


def update_stages(
    reach, slab, tile, incoming, residual_of, media, near_media, power, waves,
    refs, emit, masks,
):
    edge = DEEP - 1
    first_update = Field(refs[0], -reach, tile[0])
    second_update = Field(refs[1], 1 - reach, tile[0])
    first_update.clear()
    second_update.clear()
    powers = (
        lambda p: (tile_of(waves, 0, 0, p + edge), tile_of(waves, 0, 1, p + edge)),
        lambda p: (tile_of(power, p + 1), tile_of(power, slab - p)),
        lambda p: (tile_of(waves, 1, 0, p - slab), tile_of(waves, 1, 1, p - slab)),
    )
    coefficients = near_media.at[0], media, near_media.at[1]
    first_lanes = Lanes(first_update, masks)
    second_lanes = Lanes(second_update, masks)

    def begin(which, p):
        on, off = powers[which](p)
        onward = incoming[which, 0, 0], incoming[which, 0, 1]
        back = incoming[which, 1, 0], incoming[which, 1, 1]
        c = add(cmul(on, onward), cmul(off, back))
        inverse = pair(coefficients[which], INVERSE)
        first_update.put_both(p, cmul(inverse, add(c, residual_of(which, p))))

    def second(which, p):
        here, total = first_update.around(p, first_lanes.now)
        smoothed = cmul(pair(coefficients[which], SECOND), total)
        second_update.put_both(p, add(here, smoothed))

    def third(which, p):
        here, total = second_update.around(p, second_lanes.now)
        smoothed = cmul(pair(coefficients[which], THIRD), total)
        u = add(scale(keep * (1.0 + keep), here), smoothed)
        emit(which, p, add(u, first_update.both(p)))

    def stage(body, margin):
        def beyond(which, a, b):
            for p in range(a, b):
                body(which, p)

        return Stage(
            lambda: beyond(0, margin - reach, 0),
            lambda p, unused: body(1, p),
            lambda: beyond(2, slab, slab + reach - margin),
        )

    return [stage(begin, 0), stage(second, 1), stage(third, 2)]


def middle_kernel(start, send, given, made, rest):
    (
        mine, theirs, plan, full, sources, pack, near_media, waves, near,
        near_residual, power, residual, guess,
    ) = given
    media = media_of(pack)
    new_field, new_residual, next_full, slots = made
    incoming, *refs = rest
    _, count, slab, height, breadth = guess.shape
    tile = (height, breadth)
    masks = lane_masks(tile)
    reach = DEEP - 1
    ext = reach - 2
    more = ext - 1
    new = Field(refs[2], -ext, height)
    new.clear()
    set_incoming(incoming, mine, theirs, full, tile_of(power, slab))

    def residual_of(which, p):
        if which == 1:
            r = residual[0, :, p], residual[1, :, p]
            if isinstance(p, int) and p == 0:
                r = add(r, (near[0, 0, :, DEEP - 1], near[0, 1, :, DEEP - 1]))
            if isinstance(p, int) and p == slab - 1:
                r = add(r, (near[1, 0, :, 0], near[1, 1, :, 0]))
            return r
        i = p + reach if which == 0 else p - slab
        return near_residual[which // 2, 0, :, i], near_residual[which // 2, 1, :, i]

    def emit(which, p, u):
        for part in range(2):
            if which == 1:
                value = guess[part, :, p] + u[part]
                new_field[part, :, p] = value
            else:
                i = p + DEEP if which == 0 else p - slab
                value = near[which // 2, part, :, i] + u[part]
            new.put(part, p, value)

    stages = update_stages(
        reach, slab, tile, incoming, residual_of, media, near_media, power, waves,
        refs, emit, masks,
    )

    layer3 = media[LAYER]
    factor = pair(media, WAVE)
    lanes = Lanes(new, masks)

    def residual_at(p, diagonal):
        r = new.minus_a(p, diagonal, layer3, lanes.now)
        for part in range(2):
            new_residual[part, :, p + more] = r[part]
        return r

    def beyond(side, a, b):
        for p in range(a, b):
            residual_at(p, near_media[side, DIAGONAL])

    def inside(p, carry):
        toward_next, toward_prev = carry
        r = residual_at(p, media[DIAGONAL])
        toward_next = add(cmul(factor, toward_next), r)
        toward_prev = add(toward_prev, cmul(tile_of(power, p), r))
        return toward_next, toward_prev

    stages.append(
        Stage(lambda: beyond(0, -more, 0), inside, lambda: beyond(1, slab, slab + more))
    )
    zero = jnp.zeros((count,) + tile, jnp.float32)
    carry = pipeline(stages, slab, ((zero, zero), (zero, zero)), lambda i, reached: None)
    for way in range(2):
        for part in range(2):
            next_full[way, part] = carry[way][part]
    plan = plan.wait()
    force_emits(plan, next_full, sources, power, slab)
    fill_send(slots, next_full, None)
    add_forcing(plan, new_residual, sources, more, slab)


def final_kernel(start, send, given, made, rest):
    (
        mine, theirs, full, pack, near_media, waves, power, residual, field,
    ) = given
    (out,) = made
    media = media_of(pack)
    held, incoming, *refs = rest
    _, count, slab, height, breadth = field.shape
    tile = (height, breadth)
    reach = 2
    masks = lane_masks(tile)
    set_incoming(incoming, mine, theirs, full, tile_of(power, slab))

    def residual_of(which, p):
        return residual[0, :, p + reach], residual[1, :, p + reach]

    def emit(which, p, u):
        for part in range(2):
            held[part, :, p] = field[part, :, p] + u[part]

    stages = update_stages(
        reach, slab, tile, incoming, residual_of, media, near_media, power, waves,
        refs, emit, masks,
    )
    sent = [0]

    def send_field(top):
        part = pl.ds(sent[0], top - sent[0])
        send(held.at[:, :, part], out.at[:, :, part])
        sent[0] = top

    pipeline(stages, slab, 0, lambda i, reached: send_field(reached[2]))
    send_field(slab)


def local(sources, plan, absorb, labels, region_kk, damp_cells, guess):
    size = lax.axis_size("depth")
    _, count, slab, height, breadth = guess.shape
    tile = (height, breadth)
    edge = DEEP - 1
    planes = lambda n: (2, count, n) + tile
    scratch = lambda shape: pltpu.VMEM(shape, jnp.float32)

    tiles = (2 * count * DEEP + 2,) + tile
    for_even, for_odd = kernel_call(
        pack_kernel,
        [(region_kk, "smem"), (absorb, "vmem"), (labels, "vmem"), (guess, "hbm")],
        [(tiles, "direct")] * 2,
        pieces=4 * count, cost=1_000_000, name="pack", limit=PACK,
    )
    even_pairs = [(i, i ^ 1) for i in range(size)]
    odd_pairs = [(i, i + 1) for i in range(1, size - 1, 2)]
    odd_pairs += [(b, a) for a, b in odd_pairs]
    got_odd = lax.ppermute(for_odd, "depth", odd_pairs)
    got_even = lax.ppermute(for_even, "depth", even_pairs)

    residual, pack, power = kernel_call(
        start_kernel,
        [
            (plan, "smem"), (region_kk, "smem"), (damp_cells, "smem"),
            (sources, "vmem"), (absorb, "vmem"), (labels, "vmem"), (guess, "hbm"),
        ],
        [
            (planes(slab), "direct"), ((MEDIA + 4 + 4 * count,) + tile, "direct"),
            ((slab + 1, 2) + tile, "direct"),
        ],
        [
            scratch(planes(slab)), scratch((2, 2, count) + tile),
            Field.shape(count, slab + 2, tile),
        ],
        pieces=PIECES, cost=20_000_000, name="start", limit=16,
    )
    width = count // 2
    full, slots, near, extra = kernel_call(
        arrange_kernel,
        [(got_even, "direct"), (got_odd, "direct"), (pack, "direct")],
        [
            ((2, 2, count) + tile, "direct"), ((size, 2 * width + 2) + tile, "direct"),
            ((2, 2, count, DEEP) + tile, "direct"), ((2, 3) + tile, "direct"),
        ],
        cost=1_000_000, name="arrange", limit=4,
    )
    first_got = lax.all_to_all(slots, "depth", 0, 0)
    near_residual, near_media, waves = kernel_call(
        prepare_kernel,
        [
            (plan, "smem"), (near, "direct"), (extra, "direct"),
            (sources, "direct"), (guess, "direct"),
        ],
        [
            ((2, 2, count, edge) + tile, "direct"), ((2, MEDIA) + tile, "direct"),
            ((2, 2, edge, 2) + tile, "direct"),
        ],
        [Field.shape(count, DEEP + 1, tile)],
        cost=4_000_000, name="prepare", limit=4,
    )

    def chain(got, full):
        mine, theirs = kernel_call(
            functools.partial(chain_kernel, 2 * width),
            [(got, "direct"), (first_got, "direct"), (full, "direct")],
            [((4, 2, width) + tile, "direct")] * 2,
            cost=1_000_000, name="chain", limit=4,
        )
        return mine, lax.ppermute(theirs, "depth", even_pairs)

    mine, theirs = chain(first_got, full)
    new_field, new_residual, next_full, slots = kernel_call(
        middle_kernel,
        [
            (mine, "direct"), (theirs, "direct"),
            (plan, "smem"), (full, "direct"), (sources, "direct"),
            (pack, "direct"), (near_media, "direct"), (waves, "direct"),
            (near, "direct"), (near_residual, "direct"), (power, "direct"),
            (residual, "direct"), (guess, "direct"),
        ],
        [
            (planes(slab), "direct"), (planes(slab + 2 * (DEEP - 4)), "direct"),
            ((2, 2, count) + tile, "direct"), ((size, 2 * width) + tile, "direct"),
        ],
        [
            scratch((3, 2, 2, count) + tile),
            Field.shape(count, slab + 2 * edge, tile),
            Field.shape(count, slab + 2 * edge - 2, tile),
            Field.shape(count, slab + 2 * edge - 4, tile),
        ],
        cost=80_000_000, name="middle", limit=20,
    )
    mine, theirs = chain(lax.all_to_all(slots, "depth", 0, 0), next_full)
    (out,) = kernel_call(
        final_kernel,
        [
            (mine, "direct"), (theirs, "direct"), (next_full, "direct"),
            (pack, "direct"), (near_media, "direct"), (waves, "direct"),
            (power, "direct"), (new_residual, "direct"), (new_field, "direct"),
        ],
        [(planes(slab), "hbm")],
        [
            scratch(planes(slab)), scratch((3, 2, 2, count) + tile),
            Field.shape(count, slab + 4, tile), Field.shape(count, slab + 2, tile),
        ],
        pieces=3, cost=60_000_000, name="final", limit=16,
    )
    return out


def solution(mesh):
    return jax.shard_map(
        local,
        mesh=mesh,
        in_specs=(
            P(None, "groups", None, None),
            P("groups"),
            P("depth", "groups", None),
            P("depth", "groups", None),
            P(),
            P("groups"),
            P(None, "groups", "depth", None, None),
        ),
        out_specs=P(None, "groups", "depth", None, None),
        check_vma=False,
    )
```

```python
import functools

import jax
import jax.numpy as jnp
from jax import lax
from jax.experimental import pallas as pl
from jax.experimental.pallas import tpu as pltpu
from jax.sharding import PartitionSpec as P

relax_weight = 0.8
shift_ratio = 0.5
damping = 3.0
coupling = 0.25
keep = 1.0 - relax_weight

DEEP = 6
UNROLL = 4
LAG = UNROLL + 1
PIECES = 4
PACK = 4


def cmul(a, b):
    return a[0] * b[0] - a[1] * b[1], a[0] * b[1] + a[1] * b[0]


def add(a, b):
    return a[0] + b[0], a[1] + b[1]


def scale(c, a):
    return c * a[0], c * a[1]


def pick(cond, a, b):
    return jnp.where(cond, a[0], b[0]), jnp.where(cond, a[1], b[1])


def tile_of(ref, *at):
    return ref[at + (0,)], ref[at + (1,)]


class Inward:
    def __init__(self, source, target, sem):
        self.ref = target
        self.copy = pltpu.make_async_copy(source, target, sem)
        self.copy.start()

    def wait(self):
        self.copy.wait()
        return self.ref


def kernel_call(body, inputs, outputs, scratch=(), pieces=0, cost=0, name=None, limit=56):
    n_in, n_out = len(inputs), len(outputs)
    pinned = ("hbm", "vmem", "smem")
    extra = []
    for array, place in inputs:
        if place in ("vmem", "smem"):
            space = pltpu.SMEM if place == "smem" else pltpu.VMEM
            extra.append(space(array.shape, array.dtype))
    for shape, place in outputs:
        if place == "vmem":
            extra.append(pltpu.VMEM(shape, jnp.float32))
    n_extra = len(extra)

    def kernel(*refs):
        ins, outs = refs[:n_in], refs[n_in : n_in + n_out]
        buffers = iter(refs[n_in + n_out : n_in + n_out + n_extra])
        sems = refs[n_in + n_out + n_extra]
        rest = refs[n_in + n_out + n_extra + 1 :]
        used = iter(range(n_extra + pieces))
        pending = []

        def start(source, target):
            return Inward(source, target, sems.at[next(used)])

        def send(source, target):
            pending.append(start(source, target))

        def arrive():
            given = []
            for ref, (_, place) in zip(ins, inputs):
                copied = place in ("vmem", "smem")
                given.append(start(ref, next(buffers)) if copied else ref)
            return given

        given = arrive()
        made = []
        for ref, (_, place) in zip(outs, outputs):
            if place != "vmem":
                made.append(ref)
            else:
                buffer = next(buffers)
                made.append((buffer, functools.partial(send, buffer, ref)))
        body(start, send, given, made, rest)
        for copy in pending:
            copy.wait()

    def spec(place):
        return pl.BlockSpec(memory_space=pltpu.VMEM if place == "direct" else pltpu.HBM)

    return pl.pallas_call(
        kernel,
        out_shape=tuple(jax.ShapeDtypeStruct(s, jnp.float32) for s, _ in outputs),
        in_specs=[spec(place) for _, place in inputs],
        out_specs=tuple(spec(place) for _, place in outputs),
        scratch_shapes=[
            *extra,
            pltpu.SemaphoreType.DMA((max(1, n_extra + pieces),)),
            *scratch,
        ],
        compiler_params=pltpu.CompilerParams(vmem_limit_bytes=limit << 20),
        cost_estimate=pl.CostEstimate(
            flops=cost, bytes_accessed=4 << 20, transcendentals=0
        ),
        name=name,
    )(*[
        pltpu.with_memory_space_constraint(array, pltpu.HBM) if place in pinned else array
        for array, place in inputs
    ])


def lane_sum(here, masks):
    breadth = here.shape[-1]
    axis = here.ndim - 1
    ahead = jnp.where(masks[0], pltpu.roll(here, 1, axis), 0.0)
    behind = jnp.where(masks[1], pltpu.roll(here, breadth - 1, axis), 0.0)
    return ahead + behind


class Field:
    def __init__(self, ref, first, height):
        self.ref, self.first, self.height = ref, first, height

    @staticmethod
    def shape(count, planes, tile):
        return pltpu.VMEM((2, count, (2 * planes + 1) * tile[0], tile[1]), jnp.float32)

    def rows(self, plane, shift=0):
        start = (2 * (plane - self.first) + 1) * self.height + shift
        if shift % self.height == 0:
            start = pl.multiple_of(start, self.height)
        return pl.ds(start, self.height)

    def clear(self):
        edge = self.ref[:, :, : self.height]
        self.ref[:, :, : self.height] = jnp.zeros_like(edge)

    def get(self, part, plane, shift=0):
        return self.ref[part, :, self.rows(plane, shift)]

    def both(self, plane):
        return self.get(0, plane), self.get(1, plane)

    def put(self, part, plane, value):
        self.ref[part, :, self.rows(plane)] = value
        self.ref[part, :, self.rows(plane, self.height)] = jnp.zeros_like(value)

    def put_both(self, plane, value):
        for part in range(2):
            self.put(part, plane, value[part])

    def bump(self, plane, s, value):
        for part in range(2):
            self.ref[part, s, self.rows(plane)] += value[part]

    def lanes(self, part, plane, masks):
        return lane_sum(self.get(part, plane), masks)

    def around(self, plane, lanes):
        heres, totals = [], []
        for part in range(2):
            here = self.get(part, plane)
            beside = self.get(part, plane, -1) + self.get(part, plane, 1)
            depth = self.get(part, plane - 1) + self.get(part, plane + 1)
            heres.append(here)
            totals.append((beside + depth) + lanes(part, plane))
        return tuple(heres), tuple(totals)

    def minus_a(self, plane, diagonal, layer3, lanes):
        here, total = self.around(plane, lanes)
        return (
            (total[0] - diagonal * here[0]) + layer3 * here[1],
            (total[1] - diagonal * here[1]) - layer3 * here[0],
        )


class Lanes:
    def __init__(self, field, masks):
        self.field, self.masks = field, masks

    def now(self, part, plane):
        return self.field.lanes(part, plane, self.masks)


def lane_masks(tile):
    lane = lax.broadcasted_iota(jnp.int32, tile, 1)
    return lane > 0, lane < tile[1] - 1


INVERSE, DIAGONAL, LAYER, WAVE, SECOND, THIRD, MEDIA = 0, 2, 3, 4, 6, 8, 10


def set_media(ref, squared, layer, absorb, slab, inside=None):
    diagonal = 6.0 - squared
    imag = shift_ratio * squared + damping * layer
    size = diagonal * diagonal + imag * imag
    inverse = relax_weight * diagonal / size, -relax_weight * imag / size
    if inside is not None:
        inverse = tuple(jnp.where(inside, v, 0.0) for v in inverse)
    grow = 1.0 + keep
    decay = jnp.exp(-absorb / slab)
    angle = jnp.sqrt(squared)
    factor = decay * jnp.cos(angle), decay * jnp.sin(angle)
    values = (
        *inverse, diagonal, damping * layer, *factor,
        *scale(1.0 / grow, inverse), *scale(grow, inverse),
    )
    for i, value in enumerate(values):
        ref[i] = value
    return factor


def pair(ref, i):
    return ref[i], ref[i + 1]


def region_values(labels, kk_ref):
    squared = jnp.zeros(labels.shape, jnp.float32)
    for region in range(kk_ref.shape[0]):
        squared = jnp.where(labels == region, kk_ref[region], squared)
    return squared


def loop(start, stop, body, carry, unroll=UNROLL):
    trips = (stop - start) // unroll

    def several(trip, carry):
        for i in range(unroll):
            carry = body(start + trip * unroll + i, carry)
        return carry

    if trips > 1:
        carry = lax.fori_loop(0, trips, several, carry)
        start += trips * unroll
    for plane in range(start, stop):
        carry = body(plane, carry)
    return carry


def cuts(planes, pieces=PIECES):
    edges = [planes * i // pieces for i in range(pieces + 1)]
    return list(zip(edges[:-1], edges[1:]))


def media_of(pack):
    return pack.at[pl.ds(0, MEDIA)]


def emit_tiles(count, way, part):
    return pl.ds(MEDIA + 4 + (2 * way + part) * count, count)


def side_tiles(count):
    return 2 * count * DEEP


def pack_kernel(start, send, given, made, rest):
    kk, absorb, labels, guess = given
    (out,) = made
    _, count, slab, *_ = guess.shape
    even = lax.rem(lax.axis_index("depth"), 2) == 0
    first = jnp.where(even, 0, slab - DEEP)
    for i in range(2 * count):
        send(
            guess.at[i // count, i % count, pl.ds(first, DEEP)],
            out.at[pl.ds(i * DEEP, DEEP)],
        )
    kk, absorb, labels = kk.wait(), absorb.wait(), labels.wait()
    out[side_tiles(count)] = absorb[0]
    out[side_tiles(count) + 1] = region_values(labels[0], kk)


def start_kernel(start, send, given, made, rest):
    plan, kk, damp, sources, absorb, labels, guess = given
    residual, pack, power, for_even = made
    loaded, emits, ref = rest
    _, count, slab, height, breadth = guess.shape
    tile = (height, breadth)
    media = media_of(pack)
    copies = []
    edges = [0] + [min(b + UNROLL, slab) for _, b in cuts(slab)]
    for a, b in zip(edges[:-1], edges[1:]):
        part = pl.ds(a, b - a)
        copies.append(start(guess.at[:, :, part], loaded.at[:, :, part]))
    masks = lane_masks(tile)
    field = Field(ref, -1, height)
    zero = jnp.zeros((count,) + tile, jnp.float32)
    field.clear()
    field.put_both(-1, (zero, zero))
    field.put_both(slab, (zero, zero))
    lanes = Lanes(field, masks)

    def fill(p):
        for part in range(2):
            value = loaded[part, :, p]
            field.put(part, p, value)

    plan, kk, damp = plan.wait(), kk.wait(), damp.wait()
    row = lax.broadcasted_iota(jnp.int32, tile, 0)
    lane = lax.broadcasted_iota(jnp.int32, tile, 1)
    cell = row * breadth + lane

    def mark(i, hit):
        return jnp.where(cell == damp[i], 1.0, hit)

    layer = loop(0, damp.shape[0], mark, jnp.zeros(tile, jnp.float32), 16)
    sources, absorb, labels = sources.wait(), absorb.wait(), labels.wait()
    squared = region_values(labels[0], kk)
    factor = set_media(media, squared, layer, absorb[0], slab)
    diagonal, layer3 = media[DIAGONAL], media[LAYER]
    inverse = pair(media, INVERSE)

    def plane(k, carry):
        toward_next, toward_prev, w = carry
        power[k, 0], power[k, 1] = w
        r = field.minus_a(k, diagonal, layer3, lanes.now)
        residual[0, :, k], residual[1, :, k] = cmul(inverse, r)
        toward_next = add(cmul(factor, toward_next), r)
        toward_prev = add(toward_prev, cmul(w, r))
        return toward_next, toward_prev, cmul(factor, w)

    one = jnp.ones(tile, jnp.float32), jnp.zeros(tile, jnp.float32)
    carry = ((zero, zero), (zero, zero), one)
    for (a, b), copy in zip(cuts(slab), copies):
        copy.wait()
        if a == 0:
            fill(0)

        def group(trip, carry):
            base = a + trip * UNROLL
            for i in range(UNROLL):
                fill(base + i + 1)
            for i in range(UNROLL):
                carry = plane(base + i, carry)
            return carry

        trips = (min(b, slab - 1) - a) // UNROLL
        carry = lax.fori_loop(0, trips, group, carry)
        for k in range(a + trips * UNROLL, b):
            if k + 1 < slab:
                fill(k + 1)
            carry = plane(k, carry)
    toward_next, toward_prev, w = carry
    power[slab, 0], power[slab, 1] = w
    add_forcing(plan, residual, sources, 0, slab, inverse)
    for part in range(2):
        emits[0, part] = toward_next[part]
        emits[1, part] = toward_prev[part]
        pack[MEDIA + part] = power[slab - 1, part]
        pack[MEDIA + 2 + part] = power[slab, part]
    force_emits(plan, emits, sources, power, slab)
    for way in range(2):
        for part in range(2):
            pack[emit_tiles(count, way, part)] = emits[way, part]
    first_plane = jnp.where(lax.rem(lax.axis_index("depth"), 2) == 0, slab - DEEP, 0)
    for i in range(2 * count):
        for_even[pl.ds(i * DEEP, DEEP)] = loaded[
            i // count, i % count, pl.ds(first_plane, DEEP)
        ]
    for_even[side_tiles(count)] = absorb[0]
    for_even[side_tiles(count) + 1] = squared


def add_forcing(plan, held, sources, reach, slab, inverse=None):
    first_plane = lax.axis_index("depth") * slab
    for s in range(sources.shape[1]):
        k = plan[s] - first_plane

        @pl.when((k >= -reach) & (k < slab + reach))
        def _():
            src = sources[0, s], sources[1, s]
            if inverse is not None:
                src = cmul(inverse, src)
            for part in range(2):
                held[part, s, k + reach] += src[part]


def force_emits(plan, emits, sources, power, slab):
    first_plane = lax.axis_index("depth") * slab
    for s in range(sources.shape[1]):
        k = plan[s] - first_plane

        @pl.when((k >= 0) & (k < slab))
        def _():
            src = sources[0, s], sources[1, s]
            onward = cmul(tile_of(power, slab - 1 - k), src)
            back = cmul(tile_of(power, k), src)
            for part in range(2):
                emits[0, part, s] += onward[part]
                emits[1, part, s] += back[part]


def halves(count):
    return (0, count // 2), (count // 2, count)


def fill_send(slots, full, passage):
    place = lax.axis_index("depth")

    def one(chip, unused):
        for core, (a, b) in enumerate(halves(full.shape[2])):
            j = 2 * chip + core
            way = jnp.where(j > place, 0, 1)
            for part in range(2):
                slots[j, pl.ds(part * (b - a), b - a)] = full[way, part, a:b]
            if passage is not None:
                slots[j, 2 * (b - a)] = passage[0]
                slots[j, 2 * (b - a) + 1] = passage[1]
        return unused

    loop(0, slots.shape[0] // 2, one, 0, 4)


def arrange_kernel(start, send, given, made, rest):
    got_even, got_odd, pack = given
    full, slots, near, extra = made
    even = lax.rem(lax.axis_index("depth"), 2) == 0
    count = full.shape[2]
    weight, passage = pair(pack, MEDIA), pair(pack, MEDIA + 2)
    emits = [[pack[emit_tiles(count, way, part)] for part in range(2)] for way in range(2)]
    for s in range(count):
        at = [(part * count + s) * DEEP for part in range(2)]
        low = tuple(
            jnp.where(even, got_odd[i + DEEP - 1], got_even[i + DEEP - 1]) for i in at
        )
        high = tuple(jnp.where(even, got_even[i], got_odd[i]) for i in at)
        toward_next = add(add(cmul(weight, low), high), (emits[0][0][s], emits[0][1][s]))
        toward_prev = add(add(cmul(weight, high), low), (emits[1][0][s], emits[1][1][s]))
        for part in range(2):
            full[0, part, s] = toward_next[part]
            full[1, part, s] = toward_prev[part]
    fill_send(slots, full, passage)
    for side in range(2):
        first, second = (got_odd, got_even) if side == 0 else (got_even, got_odd)
        for i in range(2 * count):
            rows = pl.ds(i * DEEP, DEEP)
            near[side, i // count, i % count] = jnp.where(
                even, first[rows], second[rows]
            )
        for i in range(2):
            at = 2 * count * DEEP + i
            extra[side, i] = jnp.where(even, first[at], second[at])
    extra[0, 2] = extra[1, 2] = media_of(pack)[LAYER]


def prepare_kernel(start, send, given, made, rest):
    plan, near, extra, sources, guess = given
    res, near_media, waves = made
    (ref,) = rest
    _, count, slab, height, breadth = guess.shape
    tile = (height, breadth)
    masks = lane_masks(tile)
    place = lax.axis_index("depth")
    last_place = lax.axis_size("depth") - 1
    layer3 = extra[0, 2]
    layer = layer3 / damping
    factors = []
    for side in range(2):
        squared = extra[side, 1]
        inside = (place > 0) if side == 0 else (place < last_place)
        factors.append(
            set_media(near_media.at[side], squared, layer, extra[side, 0], slab, inside)
        )

    ws = list(factors)
    edge = DEEP - 1

    def keep_power(k, ws):
        for side in range(2):
            for way in range(2):
                if side == way:
                    i = k - (slab - edge + 1)
                    i = edge - 1 - i if side else i
                else:
                    i = k - 1
                    i = i if side else edge - 1 - i
                if 0 <= i < edge:
                    for part in range(2):
                        waves[side, way, i, part] = ws[side][part]

    def next_power(k, ws):
        return tuple(cmul(factors[side], ws[side]) for side in range(2))

    k = 1
    while k <= slab:
        if edge < k < slab - edge + 1:
            ws = loop(k, slab - edge + 1, next_power, tuple(ws), 8)
            k = slab - edge + 1
        keep_power(k, ws)
        ws = next_power(k, ws)
        k += 1
    for side in range(2):
        field = Field(ref, 0, height)
        field.clear()
        for i in range(DEEP + 1):
            for part in range(2):
                if side == 0:
                    value = near[0, part, :, i] if i < DEEP else guess[part, :, 0]
                else:
                    value = near[1, part, :, i - 1] if i > 0 else guess[part, :, slab - 1]
                field.put(part, i, value)
        lanes = Lanes(field, masks)
        for i in range(1, DEEP):
            r = field.minus_a(i, near_media[side, DIAGONAL], layer3, lanes.now)
            r = cmul(pair(near_media.at[side], INVERSE), r)
            for part in range(2):
                res[side, part, :, i - 1] = r[part]
    plan = plan.wait()
    for s in range(count):
        k = plan[s] - place * slab
        for side, low in ((0, -edge), (1, slab)):
            i = k - low

            @pl.when((i >= 0) & (i < edge))
            def _():
                src = sources[0, s], sources[1, s]
                src = cmul(pair(near_media.at[side], INVERSE), src)
                for part in range(2):
                    res[side, part, s, i] += src[part]


def chain_kernel(at, start, send, given, made, rest):
    got, passages, full = given
    mine, theirs = made
    place = lax.axis_index("depth")
    last_place = lax.axis_size("depth") - 1
    count = full.shape[2]
    even = lax.rem(place, 2) == 0
    low = place - lax.rem(place, 2)
    high = low + 1
    (a, b), (c, d) = halves(count)
    width = b - a
    zero = jnp.zeros((width,) + full.shape[3:], jnp.float32)
    passage = lambda j: (passages[j, at], passages[j, at + 1])
    emit = lambda way: tuple(
        jnp.where(even, full[way, part, a:b], full[way, part, c:d]) for part in range(2)
    )
    came = lambda j: (got[j, pl.ds(0, width)], got[j, pl.ds(width, width)])

    def step(j, state):
        return add(cmul(passage(j), state), came(j))

    below = jnp.maximum(low - 1, 0)
    above = jnp.minimum(high + 1, last_place)
    next_before = lax.fori_loop(0, below, step, (zero, zero))
    next_low = pick(low > 0, step(below, next_before), (zero, zero))
    next_high = add(cmul(passage(low), next_low), pick(even, emit(0), came(low)))
    prev_after = lax.fori_loop(
        0, last_place - above, lambda t, state: step(last_place - t, state), (zero, zero)
    )
    prev_high = pick(high < last_place, step(above, prev_after), (zero, zero))
    prev_low = add(cmul(passage(high), prev_high), pick(even, came(high), emit(1)))
    for_low = next_before, next_low, prev_low, prev_high
    for_high = next_low, next_high, prev_high, prev_after
    for i in range(4):
        own, other = pick(even, for_low[i], for_high[i]), pick(even, for_high[i], for_low[i])
        for part in range(2):
            mine[i, part] = own[part]
            theirs[i, part] = other[part]


def set_incoming(ref, mine, theirs, full, passage, media, near_media):
    inverses = [
        scale(coupling, pair(m, INVERSE))
        for m in (near_media.at[0], media, near_media.at[1])
    ]
    even = lax.rem(lax.axis_index("depth"), 2) == 0
    count = full.shape[2]
    spots = ((0, 0), (1, 0), (1, 1), (2, 1))
    for half, (a, b) in enumerate(halves(count)):
        own = even if half == 0 else jnp.logical_not(even)
        waves = [
            tuple(jnp.where(own, mine[i, part], theirs[i, part]) for part in range(2))
            for i in range(4)
        ]
        here = lambda way: (full[way, 0, a:b], full[way, 1, a:b])
        onward = add(cmul(passage, waves[1]), here(0))
        back = add(cmul(passage, waves[2]), here(1))
        for (side, way), value in zip(
            spots + ((2, 0), (0, 1)), [*waves, onward, back]
        ):
            ref[side, way, 0, a:b], ref[side, way, 1, a:b] = cmul(inverses[side], value)


class Stage:
    def __init__(self, below, own, above):
        self.below, self.own, self.above = below, own, above


def pipeline(stages, slab, carry, halfway):
    offsets = [LAG * (len(stages) - 1 - i) for i in range(len(stages))]
    trips = (slab - offsets[0]) // UNROLL

    def run(i, p, carry):
        out = stages[i].own(p, carry)
        return carry if out is None else out

    def own(i, start, stop, carry):
        body = lambda p, c: run(i, p, c)
        if start == 0 and stop > 0:
            carry = body(0, carry)
            start = 1
        if stop == slab and start < slab:
            return body(slab - 1, loop(start, slab - 1, body, carry))
        return loop(start, stop, body, carry)

    stages[0].below()
    stages[0].above()
    for i, stage in enumerate(stages):
        if i:
            stage.below()
        carry = own(i, 0, offsets[i], carry)

    def trip(t, carry):
        for i in reversed(range(len(stages))):
            for u in range(UNROLL):
                carry = run(i, t * UNROLL + offsets[i] + u, carry)
        return carry

    first = trips // 2
    carry = lax.fori_loop(0, first, trip, carry)
    halfway(0, [first * UNROLL + o for o in offsets])
    carry = lax.fori_loop(first, trips, trip, carry)
    halfway(1, [trips * UNROLL + o for o in offsets])
    for i, stage in enumerate(stages):
        carry = own(i, trips * UNROLL + offsets[i], slab, carry)
        if i:
            stage.above()
    return carry


def update_stages(
    reach, slab, tile, incoming, residual_of, media, near_media, power, waves,
    refs, emit, masks,
):
    edge = DEEP - 1
    first_update = Field(refs[0], -reach, tile[0])
    second_update = Field(refs[1], 1 - reach, tile[0])
    first_update.clear()
    second_update.clear()
    powers = (
        lambda p: (tile_of(waves, 0, 0, p + edge), tile_of(waves, 0, 1, p + edge)),
        lambda p: (tile_of(power, p + 1), tile_of(power, slab - p)),
        lambda p: (tile_of(waves, 1, 0, p - slab), tile_of(waves, 1, 1, p - slab)),
    )
    coefficients = near_media.at[0], media, near_media.at[1]
    first_lanes = Lanes(first_update, masks)
    second_lanes = Lanes(second_update, masks)

    def begin(which, p):
        on, off = powers[which](p)
        onward = incoming[which, 0, 0], incoming[which, 0, 1]
        back = incoming[which, 1, 0], incoming[which, 1, 1]
        c = add(cmul(on, onward), cmul(off, back))
        first_update.put_both(p, add(c, residual_of(which, p)))

    def second(which, p):
        here, total = first_update.around(p, first_lanes.now)
        smoothed = cmul(pair(coefficients[which], SECOND), total)
        second_update.put_both(p, add(here, smoothed))

    def third(which, p):
        here, total = second_update.around(p, second_lanes.now)
        smoothed = cmul(pair(coefficients[which], THIRD), total)
        u = add(scale(keep * (1.0 + keep), here), smoothed)
        emit(which, p, add(u, first_update.both(p)))

    def stage(body, margin):
        def beyond(which, a, b):
            for p in range(a, b):
                body(which, p)

        return Stage(
            lambda: beyond(0, margin - reach, 0),
            lambda p, unused: body(1, p),
            lambda: beyond(2, slab, slab + reach - margin),
        )

    return [stage(begin, 0), stage(second, 1), stage(third, 2)]


def middle_kernel(start, send, given, made, rest):
    (
        mine, theirs, plan, full, sources, pack, near_media, waves, near,
        near_residual, power, residual, guess,
    ) = given
    media = media_of(pack)
    new_field, new_residual, next_full, slots = made
    incoming, *refs = rest
    _, count, slab, height, breadth = guess.shape
    tile = (height, breadth)
    masks = lane_masks(tile)
    reach = DEEP - 1
    ext = reach - 2
    more = ext - 1
    new = Field(refs[2], -ext, height)
    new.clear()
    set_incoming(
        incoming, mine, theirs, full, tile_of(power, slab), media, near_media
    )

    def residual_of(which, p):
        if which == 1:
            r = residual[0, :, p], residual[1, :, p]
            lacks = None
            if isinstance(p, int) and p == 0:
                lacks = near[0, 0, :, DEEP - 1], near[0, 1, :, DEEP - 1]
            if isinstance(p, int) and p == slab - 1:
                lacks = near[1, 0, :, 0], near[1, 1, :, 0]
            return r if lacks is None else add(r, cmul(pair(media, INVERSE), lacks))
        i = p + reach if which == 0 else p - slab
        return near_residual[which // 2, 0, :, i], near_residual[which // 2, 1, :, i]

    def emit(which, p, u):
        for part in range(2):
            if which == 1:
                value = guess[part, :, p] + u[part]
                new_field[part, :, p] = value
            else:
                i = p + DEEP if which == 0 else p - slab
                value = near[which // 2, part, :, i] + u[part]
            new.put(part, p, value)

    stages = update_stages(
        reach, slab, tile, incoming, residual_of, media, near_media, power, waves,
        refs, emit, masks,
    )

    layer3 = media[LAYER]
    factor = pair(media, WAVE)
    lanes = Lanes(new, masks)

    def residual_at(p, diagonal):
        r = new.minus_a(p, diagonal, layer3, lanes.now)
        for part in range(2):
            new_residual[part, :, p + more] = r[part]
        return r

    def beyond(side, a, b):
        for p in range(a, b):
            residual_at(p, near_media[side, DIAGONAL])

    def inside(p, carry):
        toward_next, toward_prev = carry
        r = residual_at(p, media[DIAGONAL])
        toward_next = add(cmul(factor, toward_next), r)
        toward_prev = add(toward_prev, cmul(tile_of(power, p), r))
        return toward_next, toward_prev

    stages.append(
        Stage(lambda: beyond(0, -more, 0), inside, lambda: beyond(1, slab, slab + more))
    )
    zero = jnp.zeros((count,) + tile, jnp.float32)
    carry = pipeline(stages, slab, ((zero, zero), (zero, zero)), lambda i, reached: None)
    for way in range(2):
        for part in range(2):
            next_full[way, part] = carry[way][part]
    plan = plan.wait()
    force_emits(plan, next_full, sources, power, slab)
    fill_send(slots, next_full, None)
    add_forcing(plan, new_residual, sources, more, slab)


def scale_kernel(start, send, given, made, rest):
    residual, pack, near_media = given
    (out,) = made
    planes = residual.shape[2]
    reach = DEEP - 4

    def one(p, m):
        value = cmul(pair(m, INVERSE), (residual[0, :, p], residual[1, :, p]))
        out[0, :, p], out[1, :, p] = value

    media = media_of(pack)
    for p in range(reach):
        one(p, near_media.at[0])
        one(planes - 1 - p, near_media.at[1])
    loop(reach, planes - reach, lambda p, c: one(p, media) or c, 0, 8)


def final_kernel(start, send, given, made, rest):
    (
        mine, theirs, full, pack, near_media, waves, power, residual, field,
    ) = given
    (out,) = made
    media = media_of(pack)
    held, incoming, *refs = rest
    _, count, slab, height, breadth = field.shape
    tile = (height, breadth)
    reach = 2
    masks = lane_masks(tile)
    set_incoming(
        incoming, mine, theirs, full, tile_of(power, slab), media, near_media
    )

    def residual_of(which, p):
        return residual[0, :, p + reach], residual[1, :, p + reach]

    def emit(which, p, u):
        for part in range(2):
            held[part, :, p] = field[part, :, p] + u[part]

    stages = update_stages(
        reach, slab, tile, incoming, residual_of, media, near_media, power, waves,
        refs, emit, masks,
    )
    sent = [0]

    def send_field(top):
        part = pl.ds(sent[0], top - sent[0])
        send(held.at[:, :, part], out.at[:, :, part])
        sent[0] = top

    pipeline(stages, slab, 0, lambda i, reached: send_field(reached[2]))
    send_field(slab)


def local(sources, plan, absorb, labels, region_kk, damp_cells, guess):
    size = lax.axis_size("depth")
    _, count, slab, height, breadth = guess.shape
    tile = (height, breadth)
    edge = DEEP - 1
    planes = lambda n: (2, count, n) + tile
    scratch = lambda shape: pltpu.VMEM(shape, jnp.float32)

    tiles = (side_tiles(count) + 2,) + tile
    (for_odd,) = kernel_call(
        pack_kernel,
        [(region_kk, "smem"), (absorb, "vmem"), (labels, "vmem"), (guess, "hbm")],
        [(tiles, "direct")],
        pieces=2 * count, cost=1_000_000, name="pack", limit=PACK,
    )
    even_pairs = [(i, i ^ 1) for i in range(size)]
    odd_pairs = [(i, i + 1) for i in range(1, size - 1, 2)]
    odd_pairs += [(b, a) for a, b in odd_pairs]
    got_odd = lax.ppermute(for_odd, "depth", odd_pairs)

    residual, pack, power, for_even = kernel_call(
        start_kernel,
        [
            (plan, "smem"), (region_kk, "smem"), (damp_cells, "smem"),
            (sources, "vmem"), (absorb, "vmem"), (labels, "vmem"), (guess, "hbm"),
        ],
        [
            (planes(slab), "direct"), ((MEDIA + 4 + 4 * count,) + tile, "direct"),
            ((slab + 1, 2) + tile, "direct"), (tiles, "direct"),
        ],
        [
            scratch(planes(slab)), scratch((2, 2, count) + tile),
            Field.shape(count, slab + 2, tile),
        ],
        pieces=PIECES, cost=20_000_000, name="start", limit=16,
    )
    got_even = lax.ppermute(for_even, "depth", even_pairs)
    width = count // 2
    full, slots, near, extra = kernel_call(
        arrange_kernel,
        [(got_even, "direct"), (got_odd, "direct"), (pack, "direct")],
        [
            ((2, 2, count) + tile, "direct"), ((size, 2 * width + 2) + tile, "direct"),
            ((2, 2, count, DEEP) + tile, "direct"), ((2, 3) + tile, "direct"),
        ],
        cost=1_000_000, name="arrange", limit=4,
    )
    first_got = lax.all_to_all(slots, "depth", 0, 0)
    near_residual, near_media, waves = kernel_call(
        prepare_kernel,
        [
            (plan, "smem"), (near, "direct"), (extra, "direct"),
            (sources, "direct"), (guess, "direct"),
        ],
        [
            ((2, 2, count, edge) + tile, "direct"), ((2, MEDIA) + tile, "direct"),
            ((2, 2, edge, 2) + tile, "direct"),
        ],
        [Field.shape(count, DEEP + 1, tile)],
        cost=4_000_000, name="prepare", limit=4,
    )

    def chain(got, full):
        mine, theirs = kernel_call(
            functools.partial(chain_kernel, 2 * width),
            [(got, "direct"), (first_got, "direct"), (full, "direct")],
            [((4, 2, width) + tile, "direct")] * 2,
            cost=1_000_000, name="chain", limit=4,
        )
        return mine, lax.ppermute(theirs, "depth", even_pairs)

    mine, theirs = chain(first_got, full)
    new_field, new_residual, next_full, slots = kernel_call(
        middle_kernel,
        [
            (mine, "direct"), (theirs, "direct"),
            (plan, "smem"), (full, "direct"), (sources, "direct"),
            (pack, "direct"), (near_media, "direct"), (waves, "direct"),
            (near, "direct"), (near_residual, "direct"), (power, "direct"),
            (residual, "direct"), (guess, "direct"),
        ],
        [
            (planes(slab), "direct"), (planes(slab + 2 * (DEEP - 4)), "direct"),
            ((2, 2, count) + tile, "direct"), ((size, 2 * width) + tile, "direct"),
        ],
        [
            scratch((3, 2, 2, count) + tile),
            Field.shape(count, slab + 2 * edge, tile),
            Field.shape(count, slab + 2 * edge - 2, tile),
            Field.shape(count, slab + 2 * edge - 4, tile),
        ],
        cost=80_000_000, name="middle", limit=20,
    )
    mine, theirs = chain(lax.all_to_all(slots, "depth", 0, 0), next_full)
    (scaled,) = kernel_call(
        scale_kernel,
        [(new_residual, "direct"), (pack, "direct"), (near_media, "direct")],
        [(planes(slab + 2 * (DEEP - 4)), "direct")],
        cost=4_000_000, name="scale", limit=4,
    )
    (out,) = kernel_call(
        final_kernel,
        [
            (mine, "direct"), (theirs, "direct"), (next_full, "direct"),
            (pack, "direct"), (near_media, "direct"), (waves, "direct"),
            (power, "direct"), (scaled, "direct"), (new_field, "direct"),
        ],
        [(planes(slab), "hbm")],
        [
            scratch(planes(slab)), scratch((3, 2, 2, count) + tile),
            Field.shape(count, slab + 4, tile), Field.shape(count, slab + 2, tile),
        ],
        pieces=3, cost=60_000_000, name="final", limit=16,
    )
    return out


def solution(mesh):
    return jax.shard_map(
        local,
        mesh=mesh,
        in_specs=(
            P(None, "groups", None, None),
            P("groups"),
            P("depth", "groups", None),
            P("depth", "groups", None),
            P(),
            P("groups"),
            P(None, "groups", "depth", None, None),
        ),
        out_specs=P(None, "groups", "depth", None, None),
        check_vma=False,
    )
```

```python
import functools

import jax
import jax.numpy as jnp
from jax import lax
from jax.experimental import pallas as pl
from jax.experimental.pallas import tpu as pltpu
from jax.sharding import PartitionSpec as P

relax_weight = 0.8
shift_ratio = 0.5
damping = 3.0
coupling = 0.25
keep = 1.0 - relax_weight

DEEP = 6
UNROLL = 4
LAG = UNROLL + 1


def cmul(a, b):
    return a[0] * b[0] - a[1] * b[1], a[0] * b[1] + a[1] * b[0]


def add(a, b):
    return a[0] + b[0], a[1] + b[1]


def scale(c, a):
    return c * a[0], c * a[1]


def pick(cond, a, b):
    return jnp.where(cond, a[0], b[0]), jnp.where(cond, a[1], b[1])


def tile_of(ref, *at):
    return ref[at + (0,)], ref[at + (1,)]


class Inward:
    def __init__(self, source, target, sem):
        self.ref = target
        self.copy = pltpu.make_async_copy(source, target, sem)
        self.copy.start()

    def wait(self):
        self.copy.wait()
        return self.ref


def kernel_call(body, inputs, outputs, scratch=(), pieces=0, cost=0, name=None, limit=56):
    n_in, n_out = len(inputs), len(outputs)
    pinned = ("hbm", "vmem", "smem")
    extra = []
    for array, place in inputs:
        if place in ("vmem", "smem"):
            space = pltpu.SMEM if place == "smem" else pltpu.VMEM
            extra.append(space(array.shape, array.dtype))
    for shape, place in outputs:
        if place == "vmem":
            extra.append(pltpu.VMEM(shape, jnp.float32))
    n_extra = len(extra)

    def kernel(*refs):
        ins, outs = refs[:n_in], refs[n_in : n_in + n_out]
        buffers = iter(refs[n_in + n_out : n_in + n_out + n_extra])
        sems = refs[n_in + n_out + n_extra]
        rest = refs[n_in + n_out + n_extra + 1 :]
        used = iter(range(n_extra + pieces))
        pending = []

        def start(source, target):
            return Inward(source, target, sems.at[next(used)])

        def send(source, target):
            pending.append(start(source, target))

        def arrive():
            given = []
            for ref, (_, place) in zip(ins, inputs):
                copied = place in ("vmem", "smem")
                given.append(start(ref, next(buffers)) if copied else ref)
            return given

        given = arrive()
        made = []
        for ref, (_, place) in zip(outs, outputs):
            if place != "vmem":
                made.append(ref)
            else:
                buffer = next(buffers)
                made.append((buffer, functools.partial(send, buffer, ref)))
        body(start, send, given, made, rest)
        for copy in pending:
            copy.wait()

    def spec(place):
        return pl.BlockSpec(memory_space=pltpu.VMEM if place == "direct" else pltpu.HBM)

    return pl.pallas_call(
        kernel,
        out_shape=tuple(jax.ShapeDtypeStruct(s, jnp.float32) for s, _ in outputs),
        in_specs=[spec(place) for _, place in inputs],
        out_specs=tuple(spec(place) for _, place in outputs),
        scratch_shapes=[
            *extra,
            pltpu.SemaphoreType.DMA((max(1, n_extra + pieces),)),
            *scratch,
        ],
        compiler_params=pltpu.CompilerParams(vmem_limit_bytes=limit << 20),
        cost_estimate=pl.CostEstimate(
            flops=cost, bytes_accessed=4 << 20, transcendentals=0
        ),
        name=name,
    )(*[
        pltpu.with_memory_space_constraint(array, pltpu.HBM) if place in pinned else array
        for array, place in inputs
    ])


def lane_sum(here, masks):
    breadth = here.shape[-1]
    axis = here.ndim - 1
    ahead = jnp.where(masks[0], pltpu.roll(here, 1, axis), 0.0)
    behind = jnp.where(masks[1], pltpu.roll(here, breadth - 1, axis), 0.0)
    return ahead + behind


class Field:
    def __init__(self, ref, first, height):
        self.ref, self.first, self.height = ref, first, height

    @staticmethod
    def shape(count, planes, tile):
        return pltpu.VMEM((2, count, (2 * planes + 1) * tile[0], tile[1]), jnp.float32)

    def rows(self, plane, shift=0):
        start = (2 * (plane - self.first) + 1) * self.height + shift
        if shift % self.height == 0:
            start = pl.multiple_of(start, self.height)
        return pl.ds(start, self.height)

    def clear(self):
        edge = self.ref[:, :, : self.height]
        self.ref[:, :, : self.height] = jnp.zeros_like(edge)

    def get(self, part, plane, shift=0):
        return self.ref[part, :, self.rows(plane, shift)]

    def both(self, plane):
        return self.get(0, plane), self.get(1, plane)

    def put(self, part, plane, value):
        self.ref[part, :, self.rows(plane)] = value
        self.ref[part, :, self.rows(plane, self.height)] = jnp.zeros_like(value)

    def put_both(self, plane, value):
        for part in range(2):
            self.put(part, plane, value[part])

    def bump(self, plane, s, value):
        for part in range(2):
            self.ref[part, s, self.rows(plane)] += value[part]

    def lanes(self, part, plane, masks):
        return lane_sum(self.get(part, plane), masks)

    def around(self, plane, lanes):
        heres, totals = [], []
        for part in range(2):
            here = self.get(part, plane)
            beside = self.get(part, plane, -1) + self.get(part, plane, 1)
            depth = self.get(part, plane - 1) + self.get(part, plane + 1)
            heres.append(here)
            totals.append((beside + depth) + lanes(part, plane))
        return tuple(heres), tuple(totals)

    def minus_a(self, plane, diagonal, layer3, lanes):
        here, total = self.around(plane, lanes)
        return (
            (total[0] - diagonal * here[0]) + layer3 * here[1],
            (total[1] - diagonal * here[1]) - layer3 * here[0],
        )


class Lanes:
    def __init__(self, field, masks):
        self.field, self.masks = field, masks

    def now(self, part, plane):
        return self.field.lanes(part, plane, self.masks)


def lane_masks(tile):
    lane = lax.broadcasted_iota(jnp.int32, tile, 1)
    return lane > 0, lane < tile[1] - 1


INVERSE, DIAGONAL, LAYER, WAVE, SECOND, THIRD, MEDIA = 0, 2, 3, 4, 6, 8, 10


def set_media(ref, squared, layer, absorb, slab, inside=None):
    diagonal = 6.0 - squared
    imag = shift_ratio * squared + damping * layer
    size = diagonal * diagonal + imag * imag
    inverse = relax_weight * diagonal / size, -relax_weight * imag / size
    if inside is not None:
        inverse = tuple(jnp.where(inside, v, 0.0) for v in inverse)
    grow = 1.0 + keep
    decay = jnp.exp(-absorb / slab)
    angle = jnp.sqrt(squared)
    factor = decay * jnp.cos(angle), decay * jnp.sin(angle)
    values = (
        *inverse, diagonal, damping * layer, *factor,
        *scale(1.0 / grow, inverse), *scale(grow, inverse),
    )
    for i, value in enumerate(values):
        ref[i] = value
    return factor


def pair(ref, i):
    return ref[i], ref[i + 1]


def region_values(labels, kk_ref):
    squared = jnp.zeros(labels.shape, jnp.float32)
    for region in range(kk_ref.shape[0]):
        squared = jnp.where(labels == region, kk_ref[region], squared)
    return squared


def loop(start, stop, body, carry, unroll=UNROLL):
    trips = (stop - start) // unroll

    def several(trip, carry):
        for i in range(unroll):
            carry = body(start + trip * unroll + i, carry)
        return carry

    if trips > 1:
        carry = lax.fori_loop(0, trips, several, carry)
        start += trips * unroll
    for plane in range(start, stop):
        carry = body(plane, carry)
    return carry


def media_of(pack):
    return pack.at[pl.ds(0, MEDIA)]


def emit_tiles(count, way, part):
    return pl.ds(MEDIA + 4 + (2 * way + part) * count, count)


def side_tiles(count):
    return 2 * count * DEEP


def pack_kernel(start, send, given, made, rest):
    kk, damp, absorb, labels, guess = given
    out, base = made
    _, count, slab, *tile = guess.shape
    even = lax.rem(lax.axis_index("depth"), 2) == 0
    first = jnp.where(even, 0, slab - DEEP)
    for i in range(2 * count):
        send(
            guess.at[i // count, i % count, pl.ds(first, DEEP)],
            out.at[pl.ds(i * DEEP, DEEP)],
        )
    row = lax.broadcasted_iota(jnp.int32, tuple(tile), 0)
    lane = lax.broadcasted_iota(jnp.int32, tuple(tile), 1)
    cell = row * tile[1] + lane
    kk, absorb, labels = kk.wait(), absorb.wait(), labels.wait()
    squared = region_values(labels[0], kk)
    out[side_tiles(count)] = absorb[0]
    out[side_tiles(count) + 1] = squared
    base[MEDIA] = absorb[0]
    base[MEDIA + 1] = squared
    damp = damp.wait()

    def mark(i, hit):
        return jnp.where(cell == damp[i], 1.0, hit)

    layer = loop(0, damp.shape[0], mark, jnp.zeros(tile, jnp.float32), 16)
    set_media(base, squared, layer, absorb[0], slab)


def start_kernel(start, send, given, made, rest):
    plan, sources, base, guess = given
    residual, pack, power, for_even = made
    emits, ref = rest
    _, count, slab, height, breadth = guess.shape
    tile = (height, breadth)
    media = media_of(pack)
    media[...] = base[:MEDIA]
    masks = lane_masks(tile)
    field = Field(ref, -1, height)
    zero = jnp.zeros((count,) + tile, jnp.float32)
    field.clear()
    field.put_both(-1, (zero, zero))
    field.put_both(slab, (zero, zero))
    lanes = Lanes(field, masks)
    diagonal, layer3 = media[DIAGONAL], media[LAYER]
    inverse, factor = pair(media, INVERSE), pair(media, WAVE)

    def fill(p):
        for part in range(2):
            field.put(part, p, guess[part, :, p])

    def plane(k, carry):
        toward_next, toward_prev, w = carry
        power[k, 0], power[k, 1] = w
        r = field.minus_a(k, diagonal, layer3, lanes.now)
        residual[0, :, k], residual[1, :, k] = cmul(inverse, r)
        toward_next = add(cmul(factor, toward_next), r)
        toward_prev = add(toward_prev, cmul(w, r))
        return toward_next, toward_prev, cmul(factor, w)

    one = jnp.ones(tile, jnp.float32), jnp.zeros(tile, jnp.float32)
    carry = ((zero, zero), (zero, zero), one)
    fill(0)

    def group(trip, carry):
        base = trip * UNROLL
        for i in range(UNROLL):
            fill(base + i + 1)
        for i in range(UNROLL):
            carry = plane(base + i, carry)
        return carry

    trips = (slab - 1) // UNROLL
    carry = lax.fori_loop(0, trips, group, carry)
    for k in range(trips * UNROLL, slab):
        if k + 1 < slab:
            fill(k + 1)
        carry = plane(k, carry)
    plan, sources = plan.wait(), sources.wait()
    toward_next, toward_prev, w = carry
    power[slab, 0], power[slab, 1] = w
    add_forcing(plan, residual, sources, 0, slab, inverse)
    for part in range(2):
        emits[0, part] = toward_next[part]
        emits[1, part] = toward_prev[part]
        pack[MEDIA + part] = power[slab - 1, part]
        pack[MEDIA + 2 + part] = power[slab, part]
    force_emits(plan, emits, sources, power, slab)
    for way in range(2):
        for part in range(2):
            pack[emit_tiles(count, way, part)] = emits[way, part]
    first_plane = jnp.where(lax.rem(lax.axis_index("depth"), 2) == 0, slab - DEEP, 0)
    for i in range(2 * count):
        for_even[pl.ds(i * DEEP, DEEP)] = guess[
            i // count, i % count, pl.ds(first_plane, DEEP)
        ]
    for_even[pl.ds(side_tiles(count), 2)] = base[MEDIA : MEDIA + 2]


def add_forcing(plan, held, sources, reach, slab, inverse=None):
    first_plane = lax.axis_index("depth") * slab
    for s in range(sources.shape[1]):
        k = plan[s] - first_plane

        @pl.when((k >= -reach) & (k < slab + reach))
        def _():
            src = sources[0, s], sources[1, s]
            if inverse is not None:
                src = cmul(inverse, src)
            for part in range(2):
                held[part, s, k + reach] += src[part]


def force_emits(plan, emits, sources, power, slab):
    first_plane = lax.axis_index("depth") * slab
    for s in range(sources.shape[1]):
        k = plan[s] - first_plane

        @pl.when((k >= 0) & (k < slab))
        def _():
            src = sources[0, s], sources[1, s]
            onward = cmul(tile_of(power, slab - 1 - k), src)
            back = cmul(tile_of(power, k), src)
            for part in range(2):
                emits[0, part, s] += onward[part]
                emits[1, part, s] += back[part]


def halves(count):
    return (0, count // 2), (count // 2, count)


def fill_send(slots, full, passage):
    place = lax.axis_index("depth")

    def one(chip, unused):
        for core, (a, b) in enumerate(halves(full.shape[2])):
            j = 2 * chip + core
            way = jnp.where(j > place, 0, 1)
            for part in range(2):
                slots[j, pl.ds(part * (b - a), b - a)] = full[way, part, a:b]
            if passage is not None:
                slots[j, 2 * (b - a)] = passage[0]
                slots[j, 2 * (b - a) + 1] = passage[1]
        return unused

    loop(0, slots.shape[0] // 2, one, 0, 4)


def arrange_kernel(start, send, given, made, rest):
    got_even, got_odd, pack = given
    full, slots, near, extra = made
    even = lax.rem(lax.axis_index("depth"), 2) == 0
    count = full.shape[2]
    weight, passage = pair(pack, MEDIA), pair(pack, MEDIA + 2)
    emits = [[pack[emit_tiles(count, way, part)] for part in range(2)] for way in range(2)]
    for s in range(count):
        at = [(part * count + s) * DEEP for part in range(2)]
        low = tuple(
            jnp.where(even, got_odd[i + DEEP - 1], got_even[i + DEEP - 1]) for i in at
        )
        high = tuple(jnp.where(even, got_even[i], got_odd[i]) for i in at)
        toward_next = add(add(cmul(weight, low), high), (emits[0][0][s], emits[0][1][s]))
        toward_prev = add(add(cmul(weight, high), low), (emits[1][0][s], emits[1][1][s]))
        for part in range(2):
            full[0, part, s] = toward_next[part]
            full[1, part, s] = toward_prev[part]
    fill_send(slots, full, passage)
    for side in range(2):
        first, second = (got_odd, got_even) if side == 0 else (got_even, got_odd)
        for i in range(2 * count):
            rows = pl.ds(i * DEEP, DEEP)
            near[side, i // count, i % count] = jnp.where(
                even, first[rows], second[rows]
            )
        for i in range(2):
            at = 2 * count * DEEP + i
            extra[side, i] = jnp.where(even, first[at], second[at])
    extra[0, 2] = extra[1, 2] = media_of(pack)[LAYER]


def prepare_kernel(start, send, given, made, rest):
    plan, near, extra, sources, guess = given
    res, near_media, waves = made
    (ref,) = rest
    _, count, slab, height, breadth = guess.shape
    tile = (height, breadth)
    masks = lane_masks(tile)
    place = lax.axis_index("depth")
    last_place = lax.axis_size("depth") - 1
    layer3 = extra[0, 2]
    layer = layer3 / damping
    factors = []
    for side in range(2):
        squared = extra[side, 1]
        inside = (place > 0) if side == 0 else (place < last_place)
        factors.append(
            set_media(near_media.at[side], squared, layer, extra[side, 0], slab, inside)
        )

    ws = list(factors)
    edge = DEEP - 1

    def keep_power(k, ws):
        for side in range(2):
            for way in range(2):
                if side == way:
                    i = k - (slab - edge + 1)
                    i = edge - 1 - i if side else i
                else:
                    i = k - 1
                    i = i if side else edge - 1 - i
                if 0 <= i < edge:
                    for part in range(2):
                        waves[side, way, i, part] = ws[side][part]

    def next_power(k, ws):
        return tuple(cmul(factors[side], ws[side]) for side in range(2))

    k = 1
    while k <= slab:
        if edge < k < slab - edge + 1:
            ws = loop(k, slab - edge + 1, next_power, tuple(ws), 8)
            k = slab - edge + 1
        keep_power(k, ws)
        ws = next_power(k, ws)
        k += 1
    for side in range(2):
        field = Field(ref, 0, height)
        field.clear()
        for i in range(DEEP + 1):
            for part in range(2):
                if side == 0:
                    value = near[0, part, :, i] if i < DEEP else guess[part, :, 0]
                else:
                    value = near[1, part, :, i - 1] if i > 0 else guess[part, :, slab - 1]
                field.put(part, i, value)
        lanes = Lanes(field, masks)
        for i in range(1, DEEP):
            r = field.minus_a(i, near_media[side, DIAGONAL], layer3, lanes.now)
            r = cmul(pair(near_media.at[side], INVERSE), r)
            for part in range(2):
                res[side, part, :, i - 1] = r[part]
    plan = plan.wait()
    for s in range(count):
        k = plan[s] - place * slab
        for side, low in ((0, -edge), (1, slab)):
            i = k - low

            @pl.when((i >= 0) & (i < edge))
            def _():
                src = sources[0, s], sources[1, s]
                src = cmul(pair(near_media.at[side], INVERSE), src)
                for part in range(2):
                    res[side, part, s, i] += src[part]


def chain_kernel(at, start, send, given, made, rest):
    got, passages, full = given
    mine, theirs = made
    place = lax.axis_index("depth")
    last_place = lax.axis_size("depth") - 1
    count = full.shape[2]
    even = lax.rem(place, 2) == 0
    low = place - lax.rem(place, 2)
    high = low + 1
    (a, b), (c, d) = halves(count)
    width = b - a
    zero = jnp.zeros((width,) + full.shape[3:], jnp.float32)
    passage = lambda j: (passages[j, at], passages[j, at + 1])
    emit = lambda way: tuple(
        jnp.where(even, full[way, part, a:b], full[way, part, c:d]) for part in range(2)
    )
    came = lambda j: (got[j, pl.ds(0, width)], got[j, pl.ds(width, width)])

    def step(j, state):
        return add(cmul(passage(j), state), came(j))

    below = jnp.maximum(low - 1, 0)
    above = jnp.minimum(high + 1, last_place)
    next_before = lax.fori_loop(0, below, step, (zero, zero))
    next_low = pick(low > 0, step(below, next_before), (zero, zero))
    next_high = add(cmul(passage(low), next_low), pick(even, emit(0), came(low)))
    prev_after = lax.fori_loop(
        0, last_place - above, lambda t, state: step(last_place - t, state), (zero, zero)
    )
    prev_high = pick(high < last_place, step(above, prev_after), (zero, zero))
    prev_low = add(cmul(passage(high), prev_high), pick(even, came(high), emit(1)))
    for_low = next_before, next_low, prev_low, prev_high
    for_high = next_low, next_high, prev_high, prev_after
    for i in range(4):
        own, other = pick(even, for_low[i], for_high[i]), pick(even, for_high[i], for_low[i])
        for part in range(2):
            mine[i, part] = own[part]
            theirs[i, part] = other[part]


def set_incoming(ref, mine, theirs, full, passage, media, near_media):
    inverses = [
        scale(coupling, pair(m, INVERSE))
        for m in (near_media.at[0], media, near_media.at[1])
    ]
    even = lax.rem(lax.axis_index("depth"), 2) == 0
    count = full.shape[2]
    spots = ((0, 0), (1, 0), (1, 1), (2, 1))
    for half, (a, b) in enumerate(halves(count)):
        own = even if half == 0 else jnp.logical_not(even)
        waves = [
            tuple(jnp.where(own, mine[i, part], theirs[i, part]) for part in range(2))
            for i in range(4)
        ]
        here = lambda way: (full[way, 0, a:b], full[way, 1, a:b])
        onward = add(cmul(passage, waves[1]), here(0))
        back = add(cmul(passage, waves[2]), here(1))
        for (side, way), value in zip(
            spots + ((2, 0), (0, 1)), [*waves, onward, back]
        ):
            ref[side, way, 0, a:b], ref[side, way, 1, a:b] = cmul(inverses[side], value)


class Stage:
    def __init__(self, below, own, above):
        self.below, self.own, self.above = below, own, above


def pipeline(stages, slab, carry, halfway):
    offsets = [LAG * (len(stages) - 1 - i) for i in range(len(stages))]
    trips = (slab - offsets[0]) // UNROLL

    def run(i, p, carry):
        out = stages[i].own(p, carry)
        return carry if out is None else out

    def own(i, start, stop, carry):
        body = lambda p, c: run(i, p, c)
        if start == 0 and stop > 0:
            carry = body(0, carry)
            start = 1
        if stop == slab and start < slab:
            return body(slab - 1, loop(start, slab - 1, body, carry))
        return loop(start, stop, body, carry)

    stages[0].below()
    stages[0].above()
    for i, stage in enumerate(stages):
        if i:
            stage.below()
        carry = own(i, 0, offsets[i], carry)

    def trip(t, carry):
        for i in reversed(range(len(stages))):
            for u in range(UNROLL):
                carry = run(i, t * UNROLL + offsets[i] + u, carry)
        return carry

    first = trips // 2
    carry = lax.fori_loop(0, first, trip, carry)
    halfway(0, [first * UNROLL + o for o in offsets])
    carry = lax.fori_loop(first, trips, trip, carry)
    halfway(1, [trips * UNROLL + o for o in offsets])
    for i, stage in enumerate(stages):
        carry = own(i, trips * UNROLL + offsets[i], slab, carry)
        if i:
            stage.above()
    return carry


def update_stages(
    reach, slab, tile, incoming, residual_of, media, near_media, power, waves,
    refs, emit, masks,
):
    edge = DEEP - 1
    first_update = Field(refs[0], -reach, tile[0])
    second_update = Field(refs[1], 1 - reach, tile[0])
    first_update.clear()
    second_update.clear()
    powers = (
        lambda p: (tile_of(waves, 0, 0, p + edge), tile_of(waves, 0, 1, p + edge)),
        lambda p: (tile_of(power, p + 1), tile_of(power, slab - p)),
        lambda p: (tile_of(waves, 1, 0, p - slab), tile_of(waves, 1, 1, p - slab)),
    )
    coefficients = near_media.at[0], media, near_media.at[1]
    first_lanes = Lanes(first_update, masks)
    second_lanes = Lanes(second_update, masks)

    def begin(which, p):
        on, off = powers[which](p)
        onward = incoming[which, 0, 0], incoming[which, 0, 1]
        back = incoming[which, 1, 0], incoming[which, 1, 1]
        c = add(cmul(on, onward), cmul(off, back))
        first_update.put_both(p, add(c, residual_of(which, p)))

    def second(which, p):
        here, total = first_update.around(p, first_lanes.now)
        smoothed = cmul(pair(coefficients[which], SECOND), total)
        second_update.put_both(p, add(here, smoothed))

    def third(which, p):
        here, total = second_update.around(p, second_lanes.now)
        smoothed = cmul(pair(coefficients[which], THIRD), total)
        u = add(scale(keep * (1.0 + keep), here), smoothed)
        emit(which, p, add(u, first_update.both(p)))

    def stage(body, margin):
        def beyond(which, a, b):
            for p in range(a, b):
                body(which, p)

        return Stage(
            lambda: beyond(0, margin - reach, 0),
            lambda p, unused: body(1, p),
            lambda: beyond(2, slab, slab + reach - margin),
        )

    return [stage(begin, 0), stage(second, 1), stage(third, 2)]


def middle_kernel(start, send, given, made, rest):
    (
        mine, theirs, plan, full, sources, pack, near_media, waves, near,
        near_residual, power, residual, guess,
    ) = given
    media = media_of(pack)
    new_field, new_residual, next_full, slots = made
    incoming, *refs = rest
    _, count, slab, height, breadth = guess.shape
    tile = (height, breadth)
    masks = lane_masks(tile)
    reach = DEEP - 1
    ext = reach - 2
    more = ext - 1
    new = Field(refs[2], -ext, height)
    new.clear()
    set_incoming(
        incoming, mine, theirs, full, tile_of(power, slab), media, near_media
    )

    def residual_of(which, p):
        if which == 1:
            r = residual[0, :, p], residual[1, :, p]
            lacks = None
            if isinstance(p, int) and p == 0:
                lacks = near[0, 0, :, DEEP - 1], near[0, 1, :, DEEP - 1]
            if isinstance(p, int) and p == slab - 1:
                lacks = near[1, 0, :, 0], near[1, 1, :, 0]
            return r if lacks is None else add(r, cmul(pair(media, INVERSE), lacks))
        i = p + reach if which == 0 else p - slab
        return near_residual[which // 2, 0, :, i], near_residual[which // 2, 1, :, i]

    def emit(which, p, u):
        for part in range(2):
            if which == 1:
                value = guess[part, :, p] + u[part]
                new_field[part, :, p] = value
            else:
                i = p + DEEP if which == 0 else p - slab
                value = near[which // 2, part, :, i] + u[part]
            new.put(part, p, value)

    stages = update_stages(
        reach, slab, tile, incoming, residual_of, media, near_media, power, waves,
        refs, emit, masks,
    )

    layer3 = media[LAYER]
    factor = pair(media, WAVE)
    lanes = Lanes(new, masks)

    def residual_at(p, diagonal):
        r = new.minus_a(p, diagonal, layer3, lanes.now)
        for part in range(2):
            new_residual[part, :, p + more] = r[part]
        return r

    def beyond(side, a, b):
        for p in range(a, b):
            residual_at(p, near_media[side, DIAGONAL])

    def inside(p, carry):
        toward_next, toward_prev = carry
        r = residual_at(p, media[DIAGONAL])
        toward_next = add(cmul(factor, toward_next), r)
        toward_prev = add(toward_prev, cmul(tile_of(power, p), r))
        return toward_next, toward_prev

    stages.append(
        Stage(lambda: beyond(0, -more, 0), inside, lambda: beyond(1, slab, slab + more))
    )
    zero = jnp.zeros((count,) + tile, jnp.float32)
    carry = pipeline(stages, slab, ((zero, zero), (zero, zero)), lambda i, reached: None)
    for way in range(2):
        for part in range(2):
            next_full[way, part] = carry[way][part]
    plan = plan.wait()
    force_emits(plan, next_full, sources, power, slab)
    fill_send(slots, next_full, None)
    add_forcing(plan, new_residual, sources, more, slab)


def scale_kernel(start, send, given, made, rest):
    residual, pack, near_media = given
    (out,) = made
    planes = residual.shape[2]
    reach = DEEP - 4

    def one(p, m):
        value = cmul(pair(m, INVERSE), (residual[0, :, p], residual[1, :, p]))
        out[0, :, p], out[1, :, p] = value

    media = media_of(pack)
    for p in range(reach):
        one(p, near_media.at[0])
        one(planes - 1 - p, near_media.at[1])
    loop(reach, planes - reach, lambda p, c: one(p, media) or c, 0, 8)


def final_kernel(start, send, given, made, rest):
    (
        mine, theirs, full, pack, near_media, waves, power, residual, field,
    ) = given
    (out,) = made
    media = media_of(pack)
    held, incoming, *refs = rest
    _, count, slab, height, breadth = field.shape
    tile = (height, breadth)
    reach = 2
    masks = lane_masks(tile)
    set_incoming(
        incoming, mine, theirs, full, tile_of(power, slab), media, near_media
    )

    def residual_of(which, p):
        return residual[0, :, p + reach], residual[1, :, p + reach]

    def emit(which, p, u):
        for part in range(2):
            held[part, :, p] = field[part, :, p] + u[part]

    stages = update_stages(
        reach, slab, tile, incoming, residual_of, media, near_media, power, waves,
        refs, emit, masks,
    )
    sent = [0]

    def send_field(top):
        part = pl.ds(sent[0], top - sent[0])
        send(held.at[:, :, part], out.at[:, :, part])
        sent[0] = top

    pipeline(stages, slab, 0, lambda i, reached: send_field(reached[2]))
    send_field(slab)


def local(sources, plan, absorb, labels, region_kk, damp_cells, guess):
    size = lax.axis_size("depth")
    _, count, slab, height, breadth = guess.shape
    tile = (height, breadth)
    edge = DEEP - 1
    planes = lambda n: (2, count, n) + tile
    scratch = lambda shape: pltpu.VMEM(shape, jnp.float32)

    tiles = (side_tiles(count) + 2,) + tile
    for_odd, base = kernel_call(
        pack_kernel,
        [
            (region_kk, "smem"), (damp_cells, "smem"), (absorb, "vmem"),
            (labels, "vmem"), (guess, "hbm"),
        ],
        [(tiles, "direct"), ((MEDIA + 2,) + tile, "direct")],
        pieces=2 * count, cost=1_000_000, name="pack", limit=4,
    )
    even_pairs = [(i, i ^ 1) for i in range(size)]
    odd_pairs = [(i, i + 1) for i in range(1, size - 1, 2)]
    odd_pairs += [(b, a) for a, b in odd_pairs]
    got_odd = lax.ppermute(for_odd, "depth", odd_pairs)

    residual, pack, power, for_even = kernel_call(
        start_kernel,
        [
            (plan, "smem"), (sources, "vmem"), (base, "direct"), (guess, "direct"),
        ],
        [
            (planes(slab), "direct"), ((MEDIA + 4 + 4 * count,) + tile, "direct"),
            ((slab + 1, 2) + tile, "direct"), (tiles, "direct"),
        ],
        [
            scratch((2, 2, count) + tile), Field.shape(count, slab + 2, tile),
        ],
        cost=20_000_000, name="start", limit=12,
    )
    got_even = lax.ppermute(for_even, "depth", even_pairs)
    width = count // 2
    full, slots, near, extra = kernel_call(
        arrange_kernel,
        [(got_even, "direct"), (got_odd, "direct"), (pack, "direct")],
        [
            ((2, 2, count) + tile, "direct"), ((size, 2 * width + 2) + tile, "direct"),
            ((2, 2, count, DEEP) + tile, "direct"), ((2, 3) + tile, "direct"),
        ],
        cost=1_000_000, name="arrange", limit=4,
    )
    first_got = lax.all_to_all(slots, "depth", 0, 0)
    near_residual, near_media, waves = kernel_call(
        prepare_kernel,
        [
            (plan, "smem"), (near, "direct"), (extra, "direct"),
            (sources, "direct"), (guess, "direct"),
        ],
        [
            ((2, 2, count, edge) + tile, "direct"), ((2, MEDIA) + tile, "direct"),
            ((2, 2, edge, 2) + tile, "direct"),
        ],
        [Field.shape(count, DEEP + 1, tile)],
        cost=4_000_000, name="prepare", limit=4,
    )

    def chain(got, full):
        mine, theirs = kernel_call(
            functools.partial(chain_kernel, 2 * width),
            [(got, "direct"), (first_got, "direct"), (full, "direct")],
            [((4, 2, width) + tile, "direct")] * 2,
            cost=1_000_000, name="chain", limit=4,
        )
        return mine, lax.ppermute(theirs, "depth", even_pairs)

    mine, theirs = chain(first_got, full)
    new_field, new_residual, next_full, slots = kernel_call(
        middle_kernel,
        [
            (mine, "direct"), (theirs, "direct"),
            (plan, "smem"), (full, "direct"), (sources, "direct"),
            (pack, "direct"), (near_media, "direct"), (waves, "direct"),
            (near, "direct"), (near_residual, "direct"), (power, "direct"),
            (residual, "direct"), (guess, "direct"),
        ],
        [
            (planes(slab), "direct"), (planes(slab + 2 * (DEEP - 4)), "direct"),
            ((2, 2, count) + tile, "direct"), ((size, 2 * width) + tile, "direct"),
        ],
        [
            scratch((3, 2, 2, count) + tile),
            Field.shape(count, slab + 2 * edge, tile),
            Field.shape(count, slab + 2 * edge - 2, tile),
            Field.shape(count, slab + 2 * edge - 4, tile),
        ],
        cost=80_000_000, name="middle", limit=20,
    )
    mine, theirs = chain(lax.all_to_all(slots, "depth", 0, 0), next_full)
    (scaled,) = kernel_call(
        scale_kernel,
        [(new_residual, "direct"), (pack, "direct"), (near_media, "direct")],
        [(planes(slab + 2 * (DEEP - 4)), "direct")],
        cost=4_000_000, name="scale", limit=4,
    )
    (out,) = kernel_call(
        final_kernel,
        [
            (mine, "direct"), (theirs, "direct"), (next_full, "direct"),
            (pack, "direct"), (near_media, "direct"), (waves, "direct"),
            (power, "direct"), (scaled, "direct"), (new_field, "direct"),
        ],
        [(planes(slab), "hbm")],
        [
            scratch(planes(slab)), scratch((3, 2, 2, count) + tile),
            Field.shape(count, slab + 4, tile), Field.shape(count, slab + 2, tile),
        ],
        pieces=3, cost=60_000_000, name="final", limit=16,
    )
    return out


def solution(mesh):
    return jax.shard_map(
        local,
        mesh=mesh,
        in_specs=(
            P(None, "groups", None, None),
            P("groups"),
            P("depth", "groups", None),
            P("depth", "groups", None),
            P(),
            P("groups"),
            P(None, "groups", "depth", None, None),
        ),
        out_specs=P(None, "groups", "depth", None, None),
        check_vma=False,
    )
```

```python
import functools

import jax
import jax.numpy as jnp
from jax import lax
from jax.experimental import pallas as pl
from jax.experimental.pallas import tpu as pltpu
from jax.sharding import PartitionSpec as P

relax_weight = 0.8
shift_ratio = 0.5
damping = 3.0
coupling = 0.25
keep = 1.0 - relax_weight

DEEP = 6
UNROLL = 4
LAG = UNROLL + 1


def cmul(a, b):
    return a[0] * b[0] - a[1] * b[1], a[0] * b[1] + a[1] * b[0]


def add(a, b):
    return a[0] + b[0], a[1] + b[1]


def scale(c, a):
    return c * a[0], c * a[1]


def pick(cond, a, b):
    return jnp.where(cond, a[0], b[0]), jnp.where(cond, a[1], b[1])


def tile_of(ref, *at):
    return ref[at + (0,)], ref[at + (1,)]


class Inward:
    def __init__(self, source, target, sem):
        self.ref = target
        self.copy = pltpu.make_async_copy(source, target, sem)
        self.copy.start()

    def wait(self):
        self.copy.wait()
        return self.ref


def kernel_call(body, inputs, outputs, scratch=(), pieces=0, cost=0, name=None, limit=56):
    n_in, n_out = len(inputs), len(outputs)
    pinned = ("hbm", "vmem", "smem")
    extra = []
    for array, place in inputs:
        if place in ("vmem", "smem"):
            space = pltpu.SMEM if place == "smem" else pltpu.VMEM
            extra.append(space(array.shape, array.dtype))
    for shape, place in outputs:
        if place == "vmem":
            extra.append(pltpu.VMEM(shape, jnp.float32))
    n_extra = len(extra)

    def kernel(*refs):
        ins, outs = refs[:n_in], refs[n_in : n_in + n_out]
        buffers = iter(refs[n_in + n_out : n_in + n_out + n_extra])
        sems = refs[n_in + n_out + n_extra]
        rest = refs[n_in + n_out + n_extra + 1 :]
        used = iter(range(n_extra + pieces))
        pending = []

        def start(source, target):
            return Inward(source, target, sems.at[next(used)])

        def send(source, target):
            pending.append(start(source, target))

        def arrive():
            given = []
            for ref, (_, place) in zip(ins, inputs):
                copied = place in ("vmem", "smem")
                given.append(start(ref, next(buffers)) if copied else ref)
            return given

        given = arrive()
        made = []
        for ref, (_, place) in zip(outs, outputs):
            if place != "vmem":
                made.append(ref)
            else:
                buffer = next(buffers)
                made.append((buffer, functools.partial(send, buffer, ref)))
        body(start, send, given, made, rest)
        for copy in pending:
            copy.wait()

    def spec(place):
        return pl.BlockSpec(memory_space=pltpu.VMEM if place == "direct" else pltpu.HBM)

    return pl.pallas_call(
        kernel,
        out_shape=tuple(jax.ShapeDtypeStruct(s, jnp.float32) for s, _ in outputs),
        in_specs=[spec(place) for _, place in inputs],
        out_specs=tuple(spec(place) for _, place in outputs),
        scratch_shapes=[
            *extra,
            pltpu.SemaphoreType.DMA((max(1, n_extra + pieces),)),
            *scratch,
        ],
        compiler_params=pltpu.CompilerParams(vmem_limit_bytes=limit << 20),
        cost_estimate=pl.CostEstimate(
            flops=cost, bytes_accessed=4 << 20, transcendentals=0
        ),
        name=name,
    )(*[
        pltpu.with_memory_space_constraint(array, pltpu.HBM) if place in pinned else array
        for array, place in inputs
    ])


def lane_sum(here, masks):
    breadth = here.shape[-1]
    axis = here.ndim - 1
    ahead = jnp.where(masks[0], pltpu.roll(here, 1, axis), 0.0)
    behind = jnp.where(masks[1], pltpu.roll(here, breadth - 1, axis), 0.0)
    return ahead + behind


class Field:
    def __init__(self, ref, first, height):
        self.ref, self.first, self.height = ref, first, height

    @staticmethod
    def shape(count, planes, tile):
        return pltpu.VMEM((2, count, (2 * planes + 1) * tile[0], tile[1]), jnp.float32)

    def rows(self, plane, shift=0):
        start = (2 * (plane - self.first) + 1) * self.height + shift
        if shift % self.height == 0:
            start = pl.multiple_of(start, self.height)
        return pl.ds(start, self.height)

    def clear(self):
        edge = self.ref[:, :, : self.height]
        self.ref[:, :, : self.height] = jnp.zeros_like(edge)

    def get(self, part, plane, shift=0):
        return self.ref[part, :, self.rows(plane, shift)]

    def both(self, plane):
        return self.get(0, plane), self.get(1, plane)

    def put(self, part, plane, value):
        self.ref[part, :, self.rows(plane)] = value
        self.ref[part, :, self.rows(plane, self.height)] = jnp.zeros_like(value)

    def put_both(self, plane, value):
        for part in range(2):
            self.put(part, plane, value[part])

    def bump(self, plane, s, value):
        for part in range(2):
            self.ref[part, s, self.rows(plane)] += value[part]

    def lanes(self, part, plane, masks):
        return lane_sum(self.get(part, plane), masks)

    def around(self, plane, lanes):
        heres, totals = [], []
        for part in range(2):
            here = self.get(part, plane)
            beside = self.get(part, plane, -1) + self.get(part, plane, 1)
            depth = self.get(part, plane - 1) + self.get(part, plane + 1)
            heres.append(here)
            totals.append((beside + depth) + lanes(part, plane))
        return tuple(heres), tuple(totals)

    def minus_a(self, plane, diagonal, layer3, lanes):
        here, total = self.around(plane, lanes)
        return (
            (total[0] - diagonal * here[0]) + layer3 * here[1],
            (total[1] - diagonal * here[1]) - layer3 * here[0],
        )


class Lanes:
    def __init__(self, field, masks):
        self.field, self.masks = field, masks

    def now(self, part, plane):
        return self.field.lanes(part, plane, self.masks)


def lane_masks(tile):
    lane = lax.broadcasted_iota(jnp.int32, tile, 1)
    return lane > 0, lane < tile[1] - 1


INVERSE, DIAGONAL, LAYER, WAVE, SECOND, THIRD, MEDIA = 0, 2, 3, 4, 6, 8, 10


def set_media(ref, squared, layer, absorb, slab, inside=None):
    diagonal = 6.0 - squared
    imag = shift_ratio * squared + damping * layer
    size = diagonal * diagonal + imag * imag
    inverse = relax_weight * diagonal / size, -relax_weight * imag / size
    if inside is not None:
        inverse = tuple(jnp.where(inside, v, 0.0) for v in inverse)
    grow = 1.0 + keep
    decay = jnp.exp(-absorb / slab)
    angle = jnp.sqrt(squared)
    factor = decay * jnp.cos(angle), decay * jnp.sin(angle)
    values = (
        *inverse, diagonal, damping * layer, *factor,
        *scale(1.0 / grow, inverse), *scale(grow, inverse),
    )
    for i, value in enumerate(values):
        ref[i] = value
    return factor


def pair(ref, i):
    return ref[i], ref[i + 1]


def region_values(labels, kk_ref):
    squared = jnp.zeros(labels.shape, jnp.float32)
    for region in range(kk_ref.shape[0]):
        squared = jnp.where(labels == region, kk_ref[region], squared)
    return squared


def loop(start, stop, body, carry, unroll=UNROLL):
    trips = (stop - start) // unroll

    def several(trip, carry):
        for i in range(unroll):
            carry = body(start + trip * unroll + i, carry)
        return carry

    if trips > 1:
        carry = lax.fori_loop(0, trips, several, carry)
        start += trips * unroll
    for plane in range(start, stop):
        carry = body(plane, carry)
    return carry


def media_of(pack):
    return pack.at[pl.ds(0, MEDIA)]


def emit_tiles(count, way, part):
    return pl.ds(MEDIA + 4 + (2 * way + part) * count, count)


def side_tiles(count):
    return 2 * count * DEEP


def pack_kernel(start, send, given, made, rest):
    kk, damp, absorb, labels, guess = given
    out, base = made
    _, count, slab, *tile = guess.shape
    even = lax.rem(lax.axis_index("depth"), 2) == 0
    first = jnp.where(even, 0, slab - DEEP)
    for i in range(2 * count):
        send(
            guess.at[i // count, i % count, pl.ds(first, DEEP)],
            out.at[pl.ds(i * DEEP, DEEP)],
        )
    row = lax.broadcasted_iota(jnp.int32, tuple(tile), 0)
    lane = lax.broadcasted_iota(jnp.int32, tuple(tile), 1)
    cell = row * tile[1] + lane
    kk, absorb, labels = kk.wait(), absorb.wait(), labels.wait()
    squared = region_values(labels[0], kk)
    out[side_tiles(count)] = absorb[0]
    out[side_tiles(count) + 1] = squared
    base[MEDIA] = absorb[0]
    base[MEDIA + 1] = squared
    damp = damp.wait()

    def mark(i, hit):
        return jnp.where(cell == damp[i], 1.0, hit)

    layer = loop(0, damp.shape[0], mark, jnp.zeros(tile, jnp.float32), 16)
    set_media(base, squared, layer, absorb[0], slab)


def start_kernel(start, send, given, made, rest):
    plan, sources, base, guess = given
    residual, pack, power, for_even = made
    emits, ref = rest
    _, count, slab, height, breadth = guess.shape
    tile = (height, breadth)
    media = media_of(pack)
    media[...] = base[:MEDIA]
    masks = lane_masks(tile)
    field = Field(ref, -1, height)
    zero = jnp.zeros((count,) + tile, jnp.float32)
    field.clear()
    field.put_both(-1, (zero, zero))
    field.put_both(slab, (zero, zero))
    lanes = Lanes(field, masks)
    diagonal, layer3 = media[DIAGONAL], media[LAYER]
    inverse, factor = pair(media, INVERSE), pair(media, WAVE)

    def fill(p):
        for part in range(2):
            field.put(part, p, guess[part, :, p])

    def plane(k, carry):
        toward_next, toward_prev, w = carry
        power[k, 0], power[k, 1] = w
        r = field.minus_a(k, diagonal, layer3, lanes.now)
        residual[0, :, k], residual[1, :, k] = cmul(inverse, r)
        toward_next = add(cmul(factor, toward_next), r)
        toward_prev = add(toward_prev, cmul(w, r))
        return toward_next, toward_prev, cmul(factor, w)

    one = jnp.ones(tile, jnp.float32), jnp.zeros(tile, jnp.float32)
    carry = ((zero, zero), (zero, zero), one)
    fill(0)

    def group(trip, carry):
        base = trip * UNROLL
        for i in range(UNROLL):
            fill(base + i + 1)
        for i in range(UNROLL):
            carry = plane(base + i, carry)
        return carry

    trips = (slab - 1) // UNROLL
    carry = lax.fori_loop(0, trips, group, carry)
    for k in range(trips * UNROLL, slab):
        if k + 1 < slab:
            fill(k + 1)
        carry = plane(k, carry)
    plan, sources = plan.wait(), sources.wait()
    toward_next, toward_prev, w = carry
    power[slab, 0], power[slab, 1] = w
    add_forcing(plan, residual, sources, 0, slab, inverse)
    for part in range(2):
        emits[0, part] = toward_next[part]
        emits[1, part] = toward_prev[part]
        pack[MEDIA + part] = power[slab - 1, part]
        pack[MEDIA + 2 + part] = power[slab, part]
    force_emits(plan, emits, sources, power, slab)
    for way in range(2):
        for part in range(2):
            pack[emit_tiles(count, way, part)] = emits[way, part]
    first_plane = jnp.where(lax.rem(lax.axis_index("depth"), 2) == 0, slab - DEEP, 0)
    for i in range(2 * count):
        for_even[pl.ds(i * DEEP, DEEP)] = guess[
            i // count, i % count, pl.ds(first_plane, DEEP)
        ]
    for_even[pl.ds(side_tiles(count), 2)] = base[MEDIA : MEDIA + 2]


def add_forcing(plan, held, sources, reach, slab, inverse=None):
    first_plane = lax.axis_index("depth") * slab
    for s in range(sources.shape[1]):
        k = plan[s] - first_plane

        @pl.when((k >= -reach) & (k < slab + reach))
        def _():
            src = sources[0, s], sources[1, s]
            if inverse is not None:
                src = cmul(inverse, src)
            for part in range(2):
                held[part, s, k + reach] += src[part]


def force_emits(plan, emits, sources, power, slab):
    first_plane = lax.axis_index("depth") * slab
    for s in range(sources.shape[1]):
        k = plan[s] - first_plane

        @pl.when((k >= 0) & (k < slab))
        def _():
            src = sources[0, s], sources[1, s]
            onward = cmul(tile_of(power, slab - 1 - k), src)
            back = cmul(tile_of(power, k), src)
            for part in range(2):
                emits[0, part, s] += onward[part]
                emits[1, part, s] += back[part]


class Split:
    def __init__(self, tile):
        self.half = tile[0] // 2
        self.upper = lax.broadcasted_iota(jnp.int32, tile, 0) < self.half

    def turn(self, value):
        return pltpu.roll(value, self.half, value.ndim - 2)

    def pack(self, core, first, second):
        if core == 0:
            return jnp.where(self.upper, first, self.turn(second))
        return jnp.where(self.upper, self.turn(first), second)

    def unpack(self, core_0, core_1):
        first = jnp.where(self.upper, core_0, self.turn(core_1))
        second = jnp.where(self.upper, self.turn(core_0), core_1)
        return first, second

    def spread(self, packed):
        turned = self.turn(packed)
        return jnp.where(self.upper, packed, turned), jnp.where(self.upper, turned, packed)


def pack_waves(split, core, full, way):
    count = full.shape[2]
    return tuple(
        jnp.stack(
            [
                split.pack(core, full[way, part, s], full[way, part, s + 1])
                for s in range(0, count, 2)
            ]
        )
        for part in range(2)
    )


def fill_send(slots, full, passage):
    place = lax.axis_index("depth")
    width = full.shape[2] // 2
    split = Split(full.shape[3:])
    waves = [[pack_waves(split, core, full, way) for way in range(2)] for core in range(2)]

    def one(chip, unused):
        for core in range(2):
            j = 2 * chip + core
            onward, back = waves[core]
            for part in range(2):
                slots[j, pl.ds(part * width, width)] = jnp.where(
                    j > place, onward[part], back[part]
                )
            if passage is not None:
                slots[j, 2 * width] = split.pack(core, *passage)
        return unused

    loop(0, slots.shape[0] // 2, one, 0, 4)


def arrange_kernel(start, send, given, made, rest):
    got_even, got_odd, pack = given
    full, slots, near, extra = made
    even = lax.rem(lax.axis_index("depth"), 2) == 0
    count = full.shape[2]
    weight, passage = pair(pack, MEDIA), pair(pack, MEDIA + 2)
    emits = [[pack[emit_tiles(count, way, part)] for part in range(2)] for way in range(2)]
    for s in range(count):
        at = [(part * count + s) * DEEP for part in range(2)]
        low = tuple(
            jnp.where(even, got_odd[i + DEEP - 1], got_even[i + DEEP - 1]) for i in at
        )
        high = tuple(jnp.where(even, got_even[i], got_odd[i]) for i in at)
        toward_next = add(add(cmul(weight, low), high), (emits[0][0][s], emits[0][1][s]))
        toward_prev = add(add(cmul(weight, high), low), (emits[1][0][s], emits[1][1][s]))
        for part in range(2):
            full[0, part, s] = toward_next[part]
            full[1, part, s] = toward_prev[part]
    fill_send(slots, full, passage)
    for side in range(2):
        first, second = (got_odd, got_even) if side == 0 else (got_even, got_odd)
        for i in range(2 * count):
            rows = pl.ds(i * DEEP, DEEP)
            near[side, i // count, i % count] = jnp.where(
                even, first[rows], second[rows]
            )
        for i in range(2):
            at = 2 * count * DEEP + i
            extra[side, i] = jnp.where(even, first[at], second[at])
    extra[0, 2] = extra[1, 2] = media_of(pack)[LAYER]


def prepare_kernel(start, send, given, made, rest):
    plan, near, extra, sources, guess = given
    res, near_media, waves = made
    (ref,) = rest
    _, count, slab, height, breadth = guess.shape
    tile = (height, breadth)
    masks = lane_masks(tile)
    place = lax.axis_index("depth")
    last_place = lax.axis_size("depth") - 1
    layer3 = extra[0, 2]
    layer = layer3 / damping
    factors = []
    for side in range(2):
        squared = extra[side, 1]
        inside = (place > 0) if side == 0 else (place < last_place)
        factors.append(
            set_media(near_media.at[side], squared, layer, extra[side, 0], slab, inside)
        )

    ws = list(factors)
    edge = DEEP - 1

    def keep_power(k, ws):
        for side in range(2):
            for way in range(2):
                if side == way:
                    i = k - (slab - edge + 1)
                    i = edge - 1 - i if side else i
                else:
                    i = k - 1
                    i = i if side else edge - 1 - i
                if 0 <= i < edge:
                    for part in range(2):
                        waves[side, way, i, part] = ws[side][part]

    def next_power(k, ws):
        return tuple(cmul(factors[side], ws[side]) for side in range(2))

    k = 1
    while k <= slab:
        if edge < k < slab - edge + 1:
            ws = loop(k, slab - edge + 1, next_power, tuple(ws), 8)
            k = slab - edge + 1
        keep_power(k, ws)
        ws = next_power(k, ws)
        k += 1
    for side in range(2):
        field = Field(ref, 0, height)
        field.clear()
        for i in range(DEEP + 1):
            for part in range(2):
                if side == 0:
                    value = near[0, part, :, i] if i < DEEP else guess[part, :, 0]
                else:
                    value = near[1, part, :, i - 1] if i > 0 else guess[part, :, slab - 1]
                field.put(part, i, value)
        lanes = Lanes(field, masks)
        for i in range(1, DEEP):
            r = field.minus_a(i, near_media[side, DIAGONAL], layer3, lanes.now)
            r = cmul(pair(near_media.at[side], INVERSE), r)
            for part in range(2):
                res[side, part, :, i - 1] = r[part]
    plan = plan.wait()
    for s in range(count):
        k = plan[s] - place * slab
        for side, low in ((0, -edge), (1, slab)):
            i = k - low

            @pl.when((i >= 0) & (i < edge))
            def _():
                src = sources[0, s], sources[1, s]
                src = cmul(pair(near_media.at[side], INVERSE), src)
                for part in range(2):
                    res[side, part, s, i] += src[part]


def chain_kernel(start, send, given, made, rest):
    got, passages, full = given
    mine, theirs = made
    place = lax.axis_index("depth")
    last_place = lax.axis_size("depth") - 1
    width = full.shape[2] // 2
    split = Split(full.shape[3:])
    even = lax.rem(place, 2) == 0
    low = place - lax.rem(place, 2)
    high = low + 1
    zero = jnp.zeros((width,) + full.shape[3:], jnp.float32)
    passage = lambda j: split.spread(passages[j, 2 * width])
    emit = lambda way: pick(
        even, pack_waves(split, 0, full, way), pack_waves(split, 1, full, way)
    )
    came = lambda j: (got[j, pl.ds(0, width)], got[j, pl.ds(width, width)])

    def step(j, state):
        return add(cmul(passage(j), state), came(j))

    below = jnp.maximum(low - 1, 0)
    above = jnp.minimum(high + 1, last_place)
    next_before = lax.fori_loop(0, below, step, (zero, zero))
    next_low = pick(low > 0, step(below, next_before), (zero, zero))
    next_high = add(cmul(passage(low), next_low), pick(even, emit(0), came(low)))
    prev_after = lax.fori_loop(
        0, last_place - above, lambda t, state: step(last_place - t, state), (zero, zero)
    )
    prev_high = pick(high < last_place, step(above, prev_after), (zero, zero))
    prev_low = add(cmul(passage(high), prev_high), pick(even, came(high), emit(1)))
    for_low = next_before, next_low, prev_low, prev_high
    for_high = next_low, next_high, prev_high, prev_after
    for i in range(4):
        own, other = pick(even, for_low[i], for_high[i]), pick(even, for_high[i], for_low[i])
        for part in range(2):
            mine[i, part] = own[part]
            theirs[i, part] = other[part]


def set_incoming(ref, mine, theirs, full, passage, media, near_media):
    inverses = [
        scale(coupling, pair(m, INVERSE))
        for m in (near_media.at[0], media, near_media.at[1])
    ]
    even = lax.rem(lax.axis_index("depth"), 2) == 0
    count = full.shape[2]
    split = Split(full.shape[3:])
    waves = []
    for i in range(4):
        parts = []
        for part in range(2):
            own, other = mine[i, part], theirs[i, part]
            first, second = split.unpack(
                jnp.where(even, own, other), jnp.where(even, other, own)
            )
            parts.append(jnp.stack([first, second], 1).reshape(full.shape[2:]))
        waves.append(tuple(parts))
    onward = add(cmul(passage, waves[1]), (full[0, 0], full[0, 1]))
    back = add(cmul(passage, waves[2]), (full[1, 0], full[1, 1]))
    spots = ((0, 0), (1, 0), (1, 1), (2, 1), (2, 0), (0, 1))
    for (side, way), value in zip(spots, [*waves, onward, back]):
        ref[side, way, 0], ref[side, way, 1] = cmul(inverses[side], value)


class Stage:
    def __init__(self, below, own, above):
        self.below, self.own, self.above = below, own, above


def pipeline(stages, slab, carry, halfway):
    offsets = [LAG * (len(stages) - 1 - i) for i in range(len(stages))]
    trips = (slab - offsets[0]) // UNROLL

    def run(i, p, carry):
        out = stages[i].own(p, carry)
        return carry if out is None else out

    def own(i, start, stop, carry):
        body = lambda p, c: run(i, p, c)
        if start == 0 and stop > 0:
            carry = body(0, carry)
            start = 1
        if stop == slab and start < slab:
            return body(slab - 1, loop(start, slab - 1, body, carry))
        return loop(start, stop, body, carry)

    stages[0].below()
    stages[0].above()
    for i, stage in enumerate(stages):
        if i:
            stage.below()
        carry = own(i, 0, offsets[i], carry)

    def trip(t, carry):
        for i in reversed(range(len(stages))):
            for u in range(UNROLL):
                carry = run(i, t * UNROLL + offsets[i] + u, carry)
        return carry

    first = trips // 2
    carry = lax.fori_loop(0, first, trip, carry)
    halfway(0, [first * UNROLL + o for o in offsets])
    carry = lax.fori_loop(first, trips, trip, carry)
    halfway(1, [trips * UNROLL + o for o in offsets])
    for i, stage in enumerate(stages):
        carry = own(i, trips * UNROLL + offsets[i], slab, carry)
        if i:
            stage.above()
    return carry


def update_stages(
    reach, slab, tile, incoming, residual_of, media, near_media, power, waves,
    refs, emit, masks,
):
    edge = DEEP - 1
    first_update = Field(refs[0], -reach, tile[0])
    second_update = Field(refs[1], 1 - reach, tile[0])
    first_update.clear()
    second_update.clear()
    powers = (
        lambda p: (tile_of(waves, 0, 0, p + edge), tile_of(waves, 0, 1, p + edge)),
        lambda p: (tile_of(power, p + 1), tile_of(power, slab - p)),
        lambda p: (tile_of(waves, 1, 0, p - slab), tile_of(waves, 1, 1, p - slab)),
    )
    coefficients = near_media.at[0], media, near_media.at[1]
    first_lanes = Lanes(first_update, masks)
    second_lanes = Lanes(second_update, masks)

    def begin(which, p):
        on, off = powers[which](p)
        onward = incoming[which, 0, 0], incoming[which, 0, 1]
        back = incoming[which, 1, 0], incoming[which, 1, 1]
        c = add(cmul(on, onward), cmul(off, back))
        first_update.put_both(p, add(c, residual_of(which, p)))

    def second(which, p):
        here, total = first_update.around(p, first_lanes.now)
        smoothed = cmul(pair(coefficients[which], SECOND), total)
        second_update.put_both(p, add(here, smoothed))

    def third(which, p):
        here, total = second_update.around(p, second_lanes.now)
        smoothed = cmul(pair(coefficients[which], THIRD), total)
        u = add(scale(keep * (1.0 + keep), here), smoothed)
        emit(which, p, add(u, first_update.both(p)))

    def stage(body, margin):
        def beyond(which, a, b):
            for p in range(a, b):
                body(which, p)

        return Stage(
            lambda: beyond(0, margin - reach, 0),
            lambda p, unused: body(1, p),
            lambda: beyond(2, slab, slab + reach - margin),
        )

    return [stage(begin, 0), stage(second, 1), stage(third, 2)]


def middle_kernel(start, send, given, made, rest):
    (
        mine, theirs, plan, full, sources, pack, near_media, waves, near,
        near_residual, power, residual, guess,
    ) = given
    media = media_of(pack)
    new_field, new_residual, next_full, slots = made
    incoming, *refs = rest
    _, count, slab, height, breadth = guess.shape
    tile = (height, breadth)
    masks = lane_masks(tile)
    reach = DEEP - 1
    ext = reach - 2
    more = ext - 1
    new = Field(refs[2], -ext, height)
    new.clear()
    set_incoming(
        incoming, mine, theirs, full, tile_of(power, slab), media, near_media
    )

    def residual_of(which, p):
        if which == 1:
            r = residual[0, :, p], residual[1, :, p]
            lacks = None
            if isinstance(p, int) and p == 0:
                lacks = near[0, 0, :, DEEP - 1], near[0, 1, :, DEEP - 1]
            if isinstance(p, int) and p == slab - 1:
                lacks = near[1, 0, :, 0], near[1, 1, :, 0]
            return r if lacks is None else add(r, cmul(pair(media, INVERSE), lacks))
        i = p + reach if which == 0 else p - slab
        return near_residual[which // 2, 0, :, i], near_residual[which // 2, 1, :, i]

    def emit(which, p, u):
        for part in range(2):
            if which == 1:
                value = guess[part, :, p] + u[part]
                new_field[part, :, p] = value
            else:
                i = p + DEEP if which == 0 else p - slab
                value = near[which // 2, part, :, i] + u[part]
            new.put(part, p, value)

    stages = update_stages(
        reach, slab, tile, incoming, residual_of, media, near_media, power, waves,
        refs, emit, masks,
    )

    layer3 = media[LAYER]
    factor = pair(media, WAVE)
    lanes = Lanes(new, masks)

    def residual_at(p, diagonal):
        r = new.minus_a(p, diagonal, layer3, lanes.now)
        for part in range(2):
            new_residual[part, :, p + more] = r[part]
        return r

    def beyond(side, a, b):
        for p in range(a, b):
            residual_at(p, near_media[side, DIAGONAL])

    def inside(p, carry):
        toward_next, toward_prev = carry
        r = residual_at(p, media[DIAGONAL])
        toward_next = add(cmul(factor, toward_next), r)
        toward_prev = add(toward_prev, cmul(tile_of(power, p), r))
        return toward_next, toward_prev

    stages.append(
        Stage(lambda: beyond(0, -more, 0), inside, lambda: beyond(1, slab, slab + more))
    )
    zero = jnp.zeros((count,) + tile, jnp.float32)
    carry = pipeline(stages, slab, ((zero, zero), (zero, zero)), lambda i, reached: None)
    for way in range(2):
        for part in range(2):
            next_full[way, part] = carry[way][part]
    plan = plan.wait()
    force_emits(plan, next_full, sources, power, slab)
    fill_send(slots, next_full, None)
    add_forcing(plan, new_residual, sources, more, slab)


def scale_kernel(start, send, given, made, rest):
    residual, pack, near_media = given
    (out,) = made
    planes = residual.shape[2]
    reach = DEEP - 4

    def one(p, m):
        value = cmul(pair(m, INVERSE), (residual[0, :, p], residual[1, :, p]))
        out[0, :, p], out[1, :, p] = value

    media = media_of(pack)
    for p in range(reach):
        one(p, near_media.at[0])
        one(planes - 1 - p, near_media.at[1])
    loop(reach, planes - reach, lambda p, c: one(p, media) or c, 0, 8)


def final_kernel(start, send, given, made, rest):
    (
        mine, theirs, full, pack, near_media, waves, power, residual, field,
    ) = given
    (out,) = made
    media = media_of(pack)
    held, incoming, *refs = rest
    _, count, slab, height, breadth = field.shape
    tile = (height, breadth)
    reach = 2
    masks = lane_masks(tile)
    set_incoming(
        incoming, mine, theirs, full, tile_of(power, slab), media, near_media
    )

    def residual_of(which, p):
        return residual[0, :, p + reach], residual[1, :, p + reach]

    def emit(which, p, u):
        for part in range(2):
            held[part, :, p] = field[part, :, p] + u[part]

    stages = update_stages(
        reach, slab, tile, incoming, residual_of, media, near_media, power, waves,
        refs, emit, masks,
    )
    sent = [0]

    def send_field(top):
        part = pl.ds(sent[0], top - sent[0])
        send(held.at[:, :, part], out.at[:, :, part])
        sent[0] = top

    pipeline(stages, slab, 0, lambda i, reached: send_field(reached[2]))
    send_field(slab)


def local(sources, plan, absorb, labels, region_kk, damp_cells, guess):
    size = lax.axis_size("depth")
    _, count, slab, height, breadth = guess.shape
    tile = (height, breadth)
    edge = DEEP - 1
    planes = lambda n: (2, count, n) + tile
    scratch = lambda shape: pltpu.VMEM(shape, jnp.float32)

    tiles = (side_tiles(count) + 2,) + tile
    for_odd, base = kernel_call(
        pack_kernel,
        [
            (region_kk, "smem"), (damp_cells, "smem"), (absorb, "vmem"),
            (labels, "vmem"), (guess, "hbm"),
        ],
        [(tiles, "direct"), ((MEDIA + 2,) + tile, "direct")],
        pieces=2 * count, cost=1_000_000, name="pack", limit=4,
    )
    even_pairs = [(i, i ^ 1) for i in range(size)]
    odd_pairs = [(i, i + 1) for i in range(1, size - 1, 2)]
    odd_pairs += [(b, a) for a, b in odd_pairs]
    got_odd = lax.ppermute(for_odd, "depth", odd_pairs)

    residual, pack, power, for_even = kernel_call(
        start_kernel,
        [
            (plan, "smem"), (sources, "vmem"), (base, "direct"), (guess, "direct"),
        ],
        [
            (planes(slab), "direct"), ((MEDIA + 4 + 4 * count,) + tile, "direct"),
            ((slab + 1, 2) + tile, "direct"), (tiles, "direct"),
        ],
        [
            scratch((2, 2, count) + tile), Field.shape(count, slab + 2, tile),
        ],
        cost=20_000_000, name="start", limit=12,
    )
    got_even = lax.ppermute(for_even, "depth", even_pairs)
    width = count // 2
    full, slots, near, extra = kernel_call(
        arrange_kernel,
        [(got_even, "direct"), (got_odd, "direct"), (pack, "direct")],
        [
            ((2, 2, count) + tile, "direct"), ((size, 2 * width + 1) + tile, "direct"),
            ((2, 2, count, DEEP) + tile, "direct"), ((2, 3) + tile, "direct"),
        ],
        cost=1_000_000, name="arrange", limit=4,
    )
    first_got = lax.all_to_all(slots, "depth", 0, 0)
    near_residual, near_media, waves = kernel_call(
        prepare_kernel,
        [
            (plan, "smem"), (near, "direct"), (extra, "direct"),
            (sources, "direct"), (guess, "direct"),
        ],
        [
            ((2, 2, count, edge) + tile, "direct"), ((2, MEDIA) + tile, "direct"),
            ((2, 2, edge, 2) + tile, "direct"),
        ],
        [Field.shape(count, DEEP + 1, tile)],
        cost=4_000_000, name="prepare", limit=4,
    )

    def chain(got, full):
        mine, theirs = kernel_call(
            chain_kernel,
            [(got, "direct"), (first_got, "direct"), (full, "direct")],
            [((4, 2, width) + tile, "direct")] * 2,
            cost=1_000_000, name="chain", limit=4,
        )
        return mine, lax.ppermute(theirs, "depth", even_pairs)

    mine, theirs = chain(first_got, full)
    new_field, new_residual, next_full, slots = kernel_call(
        middle_kernel,
        [
            (mine, "direct"), (theirs, "direct"),
            (plan, "smem"), (full, "direct"), (sources, "direct"),
            (pack, "direct"), (near_media, "direct"), (waves, "direct"),
            (near, "direct"), (near_residual, "direct"), (power, "direct"),
            (residual, "direct"), (guess, "direct"),
        ],
        [
            (planes(slab), "direct"), (planes(slab + 2 * (DEEP - 4)), "direct"),
            ((2, 2, count) + tile, "direct"), ((size, 2 * width) + tile, "direct"),
        ],
        [
            scratch((3, 2, 2, count) + tile),
            Field.shape(count, slab + 2 * edge, tile),
            Field.shape(count, slab + 2 * edge - 2, tile),
            Field.shape(count, slab + 2 * edge - 4, tile),
        ],
        cost=80_000_000, name="middle", limit=20,
    )
    mine, theirs = chain(lax.all_to_all(slots, "depth", 0, 0), next_full)
    (scaled,) = kernel_call(
        scale_kernel,
        [(new_residual, "direct"), (pack, "direct"), (near_media, "direct")],
        [(planes(slab + 2 * (DEEP - 4)), "direct")],
        cost=4_000_000, name="scale", limit=4,
    )
    (out,) = kernel_call(
        final_kernel,
        [
            (mine, "direct"), (theirs, "direct"), (next_full, "direct"),
            (pack, "direct"), (near_media, "direct"), (waves, "direct"),
            (power, "direct"), (scaled, "direct"), (new_field, "direct"),
        ],
        [(planes(slab), "hbm")],
        [
            scratch(planes(slab)), scratch((3, 2, 2, count) + tile),
            Field.shape(count, slab + 4, tile), Field.shape(count, slab + 2, tile),
        ],
        pieces=3, cost=60_000_000, name="final", limit=16,
    )
    return out


def solution(mesh):
    return jax.shard_map(
        local,
        mesh=mesh,
        in_specs=(
            P(None, "groups", None, None),
            P("groups"),
            P("depth", "groups", None),
            P("depth", "groups", None),
            P(),
            P("groups"),
            P(None, "groups", "depth", None, None),
        ),
        out_specs=P(None, "groups", "depth", None, None),
        check_vma=False,
    )
```

```python
import functools

import jax
import jax.numpy as jnp
from jax import lax
from jax.experimental import pallas as pl
from jax.experimental.pallas import tpu as pltpu
from jax.sharding import PartitionSpec as P

relax_weight = 0.8
shift_ratio = 0.5
damping = 3.0
coupling = 0.25
keep = 1.0 - relax_weight

DEEP = 6
UNROLL = 4
LAG = UNROLL + 1


def cmul(a, b):
    return a[0] * b[0] - a[1] * b[1], a[0] * b[1] + a[1] * b[0]


def add(a, b):
    return a[0] + b[0], a[1] + b[1]


def scale(c, a):
    return c * a[0], c * a[1]


def pick(cond, a, b):
    return jnp.where(cond, a[0], b[0]), jnp.where(cond, a[1], b[1])


def tile_of(ref, *at):
    return ref[at + (0,)], ref[at + (1,)]


class Inward:
    def __init__(self, source, target, sem):
        self.ref = target
        self.copy = pltpu.make_async_copy(source, target, sem)
        self.copy.start()

    def wait(self):
        self.copy.wait()
        return self.ref


def kernel_call(body, inputs, outputs, scratch=(), pieces=0, cost=0, name=None, limit=56):
    n_in, n_out = len(inputs), len(outputs)
    pinned = ("hbm", "vmem", "smem")
    extra = []
    for array, place in inputs:
        if place in ("vmem", "smem"):
            space = pltpu.SMEM if place == "smem" else pltpu.VMEM
            extra.append(space(array.shape, array.dtype))
    for shape, place in outputs:
        if place == "vmem":
            extra.append(pltpu.VMEM(shape, jnp.float32))
    n_extra = len(extra)

    def kernel(*refs):
        ins, outs = refs[:n_in], refs[n_in : n_in + n_out]
        buffers = iter(refs[n_in + n_out : n_in + n_out + n_extra])
        sems = refs[n_in + n_out + n_extra]
        rest = refs[n_in + n_out + n_extra + 1 :]
        used = iter(range(n_extra + pieces))
        pending = []

        def start(source, target):
            return Inward(source, target, sems.at[next(used)])

        def send(source, target):
            pending.append(start(source, target))

        def arrive():
            given = []
            for ref, (_, place) in zip(ins, inputs):
                copied = place in ("vmem", "smem")
                given.append(start(ref, next(buffers)) if copied else ref)
            return given

        given = arrive()
        made = []
        for ref, (_, place) in zip(outs, outputs):
            if place != "vmem":
                made.append(ref)
            else:
                buffer = next(buffers)
                made.append((buffer, functools.partial(send, buffer, ref)))
        body(start, send, given, made, rest)
        for copy in pending:
            copy.wait()

    def spec(place):
        return pl.BlockSpec(memory_space=pltpu.VMEM if place == "direct" else pltpu.HBM)

    return pl.pallas_call(
        kernel,
        out_shape=tuple(jax.ShapeDtypeStruct(s, jnp.float32) for s, _ in outputs),
        in_specs=[spec(place) for _, place in inputs],
        out_specs=tuple(spec(place) for _, place in outputs),
        scratch_shapes=[
            *extra,
            pltpu.SemaphoreType.DMA((max(1, n_extra + pieces),)),
            *scratch,
        ],
        compiler_params=pltpu.CompilerParams(vmem_limit_bytes=limit << 20),
        cost_estimate=pl.CostEstimate(
            flops=cost, bytes_accessed=4 << 20, transcendentals=0
        ),
        name=name,
    )(*[
        pltpu.with_memory_space_constraint(array, pltpu.HBM) if place in pinned else array
        for array, place in inputs
    ])


def lane_sum(here, masks):
    breadth = here.shape[-1]
    axis = here.ndim - 1
    ahead = jnp.where(masks[0], pltpu.roll(here, 1, axis), 0.0)
    behind = jnp.where(masks[1], pltpu.roll(here, breadth - 1, axis), 0.0)
    return ahead + behind


class Field:
    def __init__(self, ref, first, height):
        self.ref, self.first, self.height = ref, first, height

    @staticmethod
    def shape(count, planes, tile):
        return pltpu.VMEM((2, count, (2 * planes + 1) * tile[0], tile[1]), jnp.float32)

    def rows(self, plane, shift=0):
        start = (2 * (plane - self.first) + 1) * self.height + shift
        if shift % self.height == 0:
            start = pl.multiple_of(start, self.height)
        return pl.ds(start, self.height)

    def clear(self):
        edge = self.ref[:, :, : self.height]
        self.ref[:, :, : self.height] = jnp.zeros_like(edge)

    def get(self, part, plane, shift=0):
        return self.ref[part, :, self.rows(plane, shift)]

    def both(self, plane):
        return self.get(0, plane), self.get(1, plane)

    def put(self, part, plane, value):
        self.ref[part, :, self.rows(plane)] = value
        self.ref[part, :, self.rows(plane, self.height)] = jnp.zeros_like(value)

    def put_both(self, plane, value):
        for part in range(2):
            self.put(part, plane, value[part])

    def bump(self, plane, s, value):
        for part in range(2):
            self.ref[part, s, self.rows(plane)] += value[part]

    def lanes(self, part, plane, masks):
        return lane_sum(self.get(part, plane), masks)

    def around(self, plane, lanes):
        heres, totals = [], []
        for part in range(2):
            here = self.get(part, plane)
            beside = self.get(part, plane, -1) + self.get(part, plane, 1)
            depth = self.get(part, plane - 1) + self.get(part, plane + 1)
            heres.append(here)
            totals.append((beside + depth) + lanes(part, plane))
        return tuple(heres), tuple(totals)

    def minus_a(self, plane, diagonal, layer3, lanes):
        here, total = self.around(plane, lanes)
        return (
            (total[0] - diagonal * here[0]) + layer3 * here[1],
            (total[1] - diagonal * here[1]) - layer3 * here[0],
        )


class Lanes:
    def __init__(self, field, masks):
        self.field, self.masks = field, masks

    def now(self, part, plane):
        return self.field.lanes(part, plane, self.masks)


def lane_masks(tile):
    lane = lax.broadcasted_iota(jnp.int32, tile, 1)
    return lane > 0, lane < tile[1] - 1


INVERSE, DIAGONAL, LAYER, WAVE, SECOND, THIRD, MEDIA = 0, 2, 3, 4, 6, 8, 10


def set_media(ref, squared, layer, absorb, slab, inside=None):
    diagonal = 6.0 - squared
    imag = shift_ratio * squared + damping * layer
    size = diagonal * diagonal + imag * imag
    inverse = relax_weight * diagonal / size, -relax_weight * imag / size
    if inside is not None:
        inverse = tuple(jnp.where(inside, v, 0.0) for v in inverse)
    grow = 1.0 + keep
    decay = jnp.exp(-absorb / slab)
    angle = jnp.sqrt(squared)
    factor = decay * jnp.cos(angle), decay * jnp.sin(angle)
    values = (
        *inverse, diagonal, damping * layer, *factor,
        *scale(1.0 / grow, inverse), *scale(grow, inverse),
    )
    for i, value in enumerate(values):
        ref[i] = value
    return factor


def pair(ref, i):
    return ref[i], ref[i + 1]


def region_values(labels, kk_ref):
    squared = jnp.zeros(labels.shape, jnp.float32)
    for region in range(kk_ref.shape[0]):
        squared = jnp.where(labels == region, kk_ref[region], squared)
    return squared


def loop(start, stop, body, carry, unroll=UNROLL):
    trips = (stop - start) // unroll

    def several(trip, carry):
        for i in range(unroll):
            carry = body(start + trip * unroll + i, carry)
        return carry

    if trips > 1:
        carry = lax.fori_loop(0, trips, several, carry)
        start += trips * unroll
    for plane in range(start, stop):
        carry = body(plane, carry)
    return carry


def media_of(pack):
    return pack.at[pl.ds(0, MEDIA)]


def emit_tiles(count, way, part):
    return pl.ds(MEDIA + 4 + (2 * way + part) * count, count)


def side_tiles(count):
    return 2 * count * DEEP


def pack_kernel(start, send, given, made, rest):
    kk, absorb, labels, guess = given
    (out,) = made
    _, count, slab, *_ = guess.shape
    even = lax.rem(lax.axis_index("depth"), 2) == 0
    first = jnp.where(even, 0, slab - DEEP)
    for i in range(2 * count):
        send(
            guess.at[i // count, i % count, pl.ds(first, DEEP)],
            out.at[pl.ds(i * DEEP, DEEP)],
        )
    kk, absorb, labels = kk.wait(), absorb.wait(), labels.wait()
    out[side_tiles(count)] = absorb[0]
    out[side_tiles(count) + 1] = region_values(labels[0], kk)


def start_kernel(start, send, given, made, rest):
    plan, damp, sources, for_odd, guess = given
    residual, pack, power, for_even = made
    emits, ref = rest
    _, count, slab, height, breadth = guess.shape
    tile = (height, breadth)
    media = media_of(pack)
    masks = lane_masks(tile)
    field = Field(ref, -1, height)
    zero = jnp.zeros((count,) + tile, jnp.float32)
    field.clear()
    field.put_both(-1, (zero, zero))
    field.put_both(slab, (zero, zero))
    lanes = Lanes(field, masks)
    absorb, squared = pair(for_odd, side_tiles(count))
    row = lax.broadcasted_iota(jnp.int32, tile, 0)
    lane = lax.broadcasted_iota(jnp.int32, tile, 1)
    cell = row * breadth + lane
    damp = damp.wait()

    def mark(i, hit):
        return jnp.where(cell == damp[i], 1.0, hit)

    layer = loop(0, damp.shape[0], mark, jnp.zeros(tile, jnp.float32), 16)
    set_media(media, squared, layer, absorb, slab)
    diagonal, layer3 = media[DIAGONAL], media[LAYER]
    inverse, factor = pair(media, INVERSE), pair(media, WAVE)

    def fill(p):
        for part in range(2):
            field.put(part, p, guess[part, :, p])

    def plane(k, carry):
        toward_next, toward_prev, w = carry
        power[k, 0], power[k, 1] = w
        r = field.minus_a(k, diagonal, layer3, lanes.now)
        residual[0, :, k], residual[1, :, k] = cmul(inverse, r)
        toward_next = add(cmul(factor, toward_next), r)
        toward_prev = add(toward_prev, cmul(w, r))
        return toward_next, toward_prev, cmul(factor, w)

    one = jnp.ones(tile, jnp.float32), jnp.zeros(tile, jnp.float32)
    carry = ((zero, zero), (zero, zero), one)
    fill(0)

    def group(trip, carry):
        base = trip * UNROLL
        for i in range(UNROLL):
            fill(base + i + 1)
        for i in range(UNROLL):
            carry = plane(base + i, carry)
        return carry

    trips = (slab - 1) // UNROLL
    carry = lax.fori_loop(0, trips, group, carry)
    for k in range(trips * UNROLL, slab):
        if k + 1 < slab:
            fill(k + 1)
        carry = plane(k, carry)
    plan, sources = plan.wait(), sources.wait()
    toward_next, toward_prev, w = carry
    power[slab, 0], power[slab, 1] = w
    add_forcing(plan, residual, sources, 0, slab, inverse)
    for part in range(2):
        emits[0, part] = toward_next[part]
        emits[1, part] = toward_prev[part]
        pack[MEDIA + part] = power[slab - 1, part]
        pack[MEDIA + 2 + part] = power[slab, part]
    force_emits(plan, emits, sources, power, slab)
    for way in range(2):
        for part in range(2):
            pack[emit_tiles(count, way, part)] = emits[way, part]
    first_plane = jnp.where(lax.rem(lax.axis_index("depth"), 2) == 0, slab - DEEP, 0)
    for i in range(2 * count):
        for_even[pl.ds(i * DEEP, DEEP)] = guess[
            i // count, i % count, pl.ds(first_plane, DEEP)
        ]
    for_even[side_tiles(count)] = absorb
    for_even[side_tiles(count) + 1] = squared


def add_forcing(plan, held, sources, reach, slab, inverse=None):
    first_plane = lax.axis_index("depth") * slab
    for s in range(sources.shape[1]):
        k = plan[s] - first_plane

        @pl.when((k >= -reach) & (k < slab + reach))
        def _():
            src = sources[0, s], sources[1, s]
            if inverse is not None:
                src = cmul(inverse, src)
            for part in range(2):
                held[part, s, k + reach] += src[part]


def force_emits(plan, emits, sources, power, slab):
    first_plane = lax.axis_index("depth") * slab
    for s in range(sources.shape[1]):
        k = plan[s] - first_plane

        @pl.when((k >= 0) & (k < slab))
        def _():
            src = sources[0, s], sources[1, s]
            onward = cmul(tile_of(power, slab - 1 - k), src)
            back = cmul(tile_of(power, k), src)
            for part in range(2):
                emits[0, part, s] += onward[part]
                emits[1, part, s] += back[part]


class Split:
    def __init__(self, tile):
        self.half = tile[0] // 2
        self.upper = lax.broadcasted_iota(jnp.int32, tile, 0) < self.half

    def turn(self, value):
        return pltpu.roll(value, self.half, value.ndim - 2)

    def pack(self, core, first, second):
        if core == 0:
            return jnp.where(self.upper, first, self.turn(second))
        return jnp.where(self.upper, self.turn(first), second)

    def unpack(self, core_0, core_1):
        first = jnp.where(self.upper, core_0, self.turn(core_1))
        second = jnp.where(self.upper, self.turn(core_0), core_1)
        return first, second

    def spread(self, packed):
        turned = self.turn(packed)
        return jnp.where(self.upper, packed, turned), jnp.where(self.upper, turned, packed)


def pack_waves(split, core, full, way):
    count = full.shape[2]
    return tuple(
        jnp.stack(
            [
                split.pack(core, full[way, part, s], full[way, part, s + 1])
                for s in range(0, count, 2)
            ]
        )
        for part in range(2)
    )


def fill_send(slots, full, passage):
    place = lax.axis_index("depth")
    width = full.shape[2] // 2
    split = Split(full.shape[3:])
    waves = [[pack_waves(split, core, full, way) for way in range(2)] for core in range(2)]

    def one(chip, unused):
        for core in range(2):
            j = 2 * chip + core
            onward, back = waves[core]
            for part in range(2):
                slots[j, pl.ds(part * width, width)] = jnp.where(
                    j > place, onward[part], back[part]
                )
            if passage is not None:
                slots[j, 2 * width] = split.pack(core, *passage)
        return unused

    loop(0, slots.shape[0] // 2, one, 0, 4)


def arrange_kernel(start, send, given, made, rest):
    got_even, got_odd, pack = given
    full, slots, near, extra = made
    even = lax.rem(lax.axis_index("depth"), 2) == 0
    count = full.shape[2]
    weight, passage = pair(pack, MEDIA), pair(pack, MEDIA + 2)
    emits = [[pack[emit_tiles(count, way, part)] for part in range(2)] for way in range(2)]
    for s in range(count):
        at = [(part * count + s) * DEEP for part in range(2)]
        low = tuple(
            jnp.where(even, got_odd[i + DEEP - 1], got_even[i + DEEP - 1]) for i in at
        )
        high = tuple(jnp.where(even, got_even[i], got_odd[i]) for i in at)
        toward_next = add(add(cmul(weight, low), high), (emits[0][0][s], emits[0][1][s]))
        toward_prev = add(add(cmul(weight, high), low), (emits[1][0][s], emits[1][1][s]))
        for part in range(2):
            full[0, part, s] = toward_next[part]
            full[1, part, s] = toward_prev[part]
    fill_send(slots, full, passage)
    for side in range(2):
        first, second = (got_odd, got_even) if side == 0 else (got_even, got_odd)
        for i in range(2 * count):
            rows = pl.ds(i * DEEP, DEEP)
            near[side, i // count, i % count] = jnp.where(
                even, first[rows], second[rows]
            )
        for i in range(2):
            at = 2 * count * DEEP + i
            extra[side, i] = jnp.where(even, first[at], second[at])
    extra[0, 2] = extra[1, 2] = media_of(pack)[LAYER]


def prepare_kernel(start, send, given, made, rest):
    plan, near, extra, sources, guess = given
    res, near_media, waves = made
    (ref,) = rest
    _, count, slab, height, breadth = guess.shape
    tile = (height, breadth)
    masks = lane_masks(tile)
    place = lax.axis_index("depth")
    last_place = lax.axis_size("depth") - 1
    layer3 = extra[0, 2]
    layer = layer3 / damping
    factors = []
    for side in range(2):
        squared = extra[side, 1]
        inside = (place > 0) if side == 0 else (place < last_place)
        factors.append(
            set_media(near_media.at[side], squared, layer, extra[side, 0], slab, inside)
        )

    ws = list(factors)
    edge = DEEP - 1

    def keep_power(k, ws):
        for side in range(2):
            for way in range(2):
                if side == way:
                    i = k - (slab - edge + 1)
                    i = edge - 1 - i if side else i
                else:
                    i = k - 1
                    i = i if side else edge - 1 - i
                if 0 <= i < edge:
                    for part in range(2):
                        waves[side, way, i, part] = ws[side][part]

    def next_power(k, ws):
        return tuple(cmul(factors[side], ws[side]) for side in range(2))

    k = 1
    while k <= slab:
        if edge < k < slab - edge + 1:
            ws = loop(k, slab - edge + 1, next_power, tuple(ws), 8)
            k = slab - edge + 1
        keep_power(k, ws)
        ws = next_power(k, ws)
        k += 1
    for side in range(2):
        field = Field(ref, 0, height)
        field.clear()
        for i in range(DEEP + 1):
            for part in range(2):
                if side == 0:
                    value = near[0, part, :, i] if i < DEEP else guess[part, :, 0]
                else:
                    value = near[1, part, :, i - 1] if i > 0 else guess[part, :, slab - 1]
                field.put(part, i, value)
        lanes = Lanes(field, masks)
        for i in range(1, DEEP):
            r = field.minus_a(i, near_media[side, DIAGONAL], layer3, lanes.now)
            r = cmul(pair(near_media.at[side], INVERSE), r)
            for part in range(2):
                res[side, part, :, i - 1] = r[part]
    plan = plan.wait()
    for s in range(count):
        k = plan[s] - place * slab
        for side, low in ((0, -edge), (1, slab)):
            i = k - low

            @pl.when((i >= 0) & (i < edge))
            def _():
                src = sources[0, s], sources[1, s]
                src = cmul(pair(near_media.at[side], INVERSE), src)
                for part in range(2):
                    res[side, part, s, i] += src[part]


def chain_kernel(start, send, given, made, rest):
    got, passages, full = given
    mine, theirs = made
    place = lax.axis_index("depth")
    last_place = lax.axis_size("depth") - 1
    width = full.shape[2] // 2
    split = Split(full.shape[3:])
    even = lax.rem(place, 2) == 0
    low = place - lax.rem(place, 2)
    high = low + 1
    zero = jnp.zeros((width,) + full.shape[3:], jnp.float32)
    passage = lambda j: split.spread(passages[j, 2 * width])
    emit = lambda way: pick(
        even, pack_waves(split, 0, full, way), pack_waves(split, 1, full, way)
    )
    came = lambda j: (got[j, pl.ds(0, width)], got[j, pl.ds(width, width)])

    def step(j, state):
        return add(cmul(passage(j), state), came(j))

    below = jnp.maximum(low - 1, 0)
    above = jnp.minimum(high + 1, last_place)
    next_before = lax.fori_loop(0, below, step, (zero, zero))
    next_low = pick(low > 0, step(below, next_before), (zero, zero))
    next_high = add(cmul(passage(low), next_low), pick(even, emit(0), came(low)))
    prev_after = lax.fori_loop(
        0, last_place - above, lambda t, state: step(last_place - t, state), (zero, zero)
    )
    prev_high = pick(high < last_place, step(above, prev_after), (zero, zero))
    prev_low = add(cmul(passage(high), prev_high), pick(even, came(high), emit(1)))
    for_low = next_before, next_low, prev_low, prev_high
    for_high = next_low, next_high, prev_high, prev_after
    for i in range(4):
        own, other = pick(even, for_low[i], for_high[i]), pick(even, for_high[i], for_low[i])
        for part in range(2):
            mine[i, part] = own[part]
            theirs[i, part] = other[part]


def set_incoming(ref, mine, theirs, full, passage, media, near_media):
    inverses = [
        scale(coupling, pair(m, INVERSE))
        for m in (near_media.at[0], media, near_media.at[1])
    ]
    even = lax.rem(lax.axis_index("depth"), 2) == 0
    count = full.shape[2]
    split = Split(full.shape[3:])
    waves = []
    for i in range(4):
        parts = []
        for part in range(2):
            own, other = mine[i, part], theirs[i, part]
            first, second = split.unpack(
                jnp.where(even, own, other), jnp.where(even, other, own)
            )
            parts.append(jnp.stack([first, second], 1).reshape(full.shape[2:]))
        waves.append(tuple(parts))
    onward = add(cmul(passage, waves[1]), (full[0, 0], full[0, 1]))
    back = add(cmul(passage, waves[2]), (full[1, 0], full[1, 1]))
    spots = ((0, 0), (1, 0), (1, 1), (2, 1), (2, 0), (0, 1))
    for (side, way), value in zip(spots, [*waves, onward, back]):
        ref[side, way, 0], ref[side, way, 1] = cmul(inverses[side], value)


class Stage:
    def __init__(self, below, own, above):
        self.below, self.own, self.above = below, own, above


def pipeline(stages, slab, carry, halfway, by_plane):
    offsets = [LAG * (len(stages) - 1 - i) for i in range(len(stages))]
    trips = (slab - offsets[0]) // UNROLL

    def run(i, p, carry):
        out = stages[i].own(p, carry)
        return carry if out is None else out

    def own(i, start, stop, carry):
        body = lambda p, c: run(i, p, c)
        if start == 0 and stop > 0:
            carry = body(0, carry)
            start = 1
        if stop == slab and start < slab:
            return body(slab - 1, loop(start, slab - 1, body, carry))
        return loop(start, stop, body, carry)

    stages[0].below()
    stages[0].above()
    for i, stage in enumerate(stages):
        if i:
            stage.below()
        carry = own(i, 0, offsets[i], carry)

    def trip(t, carry):
        pairs = [(i, u) for i in range(len(stages)) for u in range(UNROLL)]
        if by_plane:
            pairs.sort(key=lambda pair: pair[1])
        for i, u in pairs:
            carry = run(i, t * UNROLL + offsets[i] + u, carry)
        return carry

    first = trips // 2
    carry = lax.fori_loop(0, first, trip, carry)
    halfway(0, [first * UNROLL + o for o in offsets])
    carry = lax.fori_loop(first, trips, trip, carry)
    halfway(1, [trips * UNROLL + o for o in offsets])
    for i, stage in enumerate(stages):
        carry = own(i, trips * UNROLL + offsets[i], slab, carry)
        if i:
            stage.above()
    return carry


def update_stages(
    reach, slab, tile, incoming, residual_of, media, near_media, power, waves,
    refs, emit, masks,
):
    edge = DEEP - 1
    first_update = Field(refs[0], -reach, tile[0])
    second_update = Field(refs[1], 1 - reach, tile[0])
    first_update.clear()
    second_update.clear()
    powers = (
        lambda p: (tile_of(waves, 0, 0, p + edge), tile_of(waves, 0, 1, p + edge)),
        lambda p: (tile_of(power, p + 1), tile_of(power, slab - p)),
        lambda p: (tile_of(waves, 1, 0, p - slab), tile_of(waves, 1, 1, p - slab)),
    )
    coefficients = near_media.at[0], media, near_media.at[1]
    first_lanes = Lanes(first_update, masks)
    second_lanes = Lanes(second_update, masks)

    def begin(which, p):
        on, off = powers[which](p)
        onward = incoming[which, 0, 0], incoming[which, 0, 1]
        back = incoming[which, 1, 0], incoming[which, 1, 1]
        c = add(cmul(on, onward), cmul(off, back))
        first_update.put_both(p, add(c, residual_of(which, p)))

    def second(which, p):
        here, total = first_update.around(p, first_lanes.now)
        smoothed = cmul(pair(coefficients[which], SECOND), total)
        second_update.put_both(p, add(here, smoothed))

    def third(which, p):
        here, total = second_update.around(p, second_lanes.now)
        smoothed = cmul(pair(coefficients[which], THIRD), total)
        u = add(scale(keep * (1.0 + keep), here), smoothed)
        emit(which, p, add(u, first_update.both(p)))

    def stage(body, margin):
        def beyond(which, a, b):
            for p in range(a, b):
                body(which, p)

        return Stage(
            lambda: beyond(0, margin - reach, 0),
            lambda p, unused: body(1, p),
            lambda: beyond(2, slab, slab + reach - margin),
        )

    return [stage(begin, 0), stage(second, 1), stage(third, 2)]


def middle_kernel(start, send, given, made, rest):
    (
        mine, theirs, plan, full, sources, pack, near_media, waves, near,
        near_residual, power, residual, guess,
    ) = given
    media = media_of(pack)
    new_field, new_residual, next_full, slots = made
    incoming, *refs = rest
    _, count, slab, height, breadth = guess.shape
    tile = (height, breadth)
    masks = lane_masks(tile)
    reach = DEEP - 1
    ext = reach - 2
    more = ext - 1
    new = Field(refs[2], -ext, height)
    new.clear()
    set_incoming(
        incoming, mine, theirs, full, tile_of(power, slab), media, near_media
    )

    def residual_of(which, p):
        if which == 1:
            r = residual[0, :, p], residual[1, :, p]
            lacks = None
            if isinstance(p, int) and p == 0:
                lacks = near[0, 0, :, DEEP - 1], near[0, 1, :, DEEP - 1]
            if isinstance(p, int) and p == slab - 1:
                lacks = near[1, 0, :, 0], near[1, 1, :, 0]
            return r if lacks is None else add(r, cmul(pair(media, INVERSE), lacks))
        i = p + reach if which == 0 else p - slab
        return near_residual[which // 2, 0, :, i], near_residual[which // 2, 1, :, i]

    def emit(which, p, u):
        for part in range(2):
            if which == 1:
                value = guess[part, :, p] + u[part]
                new_field[part, :, p] = value
            else:
                i = p + DEEP if which == 0 else p - slab
                value = near[which // 2, part, :, i] + u[part]
            new.put(part, p, value)

    stages = update_stages(
        reach, slab, tile, incoming, residual_of, media, near_media, power, waves,
        refs, emit, masks,
    )

    layer3 = media[LAYER]
    factor = pair(media, WAVE)
    lanes = Lanes(new, masks)

    def residual_at(p, diagonal):
        r = new.minus_a(p, diagonal, layer3, lanes.now)
        for part in range(2):
            new_residual[part, :, p + more] = r[part]
        return r

    def beyond(side, a, b):
        for p in range(a, b):
            residual_at(p, near_media[side, DIAGONAL])

    def inside(p, carry):
        toward_next, toward_prev = carry
        r = residual_at(p, media[DIAGONAL])
        toward_next = add(cmul(factor, toward_next), r)
        toward_prev = add(toward_prev, cmul(tile_of(power, p), r))
        return toward_next, toward_prev

    stages.append(
        Stage(lambda: beyond(0, -more, 0), inside, lambda: beyond(1, slab, slab + more))
    )
    zero = jnp.zeros((count,) + tile, jnp.float32)
    carry = pipeline(
        stages, slab, ((zero, zero), (zero, zero)), lambda i, reached: None, True
    )
    for way in range(2):
        for part in range(2):
            next_full[way, part] = carry[way][part]
    plan = plan.wait()
    force_emits(plan, next_full, sources, power, slab)
    fill_send(slots, next_full, None)
    add_forcing(plan, new_residual, sources, more, slab)


def scale_kernel(start, send, given, made, rest):
    residual, pack, near_media = given
    (out,) = made
    planes = residual.shape[2]
    reach = DEEP - 4

    def one(p, m):
        value = cmul(pair(m, INVERSE), (residual[0, :, p], residual[1, :, p]))
        out[0, :, p], out[1, :, p] = value

    media = media_of(pack)
    for p in range(reach):
        one(p, near_media.at[0])
        one(planes - 1 - p, near_media.at[1])
    loop(reach, planes - reach, lambda p, c: one(p, media) or c, 0, 8)


def final_kernel(start, send, given, made, rest):
    (
        mine, theirs, full, pack, near_media, waves, power, residual, field,
    ) = given
    (out,) = made
    media = media_of(pack)
    held, incoming, *refs = rest
    _, count, slab, height, breadth = field.shape
    tile = (height, breadth)
    reach = 2
    masks = lane_masks(tile)
    set_incoming(
        incoming, mine, theirs, full, tile_of(power, slab), media, near_media
    )

    def residual_of(which, p):
        return residual[0, :, p + reach], residual[1, :, p + reach]

    def emit(which, p, u):
        for part in range(2):
            held[part, :, p] = field[part, :, p] + u[part]

    stages = update_stages(
        reach, slab, tile, incoming, residual_of, media, near_media, power, waves,
        refs, emit, masks,
    )
    sent = [0]

    def send_field(top):
        part = pl.ds(sent[0], top - sent[0])
        send(held.at[:, :, part], out.at[:, :, part])
        sent[0] = top

    pipeline(stages, slab, 0, lambda i, reached: send_field(reached[2]), False)
    send_field(slab)


def local(sources, plan, absorb, labels, region_kk, damp_cells, guess):
    size = lax.axis_size("depth")
    _, count, slab, height, breadth = guess.shape
    tile = (height, breadth)
    edge = DEEP - 1
    planes = lambda n: (2, count, n) + tile
    scratch = lambda shape: pltpu.VMEM(shape, jnp.float32)

    tiles = (side_tiles(count) + 2,) + tile
    (for_odd,) = kernel_call(
        pack_kernel,
        [
            (region_kk, "smem"), (absorb, "vmem"), (labels, "vmem"), (guess, "hbm"),
        ],
        [(tiles, "direct")],
        pieces=2 * count, cost=1_000_000, name="pack", limit=4,
    )
    even_pairs = [(i, i ^ 1) for i in range(size)]
    odd_pairs = [(i, i + 1) for i in range(1, size - 1, 2)]
    odd_pairs += [(b, a) for a, b in odd_pairs]
    got_odd = lax.ppermute(for_odd, "depth", odd_pairs)

    residual, pack, power, for_even = kernel_call(
        start_kernel,
        [
            (plan, "smem"), (damp_cells, "smem"), (sources, "vmem"),
            (for_odd, "direct"), (guess, "direct"),
        ],
        [
            (planes(slab), "direct"), ((MEDIA + 4 + 4 * count,) + tile, "direct"),
            ((slab + 1, 2) + tile, "direct"), (tiles, "direct"),
        ],
        [
            scratch((2, 2, count) + tile), Field.shape(count, slab + 2, tile),
        ],
        cost=20_000_000, name="start", limit=12,
    )
    got_even = lax.ppermute(for_even, "depth", even_pairs)
    width = count // 2
    full, slots, near, extra = kernel_call(
        arrange_kernel,
        [(got_even, "direct"), (got_odd, "direct"), (pack, "direct")],
        [
            ((2, 2, count) + tile, "direct"), ((size, 2 * width + 1) + tile, "direct"),
            ((2, 2, count, DEEP) + tile, "direct"), ((2, 3) + tile, "direct"),
        ],
        cost=1_000_000, name="arrange", limit=4,
    )
    first_got = lax.all_to_all(slots, "depth", 0, 0)
    near_residual, near_media, waves = kernel_call(
        prepare_kernel,
        [
            (plan, "smem"), (near, "direct"), (extra, "direct"),
            (sources, "direct"), (guess, "direct"),
        ],
        [
            ((2, 2, count, edge) + tile, "direct"), ((2, MEDIA) + tile, "direct"),
            ((2, 2, edge, 2) + tile, "direct"),
        ],
        [Field.shape(count, DEEP + 1, tile)],
        cost=4_000_000, name="prepare", limit=4,
    )

    def chain(got, full):
        mine, theirs = kernel_call(
            chain_kernel,
            [(got, "direct"), (first_got, "direct"), (full, "direct")],
            [((4, 2, width) + tile, "direct")] * 2,
            cost=1_000_000, name="chain", limit=4,
        )
        return mine, lax.ppermute(theirs, "depth", even_pairs)

    mine, theirs = chain(first_got, full)
    new_field, new_residual, next_full, slots = kernel_call(
        middle_kernel,
        [
            (mine, "direct"), (theirs, "direct"),
            (plan, "smem"), (full, "direct"), (sources, "direct"),
            (pack, "direct"), (near_media, "direct"), (waves, "direct"),
            (near, "direct"), (near_residual, "direct"), (power, "direct"),
            (residual, "direct"), (guess, "direct"),
        ],
        [
            (planes(slab), "direct"), (planes(slab + 2 * (DEEP - 4)), "direct"),
            ((2, 2, count) + tile, "direct"), ((size, 2 * width) + tile, "direct"),
        ],
        [
            scratch((3, 2, 2, count) + tile),
            Field.shape(count, slab + 2 * edge, tile),
            Field.shape(count, slab + 2 * edge - 2, tile),
            Field.shape(count, slab + 2 * edge - 4, tile),
        ],
        cost=80_000_000, name="middle", limit=20,
    )
    mine, theirs = chain(lax.all_to_all(slots, "depth", 0, 0), next_full)
    (scaled,) = kernel_call(
        scale_kernel,
        [(new_residual, "direct"), (pack, "direct"), (near_media, "direct")],
        [(planes(slab + 2 * (DEEP - 4)), "direct")],
        cost=4_000_000, name="scale", limit=4,
    )
    (out,) = kernel_call(
        final_kernel,
        [
            (mine, "direct"), (theirs, "direct"), (next_full, "direct"),
            (pack, "direct"), (near_media, "direct"), (waves, "direct"),
            (power, "direct"), (scaled, "direct"), (new_field, "direct"),
        ],
        [(planes(slab), "hbm")],
        [
            scratch(planes(slab)), scratch((3, 2, 2, count) + tile),
            Field.shape(count, slab + 4, tile), Field.shape(count, slab + 2, tile),
        ],
        pieces=3, cost=60_000_000, name="final", limit=16,
    )
    return out


def solution(mesh):
    return jax.shard_map(
        local,
        mesh=mesh,
        in_specs=(
            P(None, "groups", None, None),
            P("groups"),
            P("depth", "groups", None),
            P("depth", "groups", None),
            P(),
            P("groups"),
            P(None, "groups", "depth", None, None),
        ),
        out_specs=P(None, "groups", "depth", None, None),
        check_vma=False,
    )
```

```python
import functools

import jax
import jax.numpy as jnp
from jax import lax
from jax.experimental import pallas as pl
from jax.experimental.pallas import tpu as pltpu
from jax.sharding import PartitionSpec as P

relax_weight = 0.8
shift_ratio = 0.5
damping = 3.0
coupling = 0.25
keep = 1.0 - relax_weight

DEEP = 6
UNROLL = 4
LAG = UNROLL + 1


def cmul(a, b):
    return a[0] * b[0] - a[1] * b[1], a[0] * b[1] + a[1] * b[0]


def add(a, b):
    return a[0] + b[0], a[1] + b[1]


def scale(c, a):
    return c * a[0], c * a[1]


def pick(cond, a, b):
    return jnp.where(cond, a[0], b[0]), jnp.where(cond, a[1], b[1])


def tile_of(ref, *at):
    return ref[at + (0,)], ref[at + (1,)]


class Inward:
    def __init__(self, source, target, sem):
        self.ref = target
        self.copy = pltpu.make_async_copy(source, target, sem)
        self.copy.start()

    def wait(self):
        self.copy.wait()
        return self.ref


def kernel_call(body, inputs, outputs, scratch=(), pieces=0, cost=0, name=None, limit=56):
    n_in, n_out = len(inputs), len(outputs)
    pinned = ("hbm", "vmem", "smem")
    extra = []
    for array, place in inputs:
        if place in ("vmem", "smem"):
            space = pltpu.SMEM if place == "smem" else pltpu.VMEM
            extra.append(space(array.shape, array.dtype))
    for shape, place in outputs:
        if place == "vmem":
            extra.append(pltpu.VMEM(shape, jnp.float32))
    n_extra = len(extra)

    def kernel(*refs):
        ins, outs = refs[:n_in], refs[n_in : n_in + n_out]
        buffers = iter(refs[n_in + n_out : n_in + n_out + n_extra])
        sems = refs[n_in + n_out + n_extra]
        rest = refs[n_in + n_out + n_extra + 1 :]
        used = iter(range(n_extra + pieces))
        pending = []

        def start(source, target):
            return Inward(source, target, sems.at[next(used)])

        def send(source, target):
            pending.append(start(source, target))

        def arrive():
            given = []
            for ref, (_, place) in zip(ins, inputs):
                copied = place in ("vmem", "smem")
                given.append(start(ref, next(buffers)) if copied else ref)
            return given

        given = arrive()
        made = []
        for ref, (_, place) in zip(outs, outputs):
            if place != "vmem":
                made.append(ref)
            else:
                buffer = next(buffers)
                made.append((buffer, functools.partial(send, buffer, ref)))
        body(start, send, given, made, rest)
        for copy in pending:
            copy.wait()

    def spec(place):
        return pl.BlockSpec(memory_space=pltpu.VMEM if place == "direct" else pltpu.HBM)

    return pl.pallas_call(
        kernel,
        out_shape=tuple(jax.ShapeDtypeStruct(s, jnp.float32) for s, _ in outputs),
        in_specs=[spec(place) for _, place in inputs],
        out_specs=tuple(spec(place) for _, place in outputs),
        scratch_shapes=[
            *extra,
            pltpu.SemaphoreType.DMA((max(1, n_extra + pieces),)),
            *scratch,
        ],
        compiler_params=pltpu.CompilerParams(vmem_limit_bytes=limit << 20),
        cost_estimate=pl.CostEstimate(
            flops=cost, bytes_accessed=4 << 20, transcendentals=0
        ),
        name=name,
    )(*[
        pltpu.with_memory_space_constraint(array, pltpu.HBM) if place in pinned else array
        for array, place in inputs
    ])


def lane_sum(here, masks):
    breadth = here.shape[-1]
    axis = here.ndim - 1
    ahead = jnp.where(masks[0], pltpu.roll(here, 1, axis), 0.0)
    behind = jnp.where(masks[1], pltpu.roll(here, breadth - 1, axis), 0.0)
    return ahead + behind


class Field:
    def __init__(self, ref, first, height):
        self.ref, self.first, self.height = ref, first, height

    @staticmethod
    def shape(count, planes, tile):
        return pltpu.VMEM((2, count, (2 * planes + 1) * tile[0], tile[1]), jnp.float32)

    def rows(self, plane, shift=0):
        start = (2 * (plane - self.first) + 1) * self.height + shift
        if shift % self.height == 0:
            start = pl.multiple_of(start, self.height)
        return pl.ds(start, self.height)

    def clear(self):
        edge = self.ref[:, :, : self.height]
        self.ref[:, :, : self.height] = jnp.zeros_like(edge)

    def get(self, part, plane, shift=0):
        return self.ref[part, :, self.rows(plane, shift)]

    def both(self, plane):
        return self.get(0, plane), self.get(1, plane)

    def put(self, part, plane, value):
        self.ref[part, :, self.rows(plane)] = value
        self.ref[part, :, self.rows(plane, self.height)] = jnp.zeros_like(value)

    def put_both(self, plane, value):
        for part in range(2):
            self.put(part, plane, value[part])

    def bump(self, plane, s, value):
        for part in range(2):
            self.ref[part, s, self.rows(plane)] += value[part]

    def lanes(self, part, plane, masks):
        return lane_sum(self.get(part, plane), masks)

    def around(self, plane, lanes):
        heres, totals = [], []
        for part in range(2):
            here = self.get(part, plane)
            beside = self.get(part, plane, -1) + self.get(part, plane, 1)
            depth = self.get(part, plane - 1) + self.get(part, plane + 1)
            heres.append(here)
            totals.append((beside + depth) + lanes(part, plane))
        return tuple(heres), tuple(totals)

    def minus_a(self, plane, diagonal, layer3, lanes):
        here, total = self.around(plane, lanes)
        return (
            (total[0] - diagonal * here[0]) + layer3 * here[1],
            (total[1] - diagonal * here[1]) - layer3 * here[0],
        )


class Lanes:
    def __init__(self, field, masks):
        self.field, self.masks = field, masks

    def now(self, part, plane):
        return self.field.lanes(part, plane, self.masks)


def lane_masks(tile):
    lane = lax.broadcasted_iota(jnp.int32, tile, 1)
    return lane > 0, lane < tile[1] - 1


INVERSE, DIAGONAL, LAYER, WAVE, SECOND, THIRD, MEDIA = 0, 2, 3, 4, 6, 8, 10


def wave(absorb, squared, order, slab):
    decay = jnp.exp(-order * absorb / slab)
    angle = order * jnp.sqrt(squared)
    return decay * jnp.cos(angle), decay * jnp.sin(angle)


def set_media(ref, squared, layer, absorb, slab, inside=None):
    diagonal = 6.0 - squared
    imag = shift_ratio * squared + damping * layer
    size = diagonal * diagonal + imag * imag
    inverse = relax_weight * diagonal / size, -relax_weight * imag / size
    if inside is not None:
        inverse = tuple(jnp.where(inside, v, 0.0) for v in inverse)
    grow = 1.0 + keep
    factor = wave(absorb, squared, 1, slab)
    values = (
        *inverse, diagonal, damping * layer, *factor,
        *scale(1.0 / grow, inverse), *scale(grow, inverse),
    )
    for i, value in enumerate(values):
        ref[i] = value
    return factor


def pair(ref, i):
    return ref[i], ref[i + 1]


def region_values(labels, kk_ref):
    squared = jnp.zeros(labels.shape, jnp.float32)
    for region in range(kk_ref.shape[0]):
        squared = jnp.where(labels == region, kk_ref[region], squared)
    return squared


def loop(start, stop, body, carry, unroll=UNROLL):
    trips = (stop - start) // unroll

    def several(trip, carry):
        for i in range(unroll):
            carry = body(start + trip * unroll + i, carry)
        return carry

    if trips > 1:
        carry = lax.fori_loop(0, trips, several, carry)
        start += trips * unroll
    for plane in range(start, stop):
        carry = body(plane, carry)
    return carry


def media_of(pack):
    return pack.at[pl.ds(0, MEDIA)]


def emit_tiles(count, way, part):
    return pl.ds(MEDIA + 4 + (2 * way + part) * count, count)


def side_tiles(count):
    return 2 * count * DEEP


def pack_kernel(start, send, given, made, rest):
    kk, damp, absorb, labels, guess = given
    out, base = made
    _, count, slab, *tile = guess.shape
    even = lax.rem(lax.axis_index("depth"), 2) == 0
    first = jnp.where(even, 0, slab - DEEP)
    for i in range(2 * count):
        send(
            guess.at[i // count, i % count, pl.ds(first, DEEP)],
            out.at[pl.ds(i * DEEP, DEEP)],
        )
    row = lax.broadcasted_iota(jnp.int32, tuple(tile), 0)
    lane = lax.broadcasted_iota(jnp.int32, tuple(tile), 1)
    cell = row * tile[1] + lane
    kk, absorb, labels = kk.wait(), absorb.wait(), labels.wait()
    squared = region_values(labels[0], kk)
    out[side_tiles(count)] = absorb[0]
    out[side_tiles(count) + 1] = squared
    base[MEDIA] = absorb[0]
    base[MEDIA + 1] = squared
    damp = damp.wait()

    def mark(i, hit):
        return jnp.where(cell == damp[i], 1.0, hit)

    layer = loop(0, damp.shape[0], mark, jnp.zeros(tile, jnp.float32), 16)
    set_media(base, squared, layer, absorb[0], slab)


def start_kernel(start, send, given, made, rest):
    plan, sources, base, guess = given
    residual, pack, power, for_even = made
    emits, ref = rest
    _, count, slab, height, breadth = guess.shape
    tile = (height, breadth)
    media = media_of(pack)
    media[...] = base[:MEDIA]
    masks = lane_masks(tile)
    field = Field(ref, -1, height)
    zero = jnp.zeros((count,) + tile, jnp.float32)
    field.clear()
    field.put_both(-1, (zero, zero))
    field.put_both(slab, (zero, zero))
    lanes = Lanes(field, masks)
    diagonal, layer3 = media[DIAGONAL], media[LAYER]
    inverse, factor = pair(media, INVERSE), pair(media, WAVE)

    def fill(p):
        for part in range(2):
            field.put(part, p, guess[part, :, p])

    def plane(k, carry):
        toward_next, toward_prev, w = carry
        power[k, 0], power[k, 1] = w
        r = field.minus_a(k, diagonal, layer3, lanes.now)
        residual[0, :, k], residual[1, :, k] = cmul(inverse, r)
        toward_next = add(cmul(factor, toward_next), r)
        toward_prev = add(toward_prev, cmul(w, r))
        return toward_next, toward_prev, cmul(factor, w)

    one = jnp.ones(tile, jnp.float32), jnp.zeros(tile, jnp.float32)
    carry = ((zero, zero), (zero, zero), one)
    fill(0)

    def group(trip, carry):
        base = trip * UNROLL
        for i in range(UNROLL):
            fill(base + i + 1)
        for i in range(UNROLL):
            carry = plane(base + i, carry)
        return carry

    trips = (slab - 1) // UNROLL
    carry = lax.fori_loop(0, trips, group, carry)
    for k in range(trips * UNROLL, slab):
        if k + 1 < slab:
            fill(k + 1)
        carry = plane(k, carry)
    plan, sources = plan.wait(), sources.wait()
    toward_next, toward_prev, _ = carry
    power[slab, 0], power[slab, 1] = wave(*pair(base, MEDIA), slab, slab)
    add_forcing(plan, residual, sources, 0, slab, inverse)
    for part in range(2):
        emits[0, part] = toward_next[part]
        emits[1, part] = toward_prev[part]
        pack[MEDIA + part] = power[slab - 1, part]
        pack[MEDIA + 2 + part] = power[slab, part]
    force_emits(plan, emits, sources, power, slab)
    for way in range(2):
        for part in range(2):
            pack[emit_tiles(count, way, part)] = emits[way, part]
    first_plane = jnp.where(lax.rem(lax.axis_index("depth"), 2) == 0, slab - DEEP, 0)
    for i in range(2 * count):
        for_even[pl.ds(i * DEEP, DEEP)] = guess[
            i // count, i % count, pl.ds(first_plane, DEEP)
        ]
    for_even[pl.ds(side_tiles(count), 2)] = base[MEDIA : MEDIA + 2]


def add_forcing(plan, held, sources, reach, slab, inverse=None):
    first_plane = lax.axis_index("depth") * slab
    for s in range(sources.shape[1]):
        k = plan[s] - first_plane

        @pl.when((k >= -reach) & (k < slab + reach))
        def _():
            src = sources[0, s], sources[1, s]
            if inverse is not None:
                src = cmul(inverse, src)
            for part in range(2):
                held[part, s, k + reach] += src[part]


def force_emits(plan, emits, sources, power, slab):
    first_plane = lax.axis_index("depth") * slab
    for s in range(sources.shape[1]):
        k = plan[s] - first_plane

        @pl.when((k >= 0) & (k < slab))
        def _():
            src = sources[0, s], sources[1, s]
            onward = cmul(tile_of(power, slab - 1 - k), src)
            back = cmul(tile_of(power, k), src)
            for part in range(2):
                emits[0, part, s] += onward[part]
                emits[1, part, s] += back[part]


class Split:
    def __init__(self, tile):
        self.half = tile[0] // 2
        self.upper = lax.broadcasted_iota(jnp.int32, tile, 0) < self.half

    def turn(self, value):
        return pltpu.roll(value, self.half, value.ndim - 2)

    def pack(self, core, first, second):
        if core == 0:
            return jnp.where(self.upper, first, self.turn(second))
        return jnp.where(self.upper, self.turn(first), second)

    def unpack(self, core_0, core_1):
        first = jnp.where(self.upper, core_0, self.turn(core_1))
        second = jnp.where(self.upper, self.turn(core_0), core_1)
        return first, second

    def spread(self, packed):
        turned = self.turn(packed)
        return jnp.where(self.upper, packed, turned), jnp.where(self.upper, turned, packed)


def pack_waves(split, core, full, way):
    count = full.shape[2]
    return tuple(
        jnp.stack(
            [
                split.pack(core, full[way, part, s], full[way, part, s + 1])
                for s in range(0, count, 2)
            ]
        )
        for part in range(2)
    )


def fill_send(slots, full, passage):
    place = lax.axis_index("depth")
    width = full.shape[2] // 2
    split = Split(full.shape[3:])
    waves = [[pack_waves(split, core, full, way) for way in range(2)] for core in range(2)]

    def one(chip, unused):
        for core in range(2):
            j = 2 * chip + core
            onward, back = waves[core]
            for part in range(2):
                slots[j, pl.ds(part * width, width)] = jnp.where(
                    j > place, onward[part], back[part]
                )
            if passage is not None:
                slots[j, 2 * width] = split.pack(core, *passage)
        return unused

    loop(0, slots.shape[0] // 2, one, 0, 4)


def arrange_kernel(start, send, given, made, rest):
    got_even, got_odd, pack = given
    full, slots, near, extra = made
    even = lax.rem(lax.axis_index("depth"), 2) == 0
    count = full.shape[2]
    weight, passage = pair(pack, MEDIA), pair(pack, MEDIA + 2)
    emits = [[pack[emit_tiles(count, way, part)] for part in range(2)] for way in range(2)]
    for s in range(count):
        at = [(part * count + s) * DEEP for part in range(2)]
        low = tuple(
            jnp.where(even, got_odd[i + DEEP - 1], got_even[i + DEEP - 1]) for i in at
        )
        high = tuple(jnp.where(even, got_even[i], got_odd[i]) for i in at)
        toward_next = add(add(cmul(weight, low), high), (emits[0][0][s], emits[0][1][s]))
        toward_prev = add(add(cmul(weight, high), low), (emits[1][0][s], emits[1][1][s]))
        for part in range(2):
            full[0, part, s] = toward_next[part]
            full[1, part, s] = toward_prev[part]
    fill_send(slots, full, passage)
    for side in range(2):
        first, second = (got_odd, got_even) if side == 0 else (got_even, got_odd)
        for i in range(2 * count):
            rows = pl.ds(i * DEEP, DEEP)
            near[side, i // count, i % count] = jnp.where(
                even, first[rows], second[rows]
            )
        for i in range(2):
            at = 2 * count * DEEP + i
            extra[side, i] = jnp.where(even, first[at], second[at])
    extra[0, 2] = extra[1, 2] = media_of(pack)[LAYER]


def prepare_kernel(start, send, given, made, rest):
    plan, near, extra, sources, guess = given
    res, near_media, waves = made
    (ref,) = rest
    _, count, slab, height, breadth = guess.shape
    tile = (height, breadth)
    masks = lane_masks(tile)
    place = lax.axis_index("depth")
    last_place = lax.axis_size("depth") - 1
    layer3 = extra[0, 2]
    layer = layer3 / damping
    factors = []
    for side in range(2):
        squared = extra[side, 1]
        inside = (place > 0) if side == 0 else (place < last_place)
        factors.append(
            set_media(near_media.at[side], squared, layer, extra[side, 0], slab, inside)
        )

    ws = list(factors)
    edge = DEEP - 1

    def keep_power(k, ws):
        for side in range(2):
            for way in range(2):
                if side == way:
                    i = k - (slab - edge + 1)
                    i = edge - 1 - i if side else i
                else:
                    i = k - 1
                    i = i if side else edge - 1 - i
                if 0 <= i < edge:
                    for part in range(2):
                        waves[side, way, i, part] = ws[side][part]

    def next_power(k, ws):
        return tuple(cmul(factors[side], ws[side]) for side in range(2))

    k = 1
    while k <= slab:
        if edge < k < slab - edge + 1:
            ws = loop(k, slab - edge + 1, next_power, tuple(ws), 8)
            k = slab - edge + 1
        keep_power(k, ws)
        ws = next_power(k, ws)
        k += 1
    for side in range(2):
        field = Field(ref, 0, height)
        field.clear()
        for i in range(DEEP + 1):
            for part in range(2):
                if side == 0:
                    value = near[0, part, :, i] if i < DEEP else guess[part, :, 0]
                else:
                    value = near[1, part, :, i - 1] if i > 0 else guess[part, :, slab - 1]
                field.put(part, i, value)
        lanes = Lanes(field, masks)
        for i in range(1, DEEP):
            r = field.minus_a(i, near_media[side, DIAGONAL], layer3, lanes.now)
            r = cmul(pair(near_media.at[side], INVERSE), r)
            for part in range(2):
                res[side, part, :, i - 1] = r[part]
    plan = plan.wait()
    for s in range(count):
        k = plan[s] - place * slab
        for side, low in ((0, -edge), (1, slab)):
            i = k - low

            @pl.when((i >= 0) & (i < edge))
            def _():
                src = sources[0, s], sources[1, s]
                src = cmul(pair(near_media.at[side], INVERSE), src)
                for part in range(2):
                    res[side, part, s, i] += src[part]


def chain_kernel(start, send, given, made, rest):
    got, passages, full = given
    mine, theirs = made
    place = lax.axis_index("depth")
    last_place = lax.axis_size("depth") - 1
    width = full.shape[2] // 2
    split = Split(full.shape[3:])
    even = lax.rem(place, 2) == 0
    low = place - lax.rem(place, 2)
    high = low + 1
    zero = jnp.zeros((width,) + full.shape[3:], jnp.float32)
    passage = lambda j: split.spread(passages[j, 2 * width])
    emit = lambda way: pick(
        even, pack_waves(split, 0, full, way), pack_waves(split, 1, full, way)
    )
    came = lambda j: (got[j, pl.ds(0, width)], got[j, pl.ds(width, width)])

    def step(j, state):
        return add(cmul(passage(j), state), came(j))

    below = jnp.maximum(low - 1, 0)
    above = jnp.minimum(high + 1, last_place)
    next_before = lax.fori_loop(0, below, step, (zero, zero))
    next_low = pick(low > 0, step(below, next_before), (zero, zero))
    next_high = add(cmul(passage(low), next_low), pick(even, emit(0), came(low)))
    prev_after = lax.fori_loop(
        0, last_place - above, lambda t, state: step(last_place - t, state), (zero, zero)
    )
    prev_high = pick(high < last_place, step(above, prev_after), (zero, zero))
    prev_low = add(cmul(passage(high), prev_high), pick(even, came(high), emit(1)))
    for_low = next_before, next_low, prev_low, prev_high
    for_high = next_low, next_high, prev_high, prev_after
    for i in range(4):
        own, other = pick(even, for_low[i], for_high[i]), pick(even, for_high[i], for_low[i])
        for part in range(2):
            mine[i, part] = own[part]
            theirs[i, part] = other[part]


def set_incoming(ref, mine, theirs, full, passage, media, near_media):
    inverses = [
        scale(coupling, pair(m, INVERSE))
        for m in (near_media.at[0], media, near_media.at[1])
    ]
    even = lax.rem(lax.axis_index("depth"), 2) == 0
    count = full.shape[2]
    split = Split(full.shape[3:])
    waves = []
    for i in range(4):
        parts = []
        for part in range(2):
            own, other = mine[i, part], theirs[i, part]
            first, second = split.unpack(
                jnp.where(even, own, other), jnp.where(even, other, own)
            )
            parts.append(jnp.stack([first, second], 1).reshape(full.shape[2:]))
        waves.append(tuple(parts))
    onward = add(cmul(passage, waves[1]), (full[0, 0], full[0, 1]))
    back = add(cmul(passage, waves[2]), (full[1, 0], full[1, 1]))
    spots = ((0, 0), (1, 0), (1, 1), (2, 1), (2, 0), (0, 1))
    for (side, way), value in zip(spots, [*waves, onward, back]):
        ref[side, way, 0], ref[side, way, 1] = cmul(inverses[side], value)


class Stage:
    def __init__(self, below, own, above):
        self.below, self.own, self.above = below, own, above


def pipeline(stages, slab, carry, halfway, by_plane):
    offsets = [LAG * (len(stages) - 1 - i) for i in range(len(stages))]
    trips = (slab - offsets[0]) // UNROLL

    def run(i, p, carry):
        out = stages[i].own(p, carry)
        return carry if out is None else out

    def own(i, start, stop, carry):
        body = lambda p, c: run(i, p, c)
        if start == 0 and stop > 0:
            carry = body(0, carry)
            start = 1
        if stop == slab and start < slab:
            return body(slab - 1, loop(start, slab - 1, body, carry))
        return loop(start, stop, body, carry)

    stages[0].below()
    stages[0].above()
    for i, stage in enumerate(stages):
        if i:
            stage.below()
        carry = own(i, 0, offsets[i], carry)

    def trip(t, carry):
        pairs = [(i, u) for i in range(len(stages)) for u in range(UNROLL)]
        if by_plane:
            pairs.sort(key=lambda pair: pair[1])
        for i, u in pairs:
            carry = run(i, t * UNROLL + offsets[i] + u, carry)
        return carry

    first = trips // 2
    carry = lax.fori_loop(0, first, trip, carry)
    halfway(0, [first * UNROLL + o for o in offsets])
    carry = lax.fori_loop(first, trips, trip, carry)
    halfway(1, [trips * UNROLL + o for o in offsets])
    for i, stage in enumerate(stages):
        carry = own(i, trips * UNROLL + offsets[i], slab, carry)
        if i:
            stage.above()
    return carry


def update_stages(
    reach, slab, tile, incoming, residual_of, media, near_media, power, waves,
    refs, emit, masks,
):
    edge = DEEP - 1
    first_update = Field(refs[0], -reach, tile[0])
    second_update = Field(refs[1], 1 - reach, tile[0])
    first_update.clear()
    second_update.clear()
    powers = (
        lambda p: (tile_of(waves, 0, 0, p + edge), tile_of(waves, 0, 1, p + edge)),
        lambda p: (tile_of(power, p + 1), tile_of(power, slab - p)),
        lambda p: (tile_of(waves, 1, 0, p - slab), tile_of(waves, 1, 1, p - slab)),
    )
    coefficients = near_media.at[0], media, near_media.at[1]
    first_lanes = Lanes(first_update, masks)
    second_lanes = Lanes(second_update, masks)

    def begin(which, p):
        on, off = powers[which](p)
        onward = incoming[which, 0, 0], incoming[which, 0, 1]
        back = incoming[which, 1, 0], incoming[which, 1, 1]
        c = add(cmul(on, onward), cmul(off, back))
        first_update.put_both(p, add(c, residual_of(which, p)))

    def second(which, p):
        here, total = first_update.around(p, first_lanes.now)
        smoothed = cmul(pair(coefficients[which], SECOND), total)
        second_update.put_both(p, add(here, smoothed))

    def third(which, p):
        here, total = second_update.around(p, second_lanes.now)
        smoothed = cmul(pair(coefficients[which], THIRD), total)
        u = add(scale(keep * (1.0 + keep), here), smoothed)
        emit(which, p, add(u, first_update.both(p)))

    def stage(body, margin):
        def beyond(which, a, b):
            for p in range(a, b):
                body(which, p)

        return Stage(
            lambda: beyond(0, margin - reach, 0),
            lambda p, unused: body(1, p),
            lambda: beyond(2, slab, slab + reach - margin),
        )

    return [stage(begin, 0), stage(second, 1), stage(third, 2)]


def middle_kernel(start, send, given, made, rest):
    (
        mine, theirs, plan, full, sources, pack, near_media, waves, near,
        near_residual, power, residual, guess,
    ) = given
    media = media_of(pack)
    new_field, new_residual, next_full, slots = made
    incoming, *refs = rest
    _, count, slab, height, breadth = guess.shape
    tile = (height, breadth)
    masks = lane_masks(tile)
    reach = DEEP - 1
    ext = reach - 2
    more = ext - 1
    new = Field(refs[2], -ext, height)
    new.clear()
    set_incoming(
        incoming, mine, theirs, full, tile_of(power, slab), media, near_media
    )

    def residual_of(which, p):
        if which == 1:
            r = residual[0, :, p], residual[1, :, p]
            lacks = None
            if isinstance(p, int) and p == 0:
                lacks = near[0, 0, :, DEEP - 1], near[0, 1, :, DEEP - 1]
            if isinstance(p, int) and p == slab - 1:
                lacks = near[1, 0, :, 0], near[1, 1, :, 0]
            return r if lacks is None else add(r, cmul(pair(media, INVERSE), lacks))
        i = p + reach if which == 0 else p - slab
        return near_residual[which // 2, 0, :, i], near_residual[which // 2, 1, :, i]

    def emit(which, p, u):
        for part in range(2):
            if which == 1:
                value = guess[part, :, p] + u[part]
                new_field[part, :, p] = value
            else:
                i = p + DEEP if which == 0 else p - slab
                value = near[which // 2, part, :, i] + u[part]
            new.put(part, p, value)

    stages = update_stages(
        reach, slab, tile, incoming, residual_of, media, near_media, power, waves,
        refs, emit, masks,
    )

    layer3 = media[LAYER]
    factor = pair(media, WAVE)
    lanes = Lanes(new, masks)

    def residual_at(p, diagonal):
        r = new.minus_a(p, diagonal, layer3, lanes.now)
        for part in range(2):
            new_residual[part, :, p + more] = r[part]
        return r

    def beyond(side, a, b):
        for p in range(a, b):
            residual_at(p, near_media[side, DIAGONAL])

    def inside(p, carry):
        toward_next, toward_prev = carry
        r = residual_at(p, media[DIAGONAL])
        toward_next = add(cmul(factor, toward_next), r)
        toward_prev = add(toward_prev, cmul(tile_of(power, p), r))
        return toward_next, toward_prev

    stages.append(
        Stage(lambda: beyond(0, -more, 0), inside, lambda: beyond(1, slab, slab + more))
    )
    zero = jnp.zeros((count,) + tile, jnp.float32)
    carry = pipeline(
        stages, slab, ((zero, zero), (zero, zero)), lambda i, reached: None, True
    )
    for way in range(2):
        for part in range(2):
            next_full[way, part] = carry[way][part]
    plan = plan.wait()
    force_emits(plan, next_full, sources, power, slab)
    fill_send(slots, next_full, None)
    add_forcing(plan, new_residual, sources, more, slab)


def scale_kernel(start, send, given, made, rest):
    residual, pack, near_media = given
    (out,) = made
    planes = residual.shape[2]
    reach = DEEP - 4

    def one(p, m):
        value = cmul(pair(m, INVERSE), (residual[0, :, p], residual[1, :, p]))
        out[0, :, p], out[1, :, p] = value

    media = media_of(pack)
    for p in range(reach):
        one(p, near_media.at[0])
        one(planes - 1 - p, near_media.at[1])
    loop(reach, planes - reach, lambda p, c: one(p, media) or c, 0, 8)


def final_kernel(start, send, given, made, rest):
    (
        mine, theirs, full, pack, near_media, waves, power, residual, field,
    ) = given
    (out,) = made
    media = media_of(pack)
    held, incoming, *refs = rest
    _, count, slab, height, breadth = field.shape
    tile = (height, breadth)
    reach = 2
    masks = lane_masks(tile)
    set_incoming(
        incoming, mine, theirs, full, tile_of(power, slab), media, near_media
    )

    def residual_of(which, p):
        return residual[0, :, p + reach], residual[1, :, p + reach]

    def emit(which, p, u):
        for part in range(2):
            held[part, :, p] = field[part, :, p] + u[part]

    stages = update_stages(
        reach, slab, tile, incoming, residual_of, media, near_media, power, waves,
        refs, emit, masks,
    )
    sent = [0]

    def send_field(top):
        part = pl.ds(sent[0], top - sent[0])
        send(held.at[:, :, part], out.at[:, :, part])
        sent[0] = top

    pipeline(stages, slab, 0, lambda i, reached: send_field(reached[2]), False)
    send_field(slab)


def local(sources, plan, absorb, labels, region_kk, damp_cells, guess):
    size = lax.axis_size("depth")
    _, count, slab, height, breadth = guess.shape
    tile = (height, breadth)
    edge = DEEP - 1
    planes = lambda n: (2, count, n) + tile
    scratch = lambda shape: pltpu.VMEM(shape, jnp.float32)

    tiles = (side_tiles(count) + 2,) + tile
    for_odd, base = kernel_call(
        pack_kernel,
        [
            (region_kk, "smem"), (damp_cells, "smem"), (absorb, "vmem"),
            (labels, "vmem"), (guess, "hbm"),
        ],
        [(tiles, "direct"), ((MEDIA + 2,) + tile, "direct")],
        pieces=2 * count, cost=1_000_000, name="pack", limit=4,
    )
    even_pairs = [(i, i ^ 1) for i in range(size)]
    odd_pairs = [(i, i + 1) for i in range(1, size - 1, 2)]
    odd_pairs += [(b, a) for a, b in odd_pairs]
    got_odd = lax.ppermute(for_odd, "depth", odd_pairs)

    residual, pack, power, for_even = kernel_call(
        start_kernel,
        [
            (plan, "smem"), (sources, "vmem"), (base, "direct"), (guess, "direct"),
        ],
        [
            (planes(slab), "direct"), ((MEDIA + 4 + 4 * count,) + tile, "direct"),
            ((slab + 1, 2) + tile, "direct"), (tiles, "direct"),
        ],
        [
            scratch((2, 2, count) + tile), Field.shape(count, slab + 2, tile),
        ],
        cost=20_000_000, name="start", limit=12,
    )
    got_even = lax.ppermute(for_even, "depth", even_pairs)
    width = count // 2
    full, slots, near, extra = kernel_call(
        arrange_kernel,
        [(got_even, "direct"), (got_odd, "direct"), (pack, "direct")],
        [
            ((2, 2, count) + tile, "direct"), ((size, 2 * width + 1) + tile, "direct"),
            ((2, 2, count, DEEP) + tile, "direct"), ((2, 3) + tile, "direct"),
        ],
        cost=1_000_000, name="arrange", limit=4,
    )
    first_got = lax.all_to_all(slots, "depth", 0, 0)
    near_residual, near_media, waves = kernel_call(
        prepare_kernel,
        [
            (plan, "smem"), (near, "direct"), (extra, "direct"),
            (sources, "direct"), (guess, "direct"),
        ],
        [
            ((2, 2, count, edge) + tile, "direct"), ((2, MEDIA) + tile, "direct"),
            ((2, 2, edge, 2) + tile, "direct"),
        ],
        [Field.shape(count, DEEP + 1, tile)],
        cost=4_000_000, name="prepare", limit=4,
    )

    def chain(got, full):
        mine, theirs = kernel_call(
            chain_kernel,
            [(got, "direct"), (first_got, "direct"), (full, "direct")],
            [((4, 2, width) + tile, "direct")] * 2,
            cost=1_000_000, name="chain", limit=4,
        )
        return mine, lax.ppermute(theirs, "depth", even_pairs)

    mine, theirs = chain(first_got, full)
    new_field, new_residual, next_full, slots = kernel_call(
        middle_kernel,
        [
            (mine, "direct"), (theirs, "direct"),
            (plan, "smem"), (full, "direct"), (sources, "direct"),
            (pack, "direct"), (near_media, "direct"), (waves, "direct"),
            (near, "direct"), (near_residual, "direct"), (power, "direct"),
            (residual, "direct"), (guess, "direct"),
        ],
        [
            (planes(slab), "direct"), (planes(slab + 2 * (DEEP - 4)), "direct"),
            ((2, 2, count) + tile, "direct"), ((size, 2 * width) + tile, "direct"),
        ],
        [
            scratch((3, 2, 2, count) + tile),
            Field.shape(count, slab + 2 * edge, tile),
            Field.shape(count, slab + 2 * edge - 2, tile),
            Field.shape(count, slab + 2 * edge - 4, tile),
        ],
        cost=80_000_000, name="middle", limit=20,
    )
    mine, theirs = chain(lax.all_to_all(slots, "depth", 0, 0), next_full)
    (scaled,) = kernel_call(
        scale_kernel,
        [(new_residual, "direct"), (pack, "direct"), (near_media, "direct")],
        [(planes(slab + 2 * (DEEP - 4)), "direct")],
        cost=4_000_000, name="scale", limit=4,
    )
    (out,) = kernel_call(
        final_kernel,
        [
            (mine, "direct"), (theirs, "direct"), (next_full, "direct"),
            (pack, "direct"), (near_media, "direct"), (waves, "direct"),
            (power, "direct"), (scaled, "direct"), (new_field, "direct"),
        ],
        [(planes(slab), "hbm")],
        [
            scratch(planes(slab)), scratch((3, 2, 2, count) + tile),
            Field.shape(count, slab + 4, tile), Field.shape(count, slab + 2, tile),
        ],
        pieces=3, cost=60_000_000, name="final", limit=16,
    )
    return out


def solution(mesh):
    return jax.shard_map(
        local,
        mesh=mesh,
        in_specs=(
            P(None, "groups", None, None),
            P("groups"),
            P("depth", "groups", None),
            P("depth", "groups", None),
            P(),
            P("groups"),
            P(None, "groups", "depth", None, None),
        ),
        out_specs=P(None, "groups", "depth", None, None),
        check_vma=False,
    )
```

```python
import functools

import jax
import jax.numpy as jnp
from jax import lax
from jax.experimental import pallas as pl
from jax.experimental.pallas import tpu as pltpu
from jax.sharding import PartitionSpec as P

relax_weight = 0.8
shift_ratio = 0.5
damping = 3.0
coupling = 0.25
keep = 1.0 - relax_weight

DEEP = 6
UNROLL = 4
LAG = UNROLL + 1


def cmul(a, b):
    return a[0] * b[0] - a[1] * b[1], a[0] * b[1] + a[1] * b[0]


def add(a, b):
    return a[0] + b[0], a[1] + b[1]


def scale(c, a):
    return c * a[0], c * a[1]


def pick(cond, a, b):
    return jnp.where(cond, a[0], b[0]), jnp.where(cond, a[1], b[1])


def tile_of(ref, *at):
    return ref[at + (0,)], ref[at + (1,)]


class Inward:
    def __init__(self, source, target, sem):
        self.ref = target
        self.copy = pltpu.make_async_copy(source, target, sem)
        self.copy.start()

    def wait(self):
        self.copy.wait()
        return self.ref


def kernel_call(body, inputs, outputs, scratch=(), pieces=0, cost=0, name=None, limit=56):
    n_in, n_out = len(inputs), len(outputs)
    pinned = ("hbm", "vmem", "smem")
    extra = []
    for array, place in inputs:
        if place in ("vmem", "smem"):
            space = pltpu.SMEM if place == "smem" else pltpu.VMEM
            extra.append(space(array.shape, array.dtype))
    for shape, place in outputs:
        if place == "vmem":
            extra.append(pltpu.VMEM(shape, jnp.float32))
    n_extra = len(extra)

    def kernel(*refs):
        ins, outs = refs[:n_in], refs[n_in : n_in + n_out]
        buffers = iter(refs[n_in + n_out : n_in + n_out + n_extra])
        sems = refs[n_in + n_out + n_extra]
        rest = refs[n_in + n_out + n_extra + 1 :]
        used = iter(range(n_extra + pieces))
        pending = []

        def start(source, target):
            return Inward(source, target, sems.at[next(used)])

        def send(source, target):
            pending.append(start(source, target))

        def arrive():
            given = []
            for ref, (_, place) in zip(ins, inputs):
                copied = place in ("vmem", "smem")
                given.append(start(ref, next(buffers)) if copied else ref)
            return given

        given = arrive()
        made = []
        for ref, (_, place) in zip(outs, outputs):
            if place != "vmem":
                made.append(ref)
            else:
                buffer = next(buffers)
                made.append((buffer, functools.partial(send, buffer, ref)))
        body(start, send, given, made, rest)
        for copy in pending:
            copy.wait()

    def spec(place):
        return pl.BlockSpec(memory_space=pltpu.VMEM if place == "direct" else pltpu.HBM)

    return pl.pallas_call(
        kernel,
        out_shape=tuple(jax.ShapeDtypeStruct(s, jnp.float32) for s, _ in outputs),
        in_specs=[spec(place) for _, place in inputs],
        out_specs=tuple(spec(place) for _, place in outputs),
        scratch_shapes=[
            *extra,
            pltpu.SemaphoreType.DMA((max(1, n_extra + pieces),)),
            *scratch,
        ],
        compiler_params=pltpu.CompilerParams(vmem_limit_bytes=limit << 20),
        cost_estimate=pl.CostEstimate(
            flops=cost, bytes_accessed=4 << 20, transcendentals=0
        ),
        name=name,
    )(*[
        pltpu.with_memory_space_constraint(array, pltpu.HBM) if place in pinned else array
        for array, place in inputs
    ])


def lane_sum(here, masks):
    breadth = here.shape[-1]
    axis = here.ndim - 1
    ahead = jnp.where(masks[0], pltpu.roll(here, 1, axis), 0.0)
    behind = jnp.where(masks[1], pltpu.roll(here, breadth - 1, axis), 0.0)
    return ahead + behind


class Field:
    def __init__(self, ref, first, height):
        self.ref, self.first, self.height = ref, first, height

    @staticmethod
    def shape(count, planes, tile):
        return pltpu.VMEM((2, count, (2 * planes + 1) * tile[0], tile[1]), jnp.float32)

    def rows(self, plane, shift=0):
        start = (2 * (plane - self.first) + 1) * self.height + shift
        if shift % self.height == 0:
            start = pl.multiple_of(start, self.height)
        return pl.ds(start, self.height)

    def clear(self):
        edge = self.ref[:, :, : self.height]
        self.ref[:, :, : self.height] = jnp.zeros_like(edge)

    def get(self, part, plane, shift=0):
        return self.ref[part, :, self.rows(plane, shift)]

    def both(self, plane):
        return self.get(0, plane), self.get(1, plane)

    def put(self, part, plane, value):
        self.ref[part, :, self.rows(plane)] = value
        self.ref[part, :, self.rows(plane, self.height)] = jnp.zeros_like(value)

    def put_both(self, plane, value):
        for part in range(2):
            self.put(part, plane, value[part])

    def bump(self, plane, s, value):
        for part in range(2):
            self.ref[part, s, self.rows(plane)] += value[part]

    def lanes(self, part, plane, masks):
        return lane_sum(self.get(part, plane), masks)

    def around(self, plane, lanes):
        heres, totals = [], []
        for part in range(2):
            here = self.get(part, plane)
            beside = self.get(part, plane, -1) + self.get(part, plane, 1)
            depth = self.get(part, plane - 1) + self.get(part, plane + 1)
            heres.append(here)
            totals.append((beside + depth) + lanes(part, plane))
        return tuple(heres), tuple(totals)

    def minus_a(self, plane, diagonal, layer3, lanes):
        here, total = self.around(plane, lanes)
        return (
            (total[0] - diagonal * here[0]) + layer3 * here[1],
            (total[1] - diagonal * here[1]) - layer3 * here[0],
        )


class Lanes:
    def __init__(self, field, masks):
        self.field, self.masks = field, masks

    def now(self, part, plane):
        return self.field.lanes(part, plane, self.masks)


def lane_masks(tile):
    lane = lax.broadcasted_iota(jnp.int32, tile, 1)
    return lane > 0, lane < tile[1] - 1


INVERSE, DIAGONAL, LAYER, WAVE, SECOND, THIRD, MEDIA = 0, 2, 3, 4, 6, 8, 10


def wave(absorb, squared, order, slab):
    decay = jnp.exp(-order * absorb / slab)
    angle = order * jnp.sqrt(squared)
    return decay * jnp.cos(angle), decay * jnp.sin(angle)


def set_media(ref, squared, layer, absorb, slab, inside=None):
    diagonal = 6.0 - squared
    imag = shift_ratio * squared + damping * layer
    size = diagonal * diagonal + imag * imag
    inverse = relax_weight * diagonal / size, -relax_weight * imag / size
    if inside is not None:
        inverse = tuple(jnp.where(inside, v, 0.0) for v in inverse)
    grow = 1.0 + keep
    factor = wave(absorb, squared, 1, slab)
    values = (
        *inverse, diagonal, damping * layer, *factor,
        *scale(1.0 / grow, inverse), *scale(grow, inverse),
    )
    for i, value in enumerate(values):
        ref[i] = value
    return factor


def pair(ref, i):
    return ref[i], ref[i + 1]


def region_values(labels, kk_ref):
    squared = jnp.zeros(labels.shape, jnp.float32)
    for region in range(kk_ref.shape[0]):
        squared = jnp.where(labels == region, kk_ref[region], squared)
    return squared


def loop(start, stop, body, carry, unroll=UNROLL):
    trips = (stop - start) // unroll

    def several(trip, carry):
        for i in range(unroll):
            carry = body(start + trip * unroll + i, carry)
        return carry

    if trips > 1:
        carry = lax.fori_loop(0, trips, several, carry)
        start += trips * unroll
    for plane in range(start, stop):
        carry = body(plane, carry)
    return carry


def media_of(pack):
    return pack.at[pl.ds(0, MEDIA)]


def emit_tiles(count, way, part):
    return pl.ds(MEDIA + 4 + (2 * way + part) * count, count)


def side_tiles(count):
    return 2 * count * DEEP


def pack_kernel(start, send, given, made, rest):
    kk, damp, absorb, labels, guess = given
    out, base = made
    _, count, slab, *tile = guess.shape
    even = lax.rem(lax.axis_index("depth"), 2) == 0
    first = jnp.where(even, 0, slab - DEEP)
    for i in range(2 * count):
        send(
            guess.at[i // count, i % count, pl.ds(first, DEEP)],
            out.at[pl.ds(i * DEEP, DEEP)],
        )
    row = lax.broadcasted_iota(jnp.int32, tuple(tile), 0)
    lane = lax.broadcasted_iota(jnp.int32, tuple(tile), 1)
    cell = row * tile[1] + lane
    kk, absorb, labels = kk.wait(), absorb.wait(), labels.wait()
    squared = region_values(labels[0], kk)
    out[side_tiles(count)] = absorb[0]
    out[side_tiles(count) + 1] = squared
    base[MEDIA] = absorb[0]
    base[MEDIA + 1] = squared
    damp = damp.wait()

    def mark(i, hit):
        return jnp.where(cell == damp[i], 1.0, hit)

    layer = loop(0, damp.shape[0], mark, jnp.zeros(tile, jnp.float32), 16)
    set_media(base, squared, layer, absorb[0], slab)


def start_kernel(start, send, given, made, rest):
    plan, sources, base, guess = given
    residual, pack, power, for_even = made
    emits, ref = rest
    _, count, slab, height, breadth = guess.shape
    tile = (height, breadth)
    media = media_of(pack)
    media[...] = base[:MEDIA]
    masks = lane_masks(tile)
    field = Field(ref, -1, height)
    zero = jnp.zeros((count,) + tile, jnp.float32)
    field.clear()
    field.put_both(-1, (zero, zero))
    field.put_both(slab, (zero, zero))
    lanes = Lanes(field, masks)
    diagonal, layer3 = media[DIAGONAL], media[LAYER]
    inverse, factor = pair(media, INVERSE), pair(media, WAVE)

    def fill(p):
        for part in range(2):
            field.put(part, p, guess[part, :, p])

    def plane(k, carry):
        toward_next, toward_prev, w = carry
        power[k, 0], power[k, 1] = w
        r = field.minus_a(k, diagonal, layer3, lanes.now)
        residual[0, :, k], residual[1, :, k] = cmul(inverse, r)
        toward_next = add(cmul(factor, toward_next), r)
        toward_prev = add(toward_prev, cmul(w, r))
        return toward_next, toward_prev, cmul(factor, w)

    one = jnp.ones(tile, jnp.float32), jnp.zeros(tile, jnp.float32)
    carry = ((zero, zero), (zero, zero), one)
    fill(0)

    def group(trip, carry):
        base = trip * UNROLL
        for i in range(UNROLL):
            fill(base + i + 1)
        for i in range(UNROLL):
            carry = plane(base + i, carry)
        return carry

    trips = (slab - 1) // UNROLL
    carry = lax.fori_loop(0, trips, group, carry)
    for k in range(trips * UNROLL, slab):
        if k + 1 < slab:
            fill(k + 1)
        carry = plane(k, carry)
    plan, sources = plan.wait(), sources.wait()
    toward_next, toward_prev, _ = carry
    power[slab, 0], power[slab, 1] = wave(*pair(base, MEDIA), slab, slab)
    add_forcing(plan, residual, sources, 0, slab, inverse)
    for part in range(2):
        emits[0, part] = toward_next[part]
        emits[1, part] = toward_prev[part]
        pack[MEDIA + part] = power[slab - 1, part]
        pack[MEDIA + 2 + part] = power[slab, part]
    force_emits(plan, emits, sources, power, slab)
    for way in range(2):
        for part in range(2):
            pack[emit_tiles(count, way, part)] = emits[way, part]
    first_plane = jnp.where(lax.rem(lax.axis_index("depth"), 2) == 0, slab - DEEP, 0)
    for i in range(2 * count):
        for_even[pl.ds(i * DEEP, DEEP)] = guess[
            i // count, i % count, pl.ds(first_plane, DEEP)
        ]
    for_even[pl.ds(side_tiles(count), 2)] = base[MEDIA : MEDIA + 2]


def add_forcing(plan, held, sources, reach, slab, inverse=None):
    first_plane = lax.axis_index("depth") * slab
    for s in range(sources.shape[1]):
        k = plan[s] - first_plane

        @pl.when((k >= -reach) & (k < slab + reach))
        def _():
            src = sources[0, s], sources[1, s]
            if inverse is not None:
                src = cmul(inverse, src)
            for part in range(2):
                held[part, s, k + reach] += src[part]


def force_emits(plan, emits, sources, power, slab):
    first_plane = lax.axis_index("depth") * slab
    for s in range(sources.shape[1]):
        k = plan[s] - first_plane

        @pl.when((k >= 0) & (k < slab))
        def _():
            src = sources[0, s], sources[1, s]
            onward = cmul(tile_of(power, slab - 1 - k), src)
            back = cmul(tile_of(power, k), src)
            for part in range(2):
                emits[0, part, s] += onward[part]
                emits[1, part, s] += back[part]


class Split:
    def __init__(self, tile):
        self.half = tile[0] // 2
        self.upper = lax.broadcasted_iota(jnp.int32, tile, 0) < self.half

    def turn(self, value):
        return pltpu.roll(value, self.half, value.ndim - 2)

    def pack(self, core, first, second):
        if core == 0:
            return jnp.where(self.upper, first, self.turn(second))
        return jnp.where(self.upper, self.turn(first), second)

    def unpack(self, core_0, core_1):
        first = jnp.where(self.upper, core_0, self.turn(core_1))
        second = jnp.where(self.upper, self.turn(core_0), core_1)
        return first, second

    def spread(self, packed):
        turned = self.turn(packed)
        return jnp.where(self.upper, packed, turned), jnp.where(self.upper, turned, packed)


def pack_waves(split, core, full, way):
    count = full.shape[2]
    return tuple(
        jnp.stack(
            [
                split.pack(core, full[way, part, s], full[way, part, s + 1])
                for s in range(0, count, 2)
            ]
        )
        for part in range(2)
    )


def fill_send(slots, full, passage):
    place = lax.axis_index("depth")
    width = full.shape[2] // 2
    split = Split(full.shape[3:])
    waves = [[pack_waves(split, core, full, way) for way in range(2)] for core in range(2)]

    def one(chip, unused):
        for core in range(2):
            j = 2 * chip + core
            onward, back = waves[core]
            for part in range(2):
                slots[j, pl.ds(part * width, width)] = jnp.where(
                    j > place, onward[part], back[part]
                )
            if passage is not None:
                slots[j, 2 * width] = split.pack(core, *passage)
        return unused

    loop(0, slots.shape[0] // 2, one, 0, 4)


def arrange_kernel(start, send, given, made, rest):
    got_even, got_odd, pack = given
    full, slots, near, extra = made
    even = lax.rem(lax.axis_index("depth"), 2) == 0
    count = full.shape[2]
    weight, passage = pair(pack, MEDIA), pair(pack, MEDIA + 2)
    emits = [[pack[emit_tiles(count, way, part)] for part in range(2)] for way in range(2)]
    for s in range(count):
        at = [(part * count + s) * DEEP for part in range(2)]
        low = tuple(
            jnp.where(even, got_odd[i + DEEP - 1], got_even[i + DEEP - 1]) for i in at
        )
        high = tuple(jnp.where(even, got_even[i], got_odd[i]) for i in at)
        toward_next = add(add(cmul(weight, low), high), (emits[0][0][s], emits[0][1][s]))
        toward_prev = add(add(cmul(weight, high), low), (emits[1][0][s], emits[1][1][s]))
        for part in range(2):
            full[0, part, s] = toward_next[part]
            full[1, part, s] = toward_prev[part]
    fill_send(slots, full, passage)
    for side in range(2):
        first, second = (got_odd, got_even) if side == 0 else (got_even, got_odd)
        for i in range(2 * count):
            rows = pl.ds(i * DEEP, DEEP)
            near[side, i // count, i % count] = jnp.where(
                even, first[rows], second[rows]
            )
        for i in range(2):
            at = 2 * count * DEEP + i
            extra[side, i] = jnp.where(even, first[at], second[at])
    extra[0, 2] = extra[1, 2] = media_of(pack)[LAYER]


def prepare_kernel(start, send, given, made, rest):
    plan, near, extra, sources, guess = given
    res, near_media, waves = made
    (ref,) = rest
    _, count, slab, height, breadth = guess.shape
    tile = (height, breadth)
    masks = lane_masks(tile)
    place = lax.axis_index("depth")
    last_place = lax.axis_size("depth") - 1
    layer3 = extra[0, 2]
    layer = layer3 / damping
    factors = []
    for side in range(2):
        squared = extra[side, 1]
        inside = (place > 0) if side == 0 else (place < last_place)
        factors.append(
            set_media(near_media.at[side], squared, layer, extra[side, 0], slab, inside)
        )

    ws = list(factors)
    edge = DEEP - 1

    def keep_power(k, ws):
        for side in range(2):
            for way in range(2):
                if side == way:
                    i = k - (slab - edge + 1)
                    i = edge - 1 - i if side else i
                else:
                    i = k - 1
                    i = i if side else edge - 1 - i
                if 0 <= i < edge:
                    for part in range(2):
                        waves[side, way, i, part] = ws[side][part]

    def next_power(k, ws):
        return tuple(cmul(factors[side], ws[side]) for side in range(2))

    k = 1
    while k <= slab:
        if edge < k < slab - edge + 1:
            ws = loop(k, slab - edge + 1, next_power, tuple(ws), 8)
            k = slab - edge + 1
        keep_power(k, ws)
        ws = next_power(k, ws)
        k += 1
    for side in range(2):
        field = Field(ref, 0, height)
        field.clear()
        for i in range(DEEP + 1):
            for part in range(2):
                if side == 0:
                    value = near[0, part, :, i] if i < DEEP else guess[part, :, 0]
                else:
                    value = near[1, part, :, i - 1] if i > 0 else guess[part, :, slab - 1]
                field.put(part, i, value)
        lanes = Lanes(field, masks)
        for i in range(1, DEEP):
            r = field.minus_a(i, near_media[side, DIAGONAL], layer3, lanes.now)
            r = cmul(pair(near_media.at[side], INVERSE), r)
            for part in range(2):
                res[side, part, :, i - 1] = r[part]
    plan = plan.wait()
    for s in range(count):
        k = plan[s] - place * slab
        for side, low in ((0, -edge), (1, slab)):
            i = k - low

            @pl.when((i >= 0) & (i < edge))
            def _():
                src = sources[0, s], sources[1, s]
                src = cmul(pair(near_media.at[side], INVERSE), src)
                for part in range(2):
                    res[side, part, s, i] += src[part]


def chain_kernel(start, send, given, made, rest):
    got, passages, full = given
    mine, theirs = made
    place = lax.axis_index("depth")
    last_place = lax.axis_size("depth") - 1
    width = full.shape[2] // 2
    split = Split(full.shape[3:])
    even = lax.rem(place, 2) == 0
    low = place - lax.rem(place, 2)
    high = low + 1
    zero = jnp.zeros((width,) + full.shape[3:], jnp.float32)
    passage = lambda j: split.spread(passages[j, 2 * width])
    emit = lambda way: pick(
        even, pack_waves(split, 0, full, way), pack_waves(split, 1, full, way)
    )
    came = lambda j: (got[j, pl.ds(0, width)], got[j, pl.ds(width, width)])

    def step(j, state):
        return add(cmul(passage(j), state), came(j))

    below = jnp.maximum(low - 1, 0)
    above = jnp.minimum(high + 1, last_place)
    next_before = lax.fori_loop(0, below, step, (zero, zero))
    next_low = pick(low > 0, step(below, next_before), (zero, zero))
    next_high = add(cmul(passage(low), next_low), pick(even, emit(0), came(low)))
    prev_after = lax.fori_loop(
        0, last_place - above, lambda t, state: step(last_place - t, state), (zero, zero)
    )
    prev_high = pick(high < last_place, step(above, prev_after), (zero, zero))
    prev_low = add(cmul(passage(high), prev_high), pick(even, came(high), emit(1)))
    for_low = next_before, next_low, prev_low, prev_high
    for_high = next_low, next_high, prev_high, prev_after
    for i in range(4):
        own, other = pick(even, for_low[i], for_high[i]), pick(even, for_high[i], for_low[i])
        for part in range(2):
            mine[i, part] = own[part]
            theirs[i, part] = other[part]


def set_incoming(ref, mine, theirs, full, passage, media, near_media):
    inverses = [
        scale(coupling, pair(m, INVERSE))
        for m in (near_media.at[0], media, near_media.at[1])
    ]
    even = lax.rem(lax.axis_index("depth"), 2) == 0
    count = full.shape[2]
    split = Split(full.shape[3:])
    waves = []
    for i in range(4):
        parts = []
        for part in range(2):
            own, other = mine[i, part], theirs[i, part]
            first, second = split.unpack(
                jnp.where(even, own, other), jnp.where(even, other, own)
            )
            parts.append(jnp.stack([first, second], 1).reshape(full.shape[2:]))
        waves.append(tuple(parts))
    onward = add(cmul(passage, waves[1]), (full[0, 0], full[0, 1]))
    back = add(cmul(passage, waves[2]), (full[1, 0], full[1, 1]))
    spots = ((0, 0), (1, 0), (1, 1), (2, 1), (2, 0), (0, 1))
    for (side, way), value in zip(spots, [*waves, onward, back]):
        ref[side, way, 0], ref[side, way, 1] = cmul(inverses[side], value)


class Stage:
    def __init__(self, below, own, above):
        self.below, self.own, self.above = below, own, above


def pipeline(stages, slab, carry, halfway):
    offsets = [LAG * (len(stages) - 1 - i) for i in range(len(stages))]
    trips = (slab - offsets[0]) // UNROLL

    def run(i, p, carry):
        out = stages[i].own(p, carry)
        return carry if out is None else out

    def own(i, start, stop, carry):
        body = lambda p, c: run(i, p, c)
        if start == 0 and stop > 0:
            carry = body(0, carry)
            start = 1
        if stop == slab and start < slab:
            return body(slab - 1, loop(start, slab - 1, body, carry))
        return loop(start, stop, body, carry)

    stages[0].below()
    stages[0].above()
    for i, stage in enumerate(stages):
        if i:
            stage.below()
        carry = own(i, 0, offsets[i], carry)

    def trip(t, carry):
        for i in reversed(range(len(stages))):
            for u in range(UNROLL):
                carry = run(i, t * UNROLL + offsets[i] + u, carry)
        return carry

    first = trips // 2
    carry = lax.fori_loop(0, first, trip, carry)
    halfway(0, [first * UNROLL + o for o in offsets])
    carry = lax.fori_loop(first, trips, trip, carry)
    halfway(1, [trips * UNROLL + o for o in offsets])
    for i, stage in enumerate(stages):
        carry = own(i, trips * UNROLL + offsets[i], slab, carry)
        if i:
            stage.above()
    return carry


def update_stages(
    reach, slab, tile, incoming, residual_of, media, near_media, power, waves,
    refs, emit, masks,
):
    edge = DEEP - 1
    first_update = Field(refs[0], -reach, tile[0])
    second_update = Field(refs[1], 1 - reach, tile[0])
    first_update.clear()
    second_update.clear()
    powers = (
        lambda p: (tile_of(waves, 0, 0, p + edge), tile_of(waves, 0, 1, p + edge)),
        lambda p: (tile_of(power, p + 1), tile_of(power, slab - p)),
        lambda p: (tile_of(waves, 1, 0, p - slab), tile_of(waves, 1, 1, p - slab)),
    )
    coefficients = near_media.at[0], media, near_media.at[1]
    first_lanes = Lanes(first_update, masks)
    second_lanes = Lanes(second_update, masks)

    def begin(which, p):
        on, off = powers[which](p)
        onward = incoming[which, 0, 0], incoming[which, 0, 1]
        back = incoming[which, 1, 0], incoming[which, 1, 1]
        c = add(cmul(on, onward), cmul(off, back))
        first_update.put_both(p, add(c, residual_of(which, p)))

    def second(which, p):
        here, total = first_update.around(p, first_lanes.now)
        smoothed = cmul(pair(coefficients[which], SECOND), total)
        second_update.put_both(p, add(here, smoothed))

    def third(which, p):
        here, total = second_update.around(p, second_lanes.now)
        smoothed = cmul(pair(coefficients[which], THIRD), total)
        u = add(scale(keep * (1.0 + keep), here), smoothed)
        emit(which, p, add(u, first_update.both(p)))

    def stage(body, margin):
        def beyond(which, a, b):
            for p in range(a, b):
                body(which, p)

        return Stage(
            lambda: beyond(0, margin - reach, 0),
            lambda p, unused: body(1, p),
            lambda: beyond(2, slab, slab + reach - margin),
        )

    return [stage(begin, 0), stage(second, 1), stage(third, 2)]


def middle_kernel(start, send, given, made, rest):
    (
        mine, theirs, plan, full, sources, pack, near_media, waves, near,
        near_residual, power, residual, guess,
    ) = given
    media = media_of(pack)
    new_field, new_near, new_residual, next_full, slots = made
    incoming, *refs = rest
    _, count, slab, height, breadth = guess.shape
    tile = (height, breadth)
    masks = lane_masks(tile)
    reach = DEEP - 1
    ext = reach - 2
    new = Field(refs[2], -ext, height)
    new.clear()
    set_incoming(
        incoming, mine, theirs, full, tile_of(power, slab), media, near_media
    )

    def residual_of(which, p):
        if which == 1:
            r = residual[0, :, p], residual[1, :, p]
            lacks = None
            if isinstance(p, int) and p == 0:
                lacks = near[0, 0, :, DEEP - 1], near[0, 1, :, DEEP - 1]
            if isinstance(p, int) and p == slab - 1:
                lacks = near[1, 0, :, 0], near[1, 1, :, 0]
            return r if lacks is None else add(r, cmul(pair(media, INVERSE), lacks))
        i = p + reach if which == 0 else p - slab
        return near_residual[which // 2, 0, :, i], near_residual[which // 2, 1, :, i]

    def emit(which, p, u):
        for part in range(2):
            if which == 1:
                value = guess[part, :, p] + u[part]
                new_field[part, :, p] = value
            else:
                i = p + DEEP if which == 0 else p - slab
                value = near[which // 2, part, :, i] + u[part]
                new_near[which // 2, part, :, p + ext if which == 0 else i] = value
            new.put(part, p, value)

    stages = update_stages(
        reach, slab, tile, incoming, residual_of, media, near_media, power, waves,
        refs, emit, masks,
    )

    layer3 = media[LAYER]
    factor = pair(media, WAVE)
    lanes = Lanes(new, masks)

    def residual_at(p, diagonal):
        r = new.minus_a(p, diagonal, layer3, lanes.now)
        for part in range(2):
            new_residual[part, :, p] = r[part]
        return r

    def inside(p, carry):
        toward_next, toward_prev = carry
        r = residual_at(p, media[DIAGONAL])
        toward_next = add(cmul(factor, toward_next), r)
        toward_prev = add(toward_prev, cmul(tile_of(power, p), r))
        return toward_next, toward_prev

    nothing = lambda: None
    stages.append(Stage(nothing, inside, nothing))
    zero = jnp.zeros((count,) + tile, jnp.float32)
    carry = pipeline(stages, slab, ((zero, zero), (zero, zero)), lambda i, reached: None)
    for way in range(2):
        for part in range(2):
            next_full[way, part] = carry[way][part]
    plan = plan.wait()
    force_emits(plan, next_full, sources, power, slab)
    fill_send(slots, next_full, None)
    add_forcing(plan, new_residual, sources, 0, slab)


def scale_kernel(start, send, given, made, rest):
    plan, residual, field, new_near, pack, near_media, sources = given
    (out,) = made
    (ref,) = rest
    _, count, slab, height, breadth = residual.shape
    reach = DEEP - 4
    ext = reach + 1
    masks = lane_masks((height, breadth))
    media = media_of(pack)

    def put(p, m, r):
        out[0, :, p + reach], out[1, :, p + reach] = cmul(pair(m, INVERSE), r)

    loop(
        0, slab, lambda p, c: put(p, media, (residual[0, :, p], residual[1, :, p])) or c, 0, 8
    )
    for side in range(2):
        beside = Field(ref, 0, height)
        beside.clear()
        for i in range(ext + 1):
            for part in range(2):
                if side == 0:
                    value = new_near[0, part, :, i] if i < ext else field[part, :, 0]
                else:
                    value = new_near[1, part, :, i - 1] if i else field[part, :, slab - 1]
                beside.put(part, i, value)
        m = near_media.at[side]
        lanes = Lanes(beside, masks)
        for i in range(1, ext):
            p = i - ext if side == 0 else slab + i - 1
            put(p, m, beside.minus_a(i, m[DIAGONAL], media[LAYER], lanes.now))
    plan = plan.wait()
    first_plane = lax.axis_index("depth") * slab
    for s in range(count):
        k = plan[s] - first_plane
        for side, low in ((0, -reach), (1, slab)):

            @pl.when((k >= low) & (k < low + reach))
            def _():
                src = sources[0, s], sources[1, s]
                src = cmul(pair(near_media.at[side], INVERSE), src)
                for part in range(2):
                    out[part, s, k + reach] += src[part]


def final_kernel(start, send, given, made, rest):
    (
        mine, theirs, full, pack, near_media, waves, power, residual, field,
    ) = given
    (out,) = made
    media = media_of(pack)
    held, incoming, *refs = rest
    _, count, slab, height, breadth = field.shape
    tile = (height, breadth)
    reach = 2
    masks = lane_masks(tile)
    set_incoming(
        incoming, mine, theirs, full, tile_of(power, slab), media, near_media
    )

    def residual_of(which, p):
        return residual[0, :, p + reach], residual[1, :, p + reach]

    def emit(which, p, u):
        for part in range(2):
            held[part, :, p] = field[part, :, p] + u[part]

    stages = update_stages(
        reach, slab, tile, incoming, residual_of, media, near_media, power, waves,
        refs, emit, masks,
    )
    sent = [0]

    def send_field(top):
        part = pl.ds(sent[0], top - sent[0])
        send(held.at[:, :, part], out.at[:, :, part])
        sent[0] = top

    pipeline(stages, slab, 0, lambda i, reached: send_field(reached[2]))
    send_field(slab)


def local(sources, plan, absorb, labels, region_kk, damp_cells, guess):
    size = lax.axis_size("depth")
    _, count, slab, height, breadth = guess.shape
    tile = (height, breadth)
    edge = DEEP - 1
    planes = lambda n: (2, count, n) + tile
    scratch = lambda shape: pltpu.VMEM(shape, jnp.float32)

    tiles = (side_tiles(count) + 2,) + tile
    for_odd, base = kernel_call(
        pack_kernel,
        [
            (region_kk, "smem"), (damp_cells, "smem"), (absorb, "vmem"),
            (labels, "vmem"), (guess, "hbm"),
        ],
        [(tiles, "direct"), ((MEDIA + 2,) + tile, "direct")],
        pieces=2 * count, cost=1_000_000, name="pack", limit=4,
    )
    even_pairs = [(i, i ^ 1) for i in range(size)]
    odd_pairs = [(i, i + 1) for i in range(1, size - 1, 2)]
    odd_pairs += [(b, a) for a, b in odd_pairs]
    got_odd = lax.ppermute(for_odd, "depth", odd_pairs)

    residual, pack, power, for_even = kernel_call(
        start_kernel,
        [
            (plan, "smem"), (sources, "vmem"), (base, "direct"), (guess, "direct"),
        ],
        [
            (planes(slab), "direct"), ((MEDIA + 4 + 4 * count,) + tile, "direct"),
            ((slab + 1, 2) + tile, "direct"), (tiles, "direct"),
        ],
        [
            scratch((2, 2, count) + tile), Field.shape(count, slab + 2, tile),
        ],
        cost=20_000_000, name="start", limit=12,
    )
    got_even = lax.ppermute(for_even, "depth", even_pairs)
    width = count // 2
    full, slots, near, extra = kernel_call(
        arrange_kernel,
        [(got_even, "direct"), (got_odd, "direct"), (pack, "direct")],
        [
            ((2, 2, count) + tile, "direct"), ((size, 2 * width + 1) + tile, "direct"),
            ((2, 2, count, DEEP) + tile, "direct"), ((2, 3) + tile, "direct"),
        ],
        cost=1_000_000, name="arrange", limit=4,
    )
    first_got = lax.all_to_all(slots, "depth", 0, 0)
    near_residual, near_media, waves = kernel_call(
        prepare_kernel,
        [
            (plan, "smem"), (near, "direct"), (extra, "direct"),
            (sources, "direct"), (guess, "direct"),
        ],
        [
            ((2, 2, count, edge) + tile, "direct"), ((2, MEDIA) + tile, "direct"),
            ((2, 2, edge, 2) + tile, "direct"),
        ],
        [Field.shape(count, DEEP + 1, tile)],
        cost=4_000_000, name="prepare", limit=4,
    )

    def chain(got, full):
        mine, theirs = kernel_call(
            chain_kernel,
            [(got, "direct"), (first_got, "direct"), (full, "direct")],
            [((4, 2, width) + tile, "direct")] * 2,
            cost=1_000_000, name="chain", limit=4,
        )
        return mine, lax.ppermute(theirs, "depth", even_pairs)

    mine, theirs = chain(first_got, full)
    new_field, new_near, new_residual, next_full, slots = kernel_call(
        middle_kernel,
        [
            (mine, "direct"), (theirs, "direct"),
            (plan, "smem"), (full, "direct"), (sources, "direct"),
            (pack, "direct"), (near_media, "direct"), (waves, "direct"),
            (near, "direct"), (near_residual, "direct"), (power, "direct"),
            (residual, "direct"), (guess, "direct"),
        ],
        [
            (planes(slab), "direct"), ((2, 2, count, DEEP - 3) + tile, "direct"),
            (planes(slab), "direct"),
            ((2, 2, count) + tile, "direct"), ((size, 2 * width) + tile, "direct"),
        ],
        [
            scratch((3, 2, 2, count) + tile),
            Field.shape(count, slab + 2 * edge, tile),
            Field.shape(count, slab + 2 * edge - 2, tile),
            Field.shape(count, slab + 2 * edge - 4, tile),
        ],
        cost=80_000_000, name="middle", limit=20,
    )
    mine, theirs = chain(lax.all_to_all(slots, "depth", 0, 0), next_full)
    (scaled,) = kernel_call(
        scale_kernel,
        [
            (plan, "smem"), (new_residual, "direct"), (new_field, "direct"),
            (new_near, "direct"), (pack, "direct"), (near_media, "direct"),
            (sources, "direct"),
        ],
        [(planes(slab + 2 * (DEEP - 4)), "direct")],
        [Field.shape(count, DEEP - 2, tile)],
        cost=4_000_000, name="scale", limit=4,
    )
    (out,) = kernel_call(
        final_kernel,
        [
            (mine, "direct"), (theirs, "direct"), (next_full, "direct"),
            (pack, "direct"), (near_media, "direct"), (waves, "direct"),
            (power, "direct"), (scaled, "direct"), (new_field, "direct"),
        ],
        [(planes(slab), "hbm")],
        [
            scratch(planes(slab)), scratch((3, 2, 2, count) + tile),
            Field.shape(count, slab + 4, tile), Field.shape(count, slab + 2, tile),
        ],
        pieces=3, cost=60_000_000, name="final", limit=16,
    )
    return out


def solution(mesh):
    return jax.shard_map(
        local,
        mesh=mesh,
        in_specs=(
            P(None, "groups", None, None),
            P("groups"),
            P("depth", "groups", None),
            P("depth", "groups", None),
            P(),
            P("groups"),
            P(None, "groups", "depth", None, None),
        ),
        out_specs=P(None, "groups", "depth", None, None),
        check_vma=False,
    )
```

```python
import functools

import jax
import jax.numpy as jnp
from jax import lax
from jax.experimental import pallas as pl
from jax.experimental.pallas import tpu as pltpu
from jax.sharding import PartitionSpec as P

relax_weight = 0.8
shift_ratio = 0.5
damping = 3.0
coupling = 0.25
keep = 1.0 - relax_weight

DEEP = 6
UNROLL = 8
LAG = UNROLL + 1


def cmul(a, b):
    return a[0] * b[0] - a[1] * b[1], a[0] * b[1] + a[1] * b[0]


def add(a, b):
    return a[0] + b[0], a[1] + b[1]


def scale(c, a):
    return c * a[0], c * a[1]


def pick(cond, a, b):
    return jnp.where(cond, a[0], b[0]), jnp.where(cond, a[1], b[1])


def tile_of(ref, *at):
    return ref[at + (0,)], ref[at + (1,)]


class Inward:
    def __init__(self, source, target, sem):
        self.ref = target
        self.copy = pltpu.make_async_copy(source, target, sem)
        self.copy.start()

    def wait(self):
        self.copy.wait()
        return self.ref


def kernel_call(body, inputs, outputs, scratch=(), pieces=0, cost=0, name=None, limit=56):
    n_in, n_out = len(inputs), len(outputs)
    pinned = ("hbm", "vmem", "smem")
    extra = []
    for array, place in inputs:
        if place in ("vmem", "smem"):
            space = pltpu.SMEM if place == "smem" else pltpu.VMEM
            extra.append(space(array.shape, array.dtype))
    for shape, place in outputs:
        if place == "vmem":
            extra.append(pltpu.VMEM(shape, jnp.float32))
    n_extra = len(extra)

    def kernel(*refs):
        ins, outs = refs[:n_in], refs[n_in : n_in + n_out]
        buffers = iter(refs[n_in + n_out : n_in + n_out + n_extra])
        sems = refs[n_in + n_out + n_extra]
        rest = refs[n_in + n_out + n_extra + 1 :]
        used = iter(range(n_extra + pieces))
        pending = []

        def start(source, target):
            return Inward(source, target, sems.at[next(used)])

        def send(source, target):
            pending.append(start(source, target))

        def arrive():
            given = []
            for ref, (_, place) in zip(ins, inputs):
                copied = place in ("vmem", "smem")
                given.append(start(ref, next(buffers)) if copied else ref)
            return given

        given = arrive()
        made = []
        for ref, (_, place) in zip(outs, outputs):
            if place != "vmem":
                made.append(ref)
            else:
                buffer = next(buffers)
                made.append((buffer, functools.partial(send, buffer, ref)))
        body(start, send, given, made, rest)
        for copy in pending:
            copy.wait()

    def spec(place):
        return pl.BlockSpec(memory_space=pltpu.VMEM if place == "direct" else pltpu.HBM)

    return pl.pallas_call(
        kernel,
        out_shape=tuple(jax.ShapeDtypeStruct(s, jnp.float32) for s, _ in outputs),
        in_specs=[spec(place) for _, place in inputs],
        out_specs=tuple(spec(place) for _, place in outputs),
        scratch_shapes=[
            *extra,
            pltpu.SemaphoreType.DMA((max(1, n_extra + pieces),)),
            *scratch,
        ],
        compiler_params=pltpu.CompilerParams(vmem_limit_bytes=limit << 20),
        cost_estimate=pl.CostEstimate(
            flops=cost, bytes_accessed=4 << 20, transcendentals=0
        ),
        name=name,
    )(*[
        pltpu.with_memory_space_constraint(array, pltpu.HBM) if place in pinned else array
        for array, place in inputs
    ])


def lane_sum(here, masks):
    breadth = here.shape[-1]
    axis = here.ndim - 1
    ahead = jnp.where(masks[0], pltpu.roll(here, 1, axis), 0.0)
    behind = jnp.where(masks[1], pltpu.roll(here, breadth - 1, axis), 0.0)
    return ahead + behind


class Field:
    def __init__(self, ref, first, height):
        self.ref, self.first, self.height = ref, first, height

    @staticmethod
    def shape(count, planes, tile):
        return pltpu.VMEM((2, count, (2 * planes + 1) * tile[0], tile[1]), jnp.float32)

    def rows(self, plane, shift=0):
        start = (2 * (plane - self.first) + 1) * self.height + shift
        if shift % self.height == 0:
            start = pl.multiple_of(start, self.height)
        return pl.ds(start, self.height)

    def clear(self):
        edge = self.ref[:, :, : self.height]
        self.ref[:, :, : self.height] = jnp.zeros_like(edge)

    def get(self, part, plane, shift=0):
        return self.ref[part, :, self.rows(plane, shift)]

    def both(self, plane):
        return self.get(0, plane), self.get(1, plane)

    def put(self, part, plane, value):
        self.ref[part, :, self.rows(plane)] = value
        self.ref[part, :, self.rows(plane, self.height)] = jnp.zeros_like(value)

    def put_both(self, plane, value):
        for part in range(2):
            self.put(part, plane, value[part])

    def bump(self, plane, s, value):
        for part in range(2):
            self.ref[part, s, self.rows(plane)] += value[part]

    def lanes(self, part, plane, masks):
        return lane_sum(self.get(part, plane), masks)

    def around(self, plane, lanes):
        heres, totals = [], []
        for part in range(2):
            here = self.get(part, plane)
            beside = self.get(part, plane, -1) + self.get(part, plane, 1)
            depth = self.get(part, plane - 1) + self.get(part, plane + 1)
            heres.append(here)
            totals.append((beside + depth) + lanes(part, plane))
        return tuple(heres), tuple(totals)

    def minus_a(self, plane, diagonal, layer3, lanes):
        here, total = self.around(plane, lanes)
        return (
            (total[0] - diagonal * here[0]) + layer3 * here[1],
            (total[1] - diagonal * here[1]) - layer3 * here[0],
        )


class Lanes:
    def __init__(self, field, masks):
        self.field, self.masks = field, masks

    def now(self, part, plane):
        return self.field.lanes(part, plane, self.masks)


def lane_masks(tile):
    lane = lax.broadcasted_iota(jnp.int32, tile, 1)
    return lane > 0, lane < tile[1] - 1


INVERSE, DIAGONAL, LAYER, WAVE, SECOND, THIRD, MEDIA = 0, 2, 3, 4, 6, 8, 10


def wave(absorb, squared, order, slab):
    decay = jnp.exp(-order * absorb / slab)
    angle = order * jnp.sqrt(squared)
    return decay * jnp.cos(angle), decay * jnp.sin(angle)


def set_media(ref, squared, layer, absorb, slab, inside=None):
    diagonal = 6.0 - squared
    imag = shift_ratio * squared + damping * layer
    size = diagonal * diagonal + imag * imag
    inverse = relax_weight * diagonal / size, -relax_weight * imag / size
    if inside is not None:
        inverse = tuple(jnp.where(inside, v, 0.0) for v in inverse)
    grow = 1.0 + keep
    factor = wave(absorb, squared, 1, slab)
    values = (
        *inverse, diagonal, damping * layer, *factor,
        *scale(1.0 / grow, inverse), *scale(grow, inverse),
    )
    for i, value in enumerate(values):
        ref[i] = value
    return factor


def pair(ref, i):
    return ref[i], ref[i + 1]


def region_values(labels, kk_ref):
    squared = jnp.zeros(labels.shape, jnp.float32)
    for region in range(kk_ref.shape[0]):
        squared = jnp.where(labels == region, kk_ref[region], squared)
    return squared


def loop(start, stop, body, carry, unroll=UNROLL):
    trips = (stop - start) // unroll

    def several(trip, carry):
        for i in range(unroll):
            carry = body(start + trip * unroll + i, carry)
        return carry

    if trips > 1:
        carry = lax.fori_loop(0, trips, several, carry)
        start += trips * unroll
    for plane in range(start, stop):
        carry = body(plane, carry)
    return carry


def media_of(pack):
    return pack.at[pl.ds(0, MEDIA)]


def emit_tiles(count, way, part):
    return pl.ds(MEDIA + 4 + (2 * way + part) * count, count)


def side_tiles(count):
    return 2 * count * DEEP


def pack_kernel(start, send, given, made, rest):
    kk, damp, absorb, labels, guess = given
    out, base = made
    _, count, slab, *tile = guess.shape
    even = lax.rem(lax.axis_index("depth"), 2) == 0
    first = jnp.where(even, 0, slab - DEEP)
    for i in range(2 * count):
        send(
            guess.at[i // count, i % count, pl.ds(first, DEEP)],
            out.at[pl.ds(i * DEEP, DEEP)],
        )
    row = lax.broadcasted_iota(jnp.int32, tuple(tile), 0)
    lane = lax.broadcasted_iota(jnp.int32, tuple(tile), 1)
    cell = row * tile[1] + lane
    kk, absorb, labels = kk.wait(), absorb.wait(), labels.wait()
    squared = region_values(labels[0], kk)
    out[side_tiles(count)] = absorb[0]
    out[side_tiles(count) + 1] = squared
    base[MEDIA] = absorb[0]
    base[MEDIA + 1] = squared
    damp = damp.wait()

    def mark(i, hit):
        return jnp.where(cell == damp[i], 1.0, hit)

    layer = loop(0, damp.shape[0], mark, jnp.zeros(tile, jnp.float32), 16)
    set_media(base, squared, layer, absorb[0], slab)


def start_kernel(start, send, given, made, rest):
    plan, sources, base, guess = given
    residual, pack, power, for_even = made
    emits, ref = rest
    _, count, slab, height, breadth = guess.shape
    tile = (height, breadth)
    media = media_of(pack)
    media[...] = base[:MEDIA]
    masks = lane_masks(tile)
    field = Field(ref, -1, height)
    zero = jnp.zeros((count,) + tile, jnp.float32)
    field.clear()
    field.put_both(-1, (zero, zero))
    field.put_both(slab, (zero, zero))
    lanes = Lanes(field, masks)
    diagonal, layer3 = media[DIAGONAL], media[LAYER]
    inverse, factor = pair(media, INVERSE), pair(media, WAVE)

    def fill(p):
        for part in range(2):
            field.put(part, p, guess[part, :, p])

    def plane(k, carry):
        toward_next, toward_prev, w = carry
        power[k, 0], power[k, 1] = w
        r = field.minus_a(k, diagonal, layer3, lanes.now)
        residual[0, :, k], residual[1, :, k] = cmul(inverse, r)
        toward_next = add(cmul(factor, toward_next), r)
        toward_prev = add(toward_prev, cmul(w, r))
        return toward_next, toward_prev, cmul(factor, w)

    one = jnp.ones(tile, jnp.float32), jnp.zeros(tile, jnp.float32)
    carry = ((zero, zero), (zero, zero), one)
    fill(0)

    def group(trip, carry):
        base = trip * UNROLL
        for i in range(UNROLL):
            fill(base + i + 1)
        for i in range(UNROLL):
            carry = plane(base + i, carry)
        return carry

    trips = (slab - 1) // UNROLL
    carry = lax.fori_loop(0, trips, group, carry)
    for k in range(trips * UNROLL, slab):
        if k + 1 < slab:
            fill(k + 1)
        carry = plane(k, carry)
    plan, sources = plan.wait(), sources.wait()
    toward_next, toward_prev, _ = carry
    power[slab, 0], power[slab, 1] = wave(*pair(base, MEDIA), slab, slab)
    add_forcing(plan, residual, sources, 0, slab, inverse)
    for part in range(2):
        emits[0, part] = toward_next[part]
        emits[1, part] = toward_prev[part]
        pack[MEDIA + part] = power[slab - 1, part]
        pack[MEDIA + 2 + part] = power[slab, part]
    force_emits(plan, emits, sources, power, slab)
    for way in range(2):
        for part in range(2):
            pack[emit_tiles(count, way, part)] = emits[way, part]
    first_plane = jnp.where(lax.rem(lax.axis_index("depth"), 2) == 0, slab - DEEP, 0)
    for i in range(2 * count):
        for_even[pl.ds(i * DEEP, DEEP)] = guess[
            i // count, i % count, pl.ds(first_plane, DEEP)
        ]
    for_even[pl.ds(side_tiles(count), 2)] = base[MEDIA : MEDIA + 2]


def add_forcing(plan, held, sources, reach, slab, inverse=None):
    first_plane = lax.axis_index("depth") * slab
    for s in range(sources.shape[1]):
        k = plan[s] - first_plane

        @pl.when((k >= -reach) & (k < slab + reach))
        def _():
            src = sources[0, s], sources[1, s]
            if inverse is not None:
                src = cmul(inverse, src)
            for part in range(2):
                held[part, s, k + reach] += src[part]


def force_emits(plan, emits, sources, power, slab):
    first_plane = lax.axis_index("depth") * slab
    for s in range(sources.shape[1]):
        k = plan[s] - first_plane

        @pl.when((k >= 0) & (k < slab))
        def _():
            src = sources[0, s], sources[1, s]
            onward = cmul(tile_of(power, slab - 1 - k), src)
            back = cmul(tile_of(power, k), src)
            for part in range(2):
                emits[0, part, s] += onward[part]
                emits[1, part, s] += back[part]


class Split:
    def __init__(self, tile):
        self.half = tile[0] // 2
        self.upper = lax.broadcasted_iota(jnp.int32, tile, 0) < self.half

    def turn(self, value):
        return pltpu.roll(value, self.half, value.ndim - 2)

    def pack(self, core, first, second):
        if core == 0:
            return jnp.where(self.upper, first, self.turn(second))
        return jnp.where(self.upper, self.turn(first), second)

    def unpack(self, core_0, core_1):
        first = jnp.where(self.upper, core_0, self.turn(core_1))
        second = jnp.where(self.upper, self.turn(core_0), core_1)
        return first, second

    def spread(self, packed):
        turned = self.turn(packed)
        return jnp.where(self.upper, packed, turned), jnp.where(self.upper, turned, packed)


def pack_waves(split, core, full, way):
    count = full.shape[2]
    return tuple(
        jnp.stack(
            [
                split.pack(core, full[way, part, s], full[way, part, s + 1])
                for s in range(0, count, 2)
            ]
        )
        for part in range(2)
    )


def fill_send(slots, full, passage):
    place = lax.axis_index("depth")
    width = full.shape[2] // 2
    split = Split(full.shape[3:])
    waves = [[pack_waves(split, core, full, way) for way in range(2)] for core in range(2)]

    def one(chip, unused):
        for core in range(2):
            j = 2 * chip + core
            onward, back = waves[core]
            for part in range(2):
                slots[j, pl.ds(part * width, width)] = jnp.where(
                    j > place, onward[part], back[part]
                )
            if passage is not None:
                slots[j, 2 * width] = split.pack(core, *passage)
        return unused

    loop(0, slots.shape[0] // 2, one, 0, 4)


def arrange_kernel(start, send, given, made, rest):
    got_even, got_odd, pack = given
    full, slots, near, extra = made
    even = lax.rem(lax.axis_index("depth"), 2) == 0
    count = full.shape[2]
    weight, passage = pair(pack, MEDIA), pair(pack, MEDIA + 2)
    emits = [[pack[emit_tiles(count, way, part)] for part in range(2)] for way in range(2)]
    for s in range(count):
        at = [(part * count + s) * DEEP for part in range(2)]
        low = tuple(
            jnp.where(even, got_odd[i + DEEP - 1], got_even[i + DEEP - 1]) for i in at
        )
        high = tuple(jnp.where(even, got_even[i], got_odd[i]) for i in at)
        toward_next = add(add(cmul(weight, low), high), (emits[0][0][s], emits[0][1][s]))
        toward_prev = add(add(cmul(weight, high), low), (emits[1][0][s], emits[1][1][s]))
        for part in range(2):
            full[0, part, s] = toward_next[part]
            full[1, part, s] = toward_prev[part]
    fill_send(slots, full, passage)
    for side in range(2):
        first, second = (got_odd, got_even) if side == 0 else (got_even, got_odd)
        for i in range(2 * count):
            rows = pl.ds(i * DEEP, DEEP)
            near[side, i // count, i % count] = jnp.where(
                even, first[rows], second[rows]
            )
        for i in range(2):
            at = 2 * count * DEEP + i
            extra[side, i] = jnp.where(even, first[at], second[at])
    extra[0, 2] = extra[1, 2] = media_of(pack)[LAYER]


def prepare_kernel(start, send, given, made, rest):
    plan, near, extra, sources, guess = given
    res, near_media, waves = made
    (ref,) = rest
    _, count, slab, height, breadth = guess.shape
    tile = (height, breadth)
    masks = lane_masks(tile)
    place = lax.axis_index("depth")
    last_place = lax.axis_size("depth") - 1
    layer3 = extra[0, 2]
    layer = layer3 / damping
    factors = []
    for side in range(2):
        squared = extra[side, 1]
        inside = (place > 0) if side == 0 else (place < last_place)
        factors.append(
            set_media(near_media.at[side], squared, layer, extra[side, 0], slab, inside)
        )

    ws = list(factors)
    edge = DEEP - 1

    def keep_power(k, ws):
        for side in range(2):
            for way in range(2):
                if side == way:
                    i = k - (slab - edge + 1)
                    i = edge - 1 - i if side else i
                else:
                    i = k - 1
                    i = i if side else edge - 1 - i
                if 0 <= i < edge:
                    for part in range(2):
                        waves[side, way, i, part] = ws[side][part]

    def next_power(k, ws):
        return tuple(cmul(factors[side], ws[side]) for side in range(2))

    k = 1
    while k <= slab:
        if edge < k < slab - edge + 1:
            ws = loop(k, slab - edge + 1, next_power, tuple(ws), 8)
            k = slab - edge + 1
        keep_power(k, ws)
        ws = next_power(k, ws)
        k += 1
    for side in range(2):
        field = Field(ref, 0, height)
        field.clear()
        for i in range(DEEP + 1):
            for part in range(2):
                if side == 0:
                    value = near[0, part, :, i] if i < DEEP else guess[part, :, 0]
                else:
                    value = near[1, part, :, i - 1] if i > 0 else guess[part, :, slab - 1]
                field.put(part, i, value)
        lanes = Lanes(field, masks)
        for i in range(1, DEEP):
            r = field.minus_a(i, near_media[side, DIAGONAL], layer3, lanes.now)
            r = cmul(pair(near_media.at[side], INVERSE), r)
            for part in range(2):
                res[side, part, :, i - 1] = r[part]
    plan = plan.wait()
    for s in range(count):
        k = plan[s] - place * slab
        for side, low in ((0, -edge), (1, slab)):
            i = k - low

            @pl.when((i >= 0) & (i < edge))
            def _():
                src = sources[0, s], sources[1, s]
                src = cmul(pair(near_media.at[side], INVERSE), src)
                for part in range(2):
                    res[side, part, s, i] += src[part]


def chain_kernel(start, send, given, made, rest):
    got, passages, full = given
    mine, theirs = made
    place = lax.axis_index("depth")
    last_place = lax.axis_size("depth") - 1
    width = full.shape[2] // 2
    split = Split(full.shape[3:])
    even = lax.rem(place, 2) == 0
    low = place - lax.rem(place, 2)
    high = low + 1
    zero = jnp.zeros((width,) + full.shape[3:], jnp.float32)
    passage = lambda j: split.spread(passages[j, 2 * width])
    emit = lambda way: pick(
        even, pack_waves(split, 0, full, way), pack_waves(split, 1, full, way)
    )
    came = lambda j: (got[j, pl.ds(0, width)], got[j, pl.ds(width, width)])

    def step(j, state):
        return add(cmul(passage(j), state), came(j))

    below = jnp.maximum(low - 1, 0)
    above = jnp.minimum(high + 1, last_place)
    next_before = lax.fori_loop(0, below, step, (zero, zero))
    next_low = pick(low > 0, step(below, next_before), (zero, zero))
    next_high = add(cmul(passage(low), next_low), pick(even, emit(0), came(low)))
    prev_after = lax.fori_loop(
        0, last_place - above, lambda t, state: step(last_place - t, state), (zero, zero)
    )
    prev_high = pick(high < last_place, step(above, prev_after), (zero, zero))
    prev_low = add(cmul(passage(high), prev_high), pick(even, came(high), emit(1)))
    for_low = next_before, next_low, prev_low, prev_high
    for_high = next_low, next_high, prev_high, prev_after
    for i in range(4):
        own, other = pick(even, for_low[i], for_high[i]), pick(even, for_high[i], for_low[i])
        for part in range(2):
            mine[i, part] = own[part]
            theirs[i, part] = other[part]


def set_incoming(ref, mine, theirs, full, passage, media, near_media):
    inverses = [
        scale(coupling, pair(m, INVERSE))
        for m in (near_media.at[0], media, near_media.at[1])
    ]
    even = lax.rem(lax.axis_index("depth"), 2) == 0
    count = full.shape[2]
    split = Split(full.shape[3:])
    waves = []
    for i in range(4):
        parts = []
        for part in range(2):
            own, other = mine[i, part], theirs[i, part]
            first, second = split.unpack(
                jnp.where(even, own, other), jnp.where(even, other, own)
            )
            parts.append(jnp.stack([first, second], 1).reshape(full.shape[2:]))
        waves.append(tuple(parts))
    onward = add(cmul(passage, waves[1]), (full[0, 0], full[0, 1]))
    back = add(cmul(passage, waves[2]), (full[1, 0], full[1, 1]))
    spots = ((0, 0), (1, 0), (1, 1), (2, 1), (2, 0), (0, 1))
    for (side, way), value in zip(spots, [*waves, onward, back]):
        ref[side, way, 0], ref[side, way, 1] = cmul(inverses[side], value)


class Stage:
    def __init__(self, below, own, above):
        self.below, self.own, self.above = below, own, above


def pipeline(stages, slab, carry, halfway):
    offsets = [LAG * (len(stages) - 1 - i) for i in range(len(stages))]
    trips = (slab - offsets[0]) // UNROLL

    def run(i, p, carry):
        out = stages[i].own(p, carry)
        return carry if out is None else out

    def own(i, start, stop, carry):
        body = lambda p, c: run(i, p, c)
        if start == 0 and stop > 0:
            carry = body(0, carry)
            start = 1
        if stop == slab and start < slab:
            return body(slab - 1, loop(start, slab - 1, body, carry))
        return loop(start, stop, body, carry)

    stages[0].below()
    stages[0].above()
    for i, stage in enumerate(stages):
        if i:
            stage.below()
        carry = own(i, 0, offsets[i], carry)

    def trip(t, carry):
        for i in reversed(range(len(stages))):
            for u in range(UNROLL):
                carry = run(i, t * UNROLL + offsets[i] + u, carry)
        return carry

    first = 0
    if halfway is not None:
        first = trips // 2
        carry = lax.fori_loop(0, first, trip, carry)
        halfway(0, [first * UNROLL + o for o in offsets])
    carry = lax.fori_loop(first, trips, trip, carry)
    if halfway is not None:
        halfway(1, [trips * UNROLL + o for o in offsets])
    for i, stage in enumerate(stages):
        carry = own(i, trips * UNROLL + offsets[i], slab, carry)
        if i:
            stage.above()
    return carry


def update_stages(
    reach, slab, tile, incoming, residual_of, media, near_media, power, waves,
    refs, emit, masks,
):
    edge = DEEP - 1
    first_update = Field(refs[0], -reach, tile[0])
    second_update = Field(refs[1], 1 - reach, tile[0])
    first_update.clear()
    second_update.clear()
    powers = (
        lambda p: (tile_of(waves, 0, 0, p + edge), tile_of(waves, 0, 1, p + edge)),
        lambda p: (tile_of(power, p + 1), tile_of(power, slab - p)),
        lambda p: (tile_of(waves, 1, 0, p - slab), tile_of(waves, 1, 1, p - slab)),
    )
    coefficients = near_media.at[0], media, near_media.at[1]
    first_lanes = Lanes(first_update, masks)
    second_lanes = Lanes(second_update, masks)

    def begin(which, p):
        on, off = powers[which](p)
        onward = incoming[which, 0, 0], incoming[which, 0, 1]
        back = incoming[which, 1, 0], incoming[which, 1, 1]
        c = add(cmul(on, onward), cmul(off, back))
        first_update.put_both(p, add(c, residual_of(which, p)))

    def second(which, p):
        here, total = first_update.around(p, first_lanes.now)
        smoothed = cmul(pair(coefficients[which], SECOND), total)
        second_update.put_both(p, add(here, smoothed))

    def third(which, p):
        here, total = second_update.around(p, second_lanes.now)
        smoothed = cmul(pair(coefficients[which], THIRD), total)
        u = add(scale(keep * (1.0 + keep), here), smoothed)
        emit(which, p, add(u, first_update.both(p)))

    def stage(body, margin):
        def beyond(which, a, b):
            for p in range(a, b):
                body(which, p)

        return Stage(
            lambda: beyond(0, margin - reach, 0),
            lambda p, unused: body(1, p),
            lambda: beyond(2, slab, slab + reach - margin),
        )

    return [stage(begin, 0), stage(second, 1), stage(third, 2)]


def middle_kernel(start, send, given, made, rest):
    (
        mine, theirs, plan, full, sources, pack, near_media, waves, near,
        near_residual, power, residual, guess,
    ) = given
    media = media_of(pack)
    new_field, new_near, new_residual, next_full, slots = made
    incoming, *refs = rest
    _, count, slab, height, breadth = guess.shape
    tile = (height, breadth)
    masks = lane_masks(tile)
    reach = DEEP - 1
    ext = reach - 2
    new = Field(refs[2], -ext, height)
    new.clear()
    set_incoming(
        incoming, mine, theirs, full, tile_of(power, slab), media, near_media
    )

    def residual_of(which, p):
        if which == 1:
            r = residual[0, :, p], residual[1, :, p]
            lacks = None
            if isinstance(p, int) and p == 0:
                lacks = near[0, 0, :, DEEP - 1], near[0, 1, :, DEEP - 1]
            if isinstance(p, int) and p == slab - 1:
                lacks = near[1, 0, :, 0], near[1, 1, :, 0]
            return r if lacks is None else add(r, cmul(pair(media, INVERSE), lacks))
        i = p + reach if which == 0 else p - slab
        return near_residual[which // 2, 0, :, i], near_residual[which // 2, 1, :, i]

    def emit(which, p, u):
        for part in range(2):
            if which == 1:
                value = guess[part, :, p] + u[part]
                new_field[part, :, p] = value
            else:
                i = p + DEEP if which == 0 else p - slab
                value = near[which // 2, part, :, i] + u[part]
                new_near[which // 2, part, :, p + ext if which == 0 else i] = value
            new.put(part, p, value)

    stages = update_stages(
        reach, slab, tile, incoming, residual_of, media, near_media, power, waves,
        refs, emit, masks,
    )

    layer3 = media[LAYER]
    factor = pair(media, WAVE)
    lanes = Lanes(new, masks)

    def residual_at(p, diagonal):
        r = new.minus_a(p, diagonal, layer3, lanes.now)
        for part in range(2):
            new_residual[part, :, p] = r[part]
        return r

    def inside(p, carry):
        toward_next, toward_prev = carry
        r = residual_at(p, media[DIAGONAL])
        toward_next = add(cmul(factor, toward_next), r)
        toward_prev = add(toward_prev, cmul(tile_of(power, p), r))
        return toward_next, toward_prev

    nothing = lambda: None
    stages.append(Stage(nothing, inside, nothing))
    zero = jnp.zeros((count,) + tile, jnp.float32)
    carry = pipeline(stages, slab, ((zero, zero), (zero, zero)), None)
    for way in range(2):
        for part in range(2):
            next_full[way, part] = carry[way][part]
    plan = plan.wait()
    force_emits(plan, next_full, sources, power, slab)
    fill_send(slots, next_full, None)
    add_forcing(plan, new_residual, sources, 0, slab)


def scale_kernel(start, send, given, made, rest):
    plan, residual, field, new_near, pack, near_media, sources = given
    (out,) = made
    (ref,) = rest
    _, count, slab, height, breadth = residual.shape
    reach = DEEP - 4
    ext = reach + 1
    masks = lane_masks((height, breadth))
    media = media_of(pack)

    def put(p, m, r):
        out[0, :, p + reach], out[1, :, p + reach] = cmul(pair(m, INVERSE), r)

    loop(
        0, slab, lambda p, c: put(p, media, (residual[0, :, p], residual[1, :, p])) or c, 0, 8
    )
    for side in range(2):
        beside = Field(ref, 0, height)
        beside.clear()
        for i in range(ext + 1):
            for part in range(2):
                if side == 0:
                    value = new_near[0, part, :, i] if i < ext else field[part, :, 0]
                else:
                    value = new_near[1, part, :, i - 1] if i else field[part, :, slab - 1]
                beside.put(part, i, value)
        m = near_media.at[side]
        lanes = Lanes(beside, masks)
        for i in range(1, ext):
            p = i - ext if side == 0 else slab + i - 1
            put(p, m, beside.minus_a(i, m[DIAGONAL], media[LAYER], lanes.now))
    plan = plan.wait()
    first_plane = lax.axis_index("depth") * slab
    for s in range(count):
        k = plan[s] - first_plane
        for side, low in ((0, -reach), (1, slab)):

            @pl.when((k >= low) & (k < low + reach))
            def _():
                src = sources[0, s], sources[1, s]
                src = cmul(pair(near_media.at[side], INVERSE), src)
                for part in range(2):
                    out[part, s, k + reach] += src[part]


def final_kernel(start, send, given, made, rest):
    (
        mine, theirs, full, pack, near_media, waves, power, residual, field,
    ) = given
    (out,) = made
    media = media_of(pack)
    held, incoming, *refs = rest
    _, count, slab, height, breadth = field.shape
    tile = (height, breadth)
    reach = 2
    masks = lane_masks(tile)
    set_incoming(
        incoming, mine, theirs, full, tile_of(power, slab), media, near_media
    )

    def residual_of(which, p):
        return residual[0, :, p + reach], residual[1, :, p + reach]

    def emit(which, p, u):
        for part in range(2):
            held[part, :, p] = field[part, :, p] + u[part]

    stages = update_stages(
        reach, slab, tile, incoming, residual_of, media, near_media, power, waves,
        refs, emit, masks,
    )
    sent = [0]

    def send_field(top):
        part = pl.ds(sent[0], top - sent[0])
        send(held.at[:, :, part], out.at[:, :, part])
        sent[0] = top

    pipeline(stages, slab, 0, lambda i, reached: send_field(reached[2]))
    send_field(slab)


def local(sources, plan, absorb, labels, region_kk, damp_cells, guess):
    size = lax.axis_size("depth")
    _, count, slab, height, breadth = guess.shape
    tile = (height, breadth)
    edge = DEEP - 1
    planes = lambda n: (2, count, n) + tile
    scratch = lambda shape: pltpu.VMEM(shape, jnp.float32)

    tiles = (side_tiles(count) + 2,) + tile
    for_odd, base = kernel_call(
        pack_kernel,
        [
            (region_kk, "smem"), (damp_cells, "smem"), (absorb, "vmem"),
            (labels, "vmem"), (guess, "hbm"),
        ],
        [(tiles, "direct"), ((MEDIA + 2,) + tile, "direct")],
        pieces=2 * count, cost=1_000_000, name="pack", limit=4,
    )
    even_pairs = [(i, i ^ 1) for i in range(size)]
    odd_pairs = [(i, i + 1) for i in range(1, size - 1, 2)]
    odd_pairs += [(b, a) for a, b in odd_pairs]
    got_odd = lax.ppermute(for_odd, "depth", odd_pairs)

    residual, pack, power, for_even = kernel_call(
        start_kernel,
        [
            (plan, "smem"), (sources, "vmem"), (base, "direct"), (guess, "direct"),
        ],
        [
            (planes(slab), "direct"), ((MEDIA + 4 + 4 * count,) + tile, "direct"),
            ((slab + 1, 2) + tile, "direct"), (tiles, "direct"),
        ],
        [
            scratch((2, 2, count) + tile), Field.shape(count, slab + 2, tile),
        ],
        cost=20_000_000, name="start", limit=12,
    )
    got_even = lax.ppermute(for_even, "depth", even_pairs)
    width = count // 2
    full, slots, near, extra = kernel_call(
        arrange_kernel,
        [(got_even, "direct"), (got_odd, "direct"), (pack, "direct")],
        [
            ((2, 2, count) + tile, "direct"), ((size, 2 * width + 1) + tile, "direct"),
            ((2, 2, count, DEEP) + tile, "direct"), ((2, 3) + tile, "direct"),
        ],
        cost=1_000_000, name="arrange", limit=4,
    )
    first_got = lax.all_to_all(slots, "depth", 0, 0)
    near_residual, near_media, waves = kernel_call(
        prepare_kernel,
        [
            (plan, "smem"), (near, "direct"), (extra, "direct"),
            (sources, "direct"), (guess, "direct"),
        ],
        [
            ((2, 2, count, edge) + tile, "direct"), ((2, MEDIA) + tile, "direct"),
            ((2, 2, edge, 2) + tile, "direct"),
        ],
        [Field.shape(count, DEEP + 1, tile)],
        cost=4_000_000, name="prepare", limit=4,
    )

    def chain(got, full):
        mine, theirs = kernel_call(
            chain_kernel,
            [(got, "direct"), (first_got, "direct"), (full, "direct")],
            [((4, 2, width) + tile, "direct")] * 2,
            cost=1_000_000, name="chain", limit=4,
        )
        return mine, lax.ppermute(theirs, "depth", even_pairs)

    mine, theirs = chain(first_got, full)
    new_field, new_near, new_residual, next_full, slots = kernel_call(
        middle_kernel,
        [
            (mine, "direct"), (theirs, "direct"),
            (plan, "smem"), (full, "direct"), (sources, "direct"),
            (pack, "direct"), (near_media, "direct"), (waves, "direct"),
            (near, "direct"), (near_residual, "direct"), (power, "direct"),
            (residual, "direct"), (guess, "direct"),
        ],
        [
            (planes(slab), "direct"), ((2, 2, count, DEEP - 3) + tile, "direct"),
            (planes(slab), "direct"),
            ((2, 2, count) + tile, "direct"), ((size, 2 * width) + tile, "direct"),
        ],
        [
            scratch((3, 2, 2, count) + tile),
            Field.shape(count, slab + 2 * edge, tile),
            Field.shape(count, slab + 2 * edge - 2, tile),
            Field.shape(count, slab + 2 * edge - 4, tile),
        ],
        cost=80_000_000, name="middle", limit=20,
    )
    mine, theirs = chain(lax.all_to_all(slots, "depth", 0, 0), next_full)
    (scaled,) = kernel_call(
        scale_kernel,
        [
            (plan, "smem"), (new_residual, "direct"), (new_field, "direct"),
            (new_near, "direct"), (pack, "direct"), (near_media, "direct"),
            (sources, "direct"),
        ],
        [(planes(slab + 2 * (DEEP - 4)), "direct")],
        [Field.shape(count, DEEP - 2, tile)],
        cost=4_000_000, name="scale", limit=4,
    )
    (out,) = kernel_call(
        final_kernel,
        [
            (mine, "direct"), (theirs, "direct"), (next_full, "direct"),
            (pack, "direct"), (near_media, "direct"), (waves, "direct"),
            (power, "direct"), (scaled, "direct"), (new_field, "direct"),
        ],
        [(planes(slab), "hbm")],
        [
            scratch(planes(slab)), scratch((3, 2, 2, count) + tile),
            Field.shape(count, slab + 4, tile), Field.shape(count, slab + 2, tile),
        ],
        pieces=3, cost=60_000_000, name="final", limit=16,
    )
    return out


def solution(mesh):
    return jax.shard_map(
        local,
        mesh=mesh,
        in_specs=(
            P(None, "groups", None, None),
            P("groups"),
            P("depth", "groups", None),
            P("depth", "groups", None),
            P(),
            P("groups"),
            P(None, "groups", "depth", None, None),
        ),
        out_specs=P(None, "groups", "depth", None, None),
        check_vma=False,
    )
```
